32 devices in a mesh: groups: 2 (over y), strip: 16 (over z, x, core).
Axes of the slice: x: 2, y: 2, z: 4, core: 2. Of those that a mesh axis runs over, the one named last changes fastest.
Arguments:
- bands: bfloat16 [64, 2048], P(('groups', 'strip')), parts along dimension 0, may hold values from -6 to 6
- target: bfloat16 [64, 2048], P('groups', 'strip'), parts along dimension 0, may hold values from -6 to 6
- w_in: bfloat16 [32, 128], replicated, may hold values from -1 to 1
- w_conv: bfloat16 [3, 3, 4, 32, 32], replicated, may hold values from -0.375 to 0.375
- w_track: bfloat16 [3, 3, 128, 128], replicated, may hold values from -0.3125 to 0.3125
- w_out: bfloat16 [128, 32], replicated, may hold values from -0.5 to 0.5
- table: float32 [64, 32], replicated, may hold values from -6 to 6
- dilation: int32 [3], replicated, may hold values from 1 to 8, as said below
- detector: int32 [128], P(('groups', 'strip')), parts along dimension 0, may hold values from 0 to 63
- flags: int32 [128], P(('groups', 'strip')), parts along dimension 0, may hold values 0 or 1
Outputs:
- prediction: bfloat16 [64, 2048], P('groups', 'strip'), parts along dimension 0
- grad_in: float32 [64, 128], P('groups'), parts along dimension 0
- grad_conv: float32 [6, 3, 4, 32, 32], P('groups'), parts along dimension 0
- grad_track: float32 [6, 3, 128, 128], P('groups'), parts along dimension 0
- grad_out: float32 [256, 32], P('groups'), parts along dimension 0
- grad_table: float32 [128, 32], P('groups'), parts along dimension 0
The draws below stay inside these ranges and needn't reach their ends.
There are 2 independent parts, one for each index of `groups`. The reference program is written for one: setup_inputs(seed, part) draws one part's arguments, and reference() takes and returns one part's arrays. A program takes and returns all parts, laid end to end along the dimension named above; an argument that names none is the same for every part. Nothing has to cross between parts.
Inputs may be any that keep to these rules, and one draw needn't show every extreme that they name: `dilation`: each entry is 1 to 8, and one entry equals 8.
All inputs are finite; a program needn't handle non-finite values. No bound on the sum of `flags` on one device may be relied on, other than what follows from the above.
Results may differ from the reference program's by a relative error of at most 0.01.
Values may be sent and summed in bfloat16 or wider, within the bound.
No kernel may reach another device: no remote copies, remote signals or barrier semaphores. Data moves between devices by JAX's collectives and lax.ppermute only.
A program may use at most 64 MiB of HBM per device.

```python
import math
import jax
import jax.numpy as jnp
from jax import lax

C = 128
BANDS = 32
GROUPW = 32
LAYERS = 3
ROWS = 32
COLS = 64
NDET = 64
MAXDIL = 8
GROUPS = 4


def draw_dilation(key, part):
    first_key, second_key = jax.random.split(jax.random.fold_in(key, 11))
    spacing = jax.random.randint(first_key, (LAYERS,), 1, MAXDIL + 1)
    position = jax.random.randint(second_key, (), 0, LAYERS)
    return jnp.where(jnp.arange(LAYERS) == position, MAXDIL, spacing).astype(jnp.int32)


def touch_ends(result, key, low, largest):
    spot = [jax.random.randint(jax.random.fold_in(key, axis), (), 0, length) for axis, length in enumerate(result.shape)]
    main_axis = result.shape.index(max(result.shape))
    neighbour = spot[:main_axis] + [(spot[main_axis] + 1) % result.shape[main_axis]] + spot[main_axis + 1:]
    return result.at[tuple(spot)].set(low).at[tuple(neighbour)].set(largest)


def block_scale(key, dims, cuts, least, top_value):
    factor_of, own = 1.0, jax.random.fold_in(key, 6)
    for dim, parts in cuts:
        heights = jnp.exp(jax.random.uniform(jax.random.fold_in(own, dim), (parts,), jnp.float32, least / len(cuts), top_value / len(cuts)))
        factor_of = factor_of * jnp.repeat(heights, dims[dim] // parts).reshape([-1 if axis == dim else 1 for axis in range(len(dims))])
    return factor_of


def centred(rng, shape, spread, bound, pieces=(), held_as=jnp.bfloat16):
    loudness = block_scale(rng, shape, pieces, -0.22, 0.18) if pieces else 1.0
    result = jax.random.normal(rng, shape, jnp.float32) * spread * loudness
    return jnp.minimum(jnp.maximum(result, -bound), bound).astype(held_as)


def setup_inputs(seed: int = 0, part: int = 0) -> dict:
    key_of = jax.random.split(jax.random.key(seed), 11)
    part_keys = jax.random.split(jax.random.fold_in(key_of[10], part), 11)
    bands = centred(part_keys[0], (ROWS, COLS * BANDS), 1.0, 6.0, ((0, 16),))
    target = centred(part_keys[1], (ROWS, COLS * BANDS), 1.0, 6.0, ((1, 16),))
    w_in = centred(key_of[2], (BANDS, C), BANDS ** -0.5, 1.0)
    w_conv = centred(key_of[3], (3, 3, GROUPS, GROUPW, GROUPW), (9 * GROUPW) ** -0.5, 0.375)
    w_track = centred(key_of[4], (LAYERS, 3, C, C), (3 * C) ** -0.5, 0.3125)
    w_out = centred(key_of[5], (C, BANDS), C ** -0.5, 0.5)
    table = centred(key_of[6], (NDET, BANDS), 1.0, 6.0, (), jnp.float32)
    dilation = draw_dilation(jax.random.fold_in(key_of[10], 71), part)
    detector = touch_ends(jax.random.randint(part_keys[8], (COLS,), 0, NDET), jax.random.fold_in(part_keys[8], 1), 0, NDET - 1).astype(jnp.int32)
    flags = touch_ends((jax.random.randint(part_keys[9], (COLS,), 0, 4) < 1).astype(jnp.int32), jax.random.fold_in(part_keys[9], 1), 0, 1)
    return {"bands": bands, "target": target, "w_in": w_in, "w_conv": w_conv, "w_track": w_track, "w_out": w_out, "table": table, "dilation": dilation, "detector": detector, "flags": flags}


def silu_slope(preact):
    sigmoid_val = jax.nn.sigmoid(preact)
    return sigmoid_val * (1.0 + preact * (1.0 - sigmoid_val))

def grouped_view(source, groups):
    return source.reshape(source.shape[0], source.shape[1], groups, source.shape[2] // groups).astype(jnp.float32)

def conv_forward(padded, weight):
    row_count = padded.shape[0] - 2
    col_count = padded.shape[1] - 2
    groups = weight.shape[2]
    grouped = grouped_view(padded, groups)
    summed = jnp.zeros((row_count, col_count, groups, weight.shape[4]), jnp.float32)
    for i in range(3):
        for j in range(3):
            summed = summed + jnp.einsum('rkgp,gpo->rkgo', grouped[i:i + row_count, j:j + col_count], weight[i, j].astype(jnp.float32))
    return summed.reshape(row_count, col_count, -1)

def conv_transpose(padded_grad, weight):
    row_count = padded_grad.shape[0] - 2
    col_count = padded_grad.shape[1] - 2
    groups = weight.shape[2]
    grouped = grouped_view(padded_grad, groups)
    summed = jnp.zeros((row_count, col_count, groups, weight.shape[3]), jnp.float32)
    for i in range(3):
        for j in range(3):
            summed = summed + jnp.einsum('rkgo,gpo->rkgp', grouped[2 - i:2 - i + row_count, 2 - j:2 - j + col_count], weight[i, j].astype(jnp.float32))
    return summed.reshape(row_count, col_count, -1)

def conv_weight_grad(padded, gradient, groups):
    row_count = gradient.shape[0]
    col_count = gradient.shape[1]
    grouped_in = grouped_view(padded, groups)
    grouped_out = grouped_view(gradient, groups)
    return jnp.stack([jnp.stack([jnp.einsum('rkgp,rkgo->gpo', grouped_in[i:i + row_count, j:j + col_count], grouped_out) for j in range(3)]) for i in range(3)])

def shifted(source, offset, margin):
    padded = jnp.pad(source, ((margin, margin), (0, 0), (0, 0)))
    return lax.dynamic_slice_in_dim(padded, margin + offset, source.shape[0], 0)

def column_phase(features, target_block, w_track, w_out, offsets, flag_values, dilation, margin, loss_scale):
    row_count, col_count, chan_count = features.shape
    band_count = w_out.shape[1]
    layers = w_track.shape[0]
    contract = (((0,), (0,)), ((), ()))
    activations = [features]
    preacts = []
    current = features
    for layer_index in range(layers):
        spacing = dilation[layer_index]
        preact = jnp.zeros((row_count * col_count, chan_count), jnp.float32)
        for tap_index in range(3):
            moved_rows = shifted(current, (tap_index - 1) * spacing, margin)
            preact = preact + jnp.dot(moved_rows.reshape(-1, chan_count), w_track[layer_index, tap_index], preferred_element_type=jnp.float32)
        preact = preact.reshape(row_count, col_count, chan_count)
        current = (current.astype(jnp.float32) + jax.nn.silu(preact)).astype(jnp.bfloat16)
        preacts.append(preact)
        activations.append(current)
    raw_output = jnp.dot(current.reshape(-1, chan_count), w_out, preferred_element_type=jnp.float32).reshape(row_count, col_count, band_count) + offsets[None]
    prediction = raw_output.astype(jnp.bfloat16)
    residue = (prediction.astype(jnp.float32) - target_block.reshape(row_count, col_count, band_count).astype(jnp.float32)) * loss_scale
    residue_b = residue.astype(jnp.bfloat16)
    grad_out = lax.dot_general(current.reshape(-1, chan_count), residue_b.reshape(-1, band_count), contract, preferred_element_type=jnp.float32)
    column_sums = lax.optimization_barrier(jnp.sum(residue, axis=0)) * flag_values[:, None]
    backward = jnp.dot(residue_b.reshape(-1, band_count), w_out.T, preferred_element_type=jnp.float32).reshape(row_count, col_count, chan_count)
    track_grads = [None] * layers
    for layer_index in reversed(range(layers)):
        spacing = dilation[layer_index]
        gate_grad = (backward * silu_slope(preacts[layer_index])).astype(jnp.bfloat16)
        flat_grad = gate_grad.reshape(-1, chan_count)
        tap_grads = []
        for tap_index in range(3):
            moved_rows = shifted(activations[layer_index], (tap_index - 1) * spacing, margin)
            tap_grads.append(lax.dot_general(moved_rows.reshape(-1, chan_count), flat_grad, contract, preferred_element_type=jnp.float32))
            pulled = jnp.dot(flat_grad, w_track[layer_index, tap_index].T, preferred_element_type=jnp.float32).reshape(row_count, col_count, chan_count)
            backward = backward + shifted(pulled, (1 - tap_index) * spacing, margin)
        track_grads[layer_index] = jnp.stack(tap_grads)
    return (backward.astype(jnp.bfloat16), prediction.reshape(row_count, col_count * band_count), jnp.stack(track_grads), grad_out, column_sums)

def reference(bands, target, w_in, w_conv, w_track, w_out, table, dilation, detector, flags):
    row_block = math.gcd(64, ROWS)
    col_block = math.gcd(64, COLS)
    row_steps = ROWS // row_block
    col_steps = COLS // col_block
    contract = (((0,), (0,)), ((), ()))
    pixels = bands.reshape(ROWS, COLS, BANDS)

    def project_block(block):
        return jnp.dot(block, w_in, preferred_element_type=jnp.float32).astype(jnp.bfloat16)
    projected = lax.map(project_block, pixels.reshape(row_steps, row_block * COLS, BANDS)).reshape(ROWS, COLS, C)
    outer = jnp.pad(projected, ((2, 2), (1, 1), (0, 0)))
    starts = jnp.arange(row_steps, dtype=jnp.int32) * row_block

    def forward_rows(start):
        window = lax.dynamic_slice_in_dim(outer, start + 1, row_block + 2, 0)
        spatial = conv_forward(window, w_conv)
        center = window[1:-1, 1:-1]
        return (center.astype(jnp.float32) + jax.nn.silu(spatial)).astype(jnp.bfloat16)
    features = lax.map(forward_rows, starts).reshape(ROWS, COLS, C)
    loss_scale = 1.0 / math.sqrt(ROWS * COLS)
    flag_values = flags.astype(jnp.float32)
    offsets = flag_values[:, None] * table[detector]

    def column_step(carry, inputs):
        feature_block, target_block, offset_block, flag_block, detector_block = inputs
        feature_grad, prediction, track_part, out_part, column_sums = column_phase(feature_block, target_block, w_track, w_out, offset_block, flag_block, dilation, MAXDIL, loss_scale)
        track_sum, out_sum, table_sum = carry
        table_sum = table_sum.at[detector_block].add(column_sums)
        return ((track_sum + track_part, out_sum + out_part, table_sum), (feature_grad, prediction))
    inputs = (features.reshape(ROWS, col_steps, col_block, C).transpose(1, 0, 2, 3), target.reshape(ROWS, col_steps, col_block * BANDS).transpose(1, 0, 2), offsets.reshape(col_steps, col_block, BANDS), flag_values.reshape(col_steps, col_block), detector.reshape(col_steps, col_block))
    initial = (jnp.zeros((LAYERS, 3, C, C), jnp.float32), jnp.zeros((C, BANDS), jnp.float32), jnp.zeros((NDET, BANDS), jnp.float32))
    (grad_track, grad_out, grad_table), (feature_grad, prediction) = lax.scan(column_step, initial, inputs)
    feature_grad = feature_grad.transpose(1, 0, 2, 3).reshape(ROWS, COLS, C)
    prediction = prediction.transpose(1, 0, 2).reshape(ROWS, COLS * BANDS)
    grad_pad = jnp.pad(feature_grad, ((1, 1), (0, 0), (0, 0)))

    def backward_rows(carry, start):
        grad_in, grad_conv = carry
        window = lax.dynamic_slice_in_dim(outer, start, row_block + 4, 0)
        spatial = conv_forward(window, w_conv)
        near_grad = lax.dynamic_slice_in_dim(grad_pad, start, row_block + 2, 0)
        mixed_grad = (near_grad.astype(jnp.float32) * silu_slope(spatial)).astype(jnp.bfloat16)
        lifted = (near_grad[1:-1].astype(jnp.float32) + conv_transpose(jnp.pad(mixed_grad, ((0, 0), (1, 1), (0, 0))), w_conv)).astype(jnp.bfloat16)
        grad_conv = grad_conv + conv_weight_grad(window[1:-1], mixed_grad[1:-1], GROUPS)
        pixel_block = lax.dynamic_slice_in_dim(pixels, start, row_block, 0)
        grad_in = grad_in + lax.dot_general(pixel_block.reshape(-1, BANDS), lifted.reshape(-1, C), contract, preferred_element_type=jnp.float32)
        return ((grad_in, grad_conv), None)
    initial_rows = (jnp.zeros((BANDS, C), jnp.float32), jnp.zeros((3, 3, GROUPS, GROUPW, GROUPW), jnp.float32))
    (grad_in, grad_conv), _ = lax.scan(backward_rows, initial_rows, starts)
    return (prediction, grad_in, grad_conv, grad_track, grad_out, grad_table)
```

```python
import math

import jax
import jax.numpy as jnp
from jax import lax
from jax.experimental import pallas as pl
from jax.experimental.pallas import tpu as pltpu
from jax.sharding import PartitionSpec as P

INTERPRET = False


def with_halo(x, sides, width):
    for axis, dim in sides:
        size, length = (lax.axis_size(axis), x.shape[dim])
        up = [(i, (i + 1) % size) for i in range(size - 1)]
        down = [(j, i) for i, j in up]
        last = lax.slice_in_dim(x, length - width, length, axis=dim)
        initial = lax.slice_in_dim(x, 0, width, axis=dim)
        before = lax.ppermute(last, axis, up)
        after = lax.ppermute(initial, axis, down)
        x = jnp.concatenate([before, x, after], axis=dim)
    return x


def silu_slope(preact):
    sigmoid_val = jax.nn.sigmoid(preact)
    return sigmoid_val * (1.0 + preact * (1.0 - sigmoid_val))


def block_diagonal(weight):
    groups = weight.shape[2]
    width = weight.shape[3]
    identity = jnp.eye(groups, dtype=weight.dtype)
    spread = weight[:, :, :, :, None, :] * identity[None, None, :, None, :, None]
    return spread.reshape(3, 3, groups * width, groups * width)


def conv_forward(padded, dense_weight):
    row_count = padded.shape[0] - 2
    col_count = padded.shape[1] - 2
    chan_count = padded.shape[2]
    summed = jnp.zeros((row_count * col_count, dense_weight.shape[3]), jnp.float32)
    for i in range(3):
        for j in range(3):
            window = padded[i : i + row_count, j : j + col_count].reshape(-1, chan_count)
            summed = summed + jnp.dot(
                window, dense_weight[i, j], preferred_element_type=jnp.float32
            )
    return summed.reshape(row_count, col_count, -1)


def conv_transpose(padded_grad, dense_weight):
    row_count = padded_grad.shape[0] - 2
    col_count = padded_grad.shape[1] - 2
    chan_count = padded_grad.shape[2]
    summed = jnp.zeros((row_count * col_count, dense_weight.shape[2]), jnp.float32)
    for i in range(3):
        for j in range(3):
            window = padded_grad[2 - i : 2 - i + row_count, 2 - j : 2 - j + col_count].reshape(
                -1, chan_count
            )
            summed = summed + jnp.dot(
                window, dense_weight[i, j].T, preferred_element_type=jnp.float32
            )
    return summed.reshape(row_count, col_count, -1)


def conv_weight_grad(padded, gradient, groups):
    row_count = gradient.shape[0]
    col_count = gradient.shape[1]
    chan_count = gradient.shape[2]
    width = chan_count // groups
    contract = (((0,), (0,)), ((), ()))
    flat_out = gradient.reshape(-1, chan_count)
    rows_of_taps = []
    for i in range(3):
        taps = []
        for j in range(3):
            window = padded[i : i + row_count, j : j + col_count].reshape(-1, chan_count)
            full = lax.dot_general(window, flat_out, contract, preferred_element_type=jnp.float32)
            taps.append(
                jnp.stack(
                    [
                        full[g * width : (g + 1) * width, g * width : (g + 1) * width]
                        for g in range(groups)
                    ]
                )
            )
        rows_of_taps.append(jnp.stack(taps))
    return jnp.stack(rows_of_taps)


def shifted(source, offset, margin):
    padded = jnp.pad(source, ((margin, margin), (0, 0), (0, 0)))
    return lax.dynamic_slice_in_dim(padded, margin + offset, source.shape[0], 0)


def project_pixels(pixels, w_in):
    flat = jnp.dot(pixels.reshape(-1, pixels.shape[2]), w_in, preferred_element_type=jnp.float32)
    return flat.astype(jnp.bfloat16).reshape(pixels.shape[0], pixels.shape[1], w_in.shape[1])


def column_work(
    features, target_block, w_track, w_out, table, dilation, detector, flags, loss_scale
):
    row_count, col_count, chan_count = features.shape
    band_count = w_out.shape[1]
    layers = w_track.shape[0]
    margin = row_count // 4
    contract = (((0,), (0,)), ((), ()))
    selector = (detector[:, None] == jnp.arange(table.shape[0], dtype=jnp.int32)[None, :]).astype(
        jnp.float32
    )
    flag_values = flags.astype(jnp.float32)
    offsets = flag_values[:, None] * jnp.dot(selector, table, precision=lax.Precision.HIGHEST)
    activations = [features]
    preacts = []
    current = features
    for layer_index in range(layers):
        spacing = dilation[layer_index]
        preact = jnp.zeros((row_count * col_count, chan_count), jnp.float32)
        for tap_index in range(3):
            moved_rows = shifted(current, (tap_index - 1) * spacing, margin)
            preact = preact + jnp.dot(
                moved_rows.reshape(-1, chan_count),
                w_track[layer_index, tap_index],
                preferred_element_type=jnp.float32,
            )
        preact = preact.reshape(row_count, col_count, chan_count)
        current = (current.astype(jnp.float32) + jax.nn.silu(preact)).astype(jnp.bfloat16)
        preacts.append(preact)
        activations.append(current)
    raw_output = (
        jnp.dot(current.reshape(-1, chan_count), w_out, preferred_element_type=jnp.float32).reshape(
            row_count, col_count, band_count
        )
        + offsets[None]
    )
    prediction = raw_output.astype(jnp.bfloat16)
    residue = (
        prediction.astype(jnp.float32)
        - target_block.reshape(row_count, col_count, band_count).astype(jnp.float32)
    ) * loss_scale
    residue_b = residue.astype(jnp.bfloat16)
    grad_out = lax.dot_general(
        current.reshape(-1, chan_count),
        residue_b.reshape(-1, band_count),
        contract,
        preferred_element_type=jnp.float32,
    )
    column_sums = jnp.sum(residue, axis=0) * flag_values[:, None]
    grad_table = jnp.dot(selector.T, column_sums, precision=lax.Precision.HIGHEST)
    backward = jnp.dot(
        residue_b.reshape(-1, band_count), w_out.T, preferred_element_type=jnp.float32
    ).reshape(row_count, col_count, chan_count)
    track_grads = [None] * layers
    for layer_index in reversed(range(layers)):
        spacing = dilation[layer_index]
        gate_grad = (backward * silu_slope(preacts[layer_index])).astype(jnp.bfloat16)
        flat_grad = gate_grad.reshape(-1, chan_count)
        tap_grads = []
        for tap_index in range(3):
            moved_rows = shifted(activations[layer_index], (tap_index - 1) * spacing, margin)
            tap_grads.append(
                lax.dot_general(
                    moved_rows.reshape(-1, chan_count),
                    flat_grad,
                    contract,
                    preferred_element_type=jnp.float32,
                )
            )
            pulled = jnp.dot(
                flat_grad, w_track[layer_index, tap_index].T, preferred_element_type=jnp.float32
            ).reshape(row_count, col_count, chan_count)
            backward = backward + shifted(pulled, (1 - tap_index) * spacing, margin)
        track_grads[layer_index] = jnp.stack(tap_grads)
    return (
        backward.astype(jnp.bfloat16),
        prediction.reshape(row_count, col_count * band_count),
        jnp.stack(track_grads),
        grad_out,
        grad_table,
    )


def body_distributed(bands, target, w_in, w_conv, w_track, w_out, table, dilation, detector, flags):
    band_count = w_in.shape[0]
    chan_count = w_in.shape[1]
    groups = w_conv.shape[2]
    device_count = lax.axis_size("strip")
    dense_conv = block_diagonal(w_conv)
    row_count = bands.shape[0]
    col_count = bands.shape[1] // band_count
    pixels = bands.reshape(row_count, col_count, band_count)
    projected = project_pixels(pixels, w_in)
    padded = with_halo(projected, (("strip", 0),), 1)
    padded = jnp.pad(padded, ((0, 0), (1, 1), (0, 0)))
    spatial = conv_forward(padded, dense_conv)
    features = (projected.astype(jnp.float32) + jax.nn.silu(spatial)).astype(jnp.bfloat16)
    feature_cols = lax.all_to_all(features, "strip", split_axis=1, concat_axis=0, tiled=True)
    loss_scale = 1.0 / math.sqrt(feature_cols.shape[0] * feature_cols.shape[1] * device_count)
    feature_grad, prediction, grad_track, grad_out, grad_table = column_work(
        feature_cols, target, w_track, w_out, table, dilation, detector, flags, loss_scale
    )
    local_grad = lax.all_to_all(feature_grad, "strip", split_axis=0, concat_axis=1, tiled=True)
    mixed_grad = (local_grad.astype(jnp.float32) * silu_slope(spatial)).astype(jnp.bfloat16)
    grad_pad = with_halo(mixed_grad, (("strip", 0),), 1)
    grad_pad = jnp.pad(grad_pad, ((0, 0), (1, 1), (0, 0)))
    lifted = (local_grad.astype(jnp.float32) + conv_transpose(grad_pad, dense_conv)).astype(
        jnp.bfloat16
    )
    grad_conv = conv_weight_grad(padded, mixed_grad, groups)
    contract = (((0,), (0,)), ((), ()))
    grad_in = lax.dot_general(
        pixels.reshape(-1, band_count),
        lifted.reshape(-1, chan_count),
        contract,
        preferred_element_type=jnp.float32,
    )
    grad_in, grad_conv, grad_track, grad_out, grad_table = lax.psum(
        (grad_in, grad_conv, grad_track, grad_out, grad_table), "strip"
    )
    return (prediction, grad_in, grad_conv, grad_track, grad_out, grad_table)


LANES = 128
HALF = 64
SLOTS = 4
VMEM_BUDGET = 48 * 1024 * 1024


def low_half(shape):
    return lax.broadcasted_iota(jnp.int32, shape, len(shape) - 1) % LANES < HALF


def swap_halves(x):
    return pltpu.roll(x, HALF, 1)


def expand_tap(weight):
    turned = swap_halves(weight)
    low = low_half((HALF, LANES))
    zero = jnp.zeros((HALF, LANES), jnp.float32)
    blocks = []
    for h in range(2):
        own = weight[h * HALF : (h + 1) * HALF]
        other = turned[h * HALF : (h + 1) * HALF]
        blocks.append(jnp.concatenate([jnp.where(low, own, zero), jnp.where(low, other, zero)], axis=1))
        blocks.append(jnp.concatenate([jnp.where(low, zero, other), jnp.where(low, zero, own)], axis=1))
    return jnp.concatenate(blocks, axis=0)


def expand_band(weight):
    band_count = weight.shape[0]
    turned = swap_halves(weight)
    low = low_half((band_count, LANES))
    zero = jnp.zeros((band_count, LANES), jnp.float32)
    columns = []
    for h in range(2):
        first, second = (weight, turned) if h == 0 else (turned, weight)
        for pair in range(2):
            rows = [zero] * SLOTS
            rows[2 * pair] = jnp.where(low, first, zero)
            rows[2 * pair + 1] = jnp.where(low, zero, second)
            columns.append(jnp.concatenate(rows, axis=0))
    return jnp.concatenate(columns, axis=1)


INPUT_SLOTS = (0, 1, 2, 3, 4, -1)


def expand_conv(taps, ref, transposed):
    width = taps.shape[0] // 9
    low = low_half((HALF, LANES))
    zero = jnp.zeros((HALF, LANES), jnp.float32)
    row = lax.broadcasted_iota(jnp.int32, (HALF, LANES), 0) // width
    lane = lax.broadcasted_iota(jnp.int32, (HALF, LANES), 1) // width % 2
    same = row == lane
    for i in range(3):
        for h in range(2):
            values = []
            for j in range(3):
                tap = taps[(3 * i + j) * width : (3 * i + j + 1) * width]
                turned = swap_halves(tap)
                spread = jnp.where(low[:width], tap, turned) if h == 0 else jnp.where(low[:width], turned, tap)
                values.append(jnp.where(same, jnp.concatenate([spread, spread], axis=0), zero))
            place = 2 - i if transposed else i
            for position, slot in enumerate(INPUT_SLOTS):
                tiles = []
                for pair in range(2):
                    pieces = []
                    for half in range(2):
                        out_slot = 2 * pair + half
                        j = out_slot + 1 - slot if transposed else slot - out_slot + 1
                        pieces.append(values[j] if 0 <= j <= 2 else zero)
                    tiles.append(jnp.where(low, pieces[0], pieces[1]))
                start = (place * len(INPUT_SLOTS) + position) * HALF
                ref[h, start : start + HALF, :] = jnp.concatenate(tiles, axis=1).astype(ref.dtype)


def prepare_kernel(w_in, w_out_t, taps, taps_t, w_track, w4, wo4, wc, wt, wf, wb):
    w4[...] = expand_band(w_in[...].astype(jnp.float32)).astype(w4.dtype)
    wo4[...] = expand_band(w_out_t[...].astype(jnp.float32)).astype(wo4.dtype)
    expand_conv(taps[...].astype(jnp.float32), wc, False)
    expand_conv(taps_t[...].astype(jnp.float32), wt, True)
    layers = w_track.shape[0]
    for layer in range(layers):
        for tap in range(3):
            weight = w_track[layer, tap].astype(jnp.float32)
            rows = pl.ds(tap * 2 * LANES, 2 * LANES)
            wf[layer, rows, :] = expand_tap(weight).astype(wf.dtype)
            wb[layer, rows, :] = expand_tap(weight.T).astype(wb.dtype)


def prepare_weights(w_in, w_conv, w_track, w_out):
    chan_count = w_in.shape[1]
    width = w_conv.shape[3]
    layers = w_track.shape[0]
    taps = jnp.transpose(w_conv, (0, 1, 3, 2, 4)).reshape(9 * width, chan_count)
    taps_t = jnp.transpose(w_conv, (0, 1, 4, 2, 3)).reshape(9 * width, chan_count)
    shapes = (
        (SLOTS * w_in.shape[0], SLOTS * chan_count),
        (SLOTS * w_out.shape[1], SLOTS * chan_count),
        (2, 18 * HALF, 2 * LANES),
        (2, 18 * HALF, 2 * LANES),
        (layers, 6 * LANES, 2 * LANES),
        (layers, 6 * LANES, 2 * LANES),
    )
    return pl.pallas_call(
        prepare_kernel,
        out_shape=tuple(jax.ShapeDtypeStruct(s, jnp.bfloat16) for s in shapes),
        interpret=INTERPRET,
        name="prepare_weights",
    )(w_in, w_out.T, taps, taps_t, w_track)


def silu_and_slope(v):
    s = 0.5 * jnp.tanh(0.5 * v) + 0.5
    return v * s, s * (1.0 + v * (1.0 - s))


def dot(a, b):
    return jnp.dot(a, b, preferred_element_type=jnp.float32)


def dot_tn(a, b):
    return lax.dot_general(a, b, (((0,), (0,)), ((), ())), preferred_element_type=jnp.float32)


def dot_nt(a, b):
    return lax.dot_general(a, b, (((1,), (1,)), ((), ())), preferred_element_type=jnp.float32)


def thirds(x):
    first = x.astype(jnp.bfloat16)
    rest = x - first.astype(jnp.float32)
    second = rest.astype(jnp.bfloat16)
    third = (rest - second.astype(jnp.float32)).astype(jnp.bfloat16)
    return first, second, third


def band_diagonal(full):
    rows = full.shape[0] // SLOTS
    low = low_half((rows, LANES))
    straight, crossed = None, None
    for pair in range(2):
        even = [full[2 * pair * rows : (2 * pair + 1) * rows, (2 * h + pair) * LANES : (2 * h + pair + 1) * LANES] for h in range(2)]
        odd = [full[(2 * pair + 1) * rows : (2 * pair + 2) * rows, (2 * h + pair) * LANES : (2 * h + pair + 1) * LANES] for h in range(2)]
        direct = jnp.where(low, even[0], odd[1])
        swapped = jnp.where(low, even[1], odd[0])
        straight = direct if straight is None else straight + direct
        crossed = swapped if crossed is None else crossed + swapped
    return straight + swap_halves(crossed)


def step_kernel(
    rows_total,
    blocks,
    margin,
    loss_scale,
    own,
    dilation,
    gathered,
    w4,
    wo4,
    wc,
    wt,
    wf,
    wb,
    table_t,
    prediction,
    grad_in,
    grad_conv,
    grad_track,
    grad_out_t,
    grad_table_t,
    pixels,
    target,
    meta,
    proj,
    mixed,
    acts,
    gates,
    slopes,
    backward,
    shown,
):
    size = rows_total * blocks
    strips = gathered.shape[0]
    rows_local = rows_total // strips
    layers = wf.shape[0]
    bf16 = jnp.bfloat16
    f32 = jnp.float32
    mine = own[0]
    bits = strips.bit_length() - 1
    local = rows_local * blocks
    middle = pl.ds(margin * blocks, size)

    for s in range(strips):
        apart = mine ^ s
        place = 0
        for b in range(bits):
            place = place * 2 + ((apart >> b) & 1)
        pixels[s * local : (s + 1) * local, :] = gathered[place, 0:local, :]
        target[pl.ds(s, rows_total, stride=blocks), :] = gathered[place, local : local + rows_total, :].astype(f32)
        meta[s : s + 1, :] = gathered[place, local + rows_total : local + rows_total + 16, :].astype(f32)[0:1]

    for ref in (proj, mixed):
        ref[0:blocks, :] = jnp.zeros((blocks, ref.shape[1]), bf16)
        ref[size + blocks : size + 2 * blocks, :] = jnp.zeros((blocks, ref.shape[1]), bf16)
    edge = jnp.zeros((margin * blocks, acts.shape[2]), bf16)
    for layer in range(layers):
        acts[layer, 0 : margin * blocks, :] = edge
        acts[layer, margin * blocks + size :, :] = edge
    gates[0 : margin * blocks, :] = edge
    gates[margin * blocks + size :, :] = edge

    low = low_half((size, LANES))
    position = lax.broadcasted_iota(jnp.int32, (size, LANES), 0) % blocks
    outside = jnp.where(low, blocks - 1, 0)
    keep = position != outside

    def put_padded(ref, value):
        rounded = value.astype(bf16)
        ref[blocks : blocks + size, 0 : 4 * LANES] = rounded
        wide = rounded.astype(f32)
        for h in range(2):
            following = pltpu.roll(wide[:, 2 * h * LANES : (2 * h + 1) * LANES], size - 1, 0)
            previous = pltpu.roll(wide[:, (2 * h + 1) * LANES : (2 * h + 2) * LANES], 1, 0)
            side = jnp.where(keep, jnp.where(low, following, previous), 0.0)
            ref[blocks : blocks + size, (4 + h) * LANES : (5 + h) * LANES] = side.astype(bf16)

    def window(ref, h, i):
        rows = slice(i * blocks, i * blocks + size)
        return [ref[rows, 2 * h * LANES : (2 * h + 2) * LANES], ref[rows, (4 + h) * LANES : (5 + h) * LANES]]

    put_padded(proj, dot(pixels[...], w4[...]))
    for h in range(2):
        lanes = slice(2 * h * LANES, (2 * h + 2) * LANES)
        left = jnp.concatenate([piece for i in range(3) for piece in window(proj, h, i)], axis=1)
        silu, slope = silu_and_slope(dot(left, wc[h]))
        slopes[layers, :, lanes] = slope
        centre = proj[blocks : blocks + size, lanes].astype(f32)
        acts[0, middle, lanes] = (centre + silu).astype(bf16)

    def tap_window(ref, spacing, sign, pair):
        pieces = []
        for tap in range(3):
            start = pl.multiple_of((margin + sign * (tap - 1) * spacing) * blocks, 16)
            for h in range(2):
                pieces.append(ref[pl.ds(start, size), (2 * h + pair) * LANES : (2 * h + pair + 1) * LANES])
        return jnp.concatenate(pieces, axis=1)

    def forward(layer, carry):
        spacing = dilation[layer]
        for pair in range(2):
            silu, slope = silu_and_slope(dot(tap_window(acts.at[layer], spacing, 1, pair), wf[layer]))
            for h in range(2):
                lanes = slice((2 * h + pair) * LANES, (2 * h + pair + 1) * LANES)
                part = slice(h * LANES, (h + 1) * LANES)
                slopes[layer, :, lanes] = slope[:, part]
                centre = acts[layer, middle, lanes].astype(f32)
                acts[layer + 1, middle, lanes] = (centre + silu[:, part]).astype(bf16)
        return carry

    lax.fori_loop(0, layers, forward, 0)

    det_count = table_t.shape[1] // SLOTS
    meta_b = meta[...].astype(bf16)
    source = lax.broadcasted_iota(jnp.int32, (LANES, SLOTS * det_count), 0)
    slot_of = lax.broadcasted_iota(jnp.int32, (LANES, SLOTS * det_count), 1) // det_count
    spread = jnp.where(source == slot_of, 1.0, jnp.where(source == slot_of + SLOTS, 256.0, 0.0)).astype(bf16)
    element = (lax.broadcasted_iota(jnp.int32, (blocks, SLOTS * det_count), 1) % det_count).astype(f32)
    selector = jnp.where(dot(meta_b, spread) == element, 1.0, 0.0).astype(bf16)
    source = lax.broadcasted_iota(jnp.int32, (LANES, LANES), 0)
    slot_of = lax.broadcasted_iota(jnp.int32, (LANES, LANES), 1) // (LANES // SLOTS)
    flag = dot(meta_b, jnp.where(source == slot_of + 2 * SLOTS, 1.0, 0.0).astype(bf16))
    offsets = sum(dot_nt(selector, part) for part in thirds(table_t[...])) * flag

    raw = dot_nt(acts[layers, middle, :], wo4[...]).reshape(rows_total, blocks, LANES) + offsets[None]
    rounded = raw.astype(bf16).astype(f32)
    shown[...] = rounded.reshape(size, LANES)
    prediction[...] = shown[pl.ds(mine, rows_total, stride=blocks), :].astype(bf16)
    residue = (rounded - target[...].reshape(rows_total, blocks, LANES)) * loss_scale
    column_sums = jnp.sum(residue, axis=0) * flag
    residue_b = residue.reshape(size, LANES).astype(bf16)
    backward[...] = dot(residue_b, wo4[...])
    grad_out_t[...] = band_diagonal(dot_tn(residue_b, acts[layers, middle, :]))
    sums = jnp.concatenate(thirds(column_sums), axis=0)
    full = dot_tn(sums, jnp.concatenate([selector] * 3, axis=0))
    band_count = LANES // SLOTS
    grad_table_t[...] = sum(
        full[k * band_count : (k + 1) * band_count, k * det_count : (k + 1) * det_count] for k in range(SLOTS)
    )

    tap_low = low_half((HALF, LANES))

    def back(step, carry):
        layer = layers - 1 - step
        spacing = dilation[layer]
        gates[middle, :] = (backward[...] * slopes[layer]).astype(bf16)
        moved = []
        for pair in range(2):
            right = tap_window(gates, spacing, -1, pair)
            moved.append(right)
            update = dot(right, wb[layer])
            for h in range(2):
                lanes = slice((2 * h + pair) * LANES, (2 * h + pair + 1) * LANES)
                backward[:, lanes] = backward[:, lanes] + update[:, h * LANES : (h + 1) * LANES]
        left = [
            jnp.concatenate(
                [acts[layer, middle, (2 * h + pair) * LANES : (2 * h + pair + 1) * LANES] for h in range(2)], axis=1
            )
            for pair in range(2)
        ]
        full = dot_tn(jnp.concatenate(left, axis=0), jnp.concatenate(moved, axis=0))
        for tap in range(3):
            first = full[:, 2 * tap * LANES : (2 * tap + 1) * LANES]
            second = full[:, (2 * tap + 1) * LANES : (2 * tap + 2) * LANES]
            for h in range(2):
                upper = slice(2 * h * HALF, (2 * h + 1) * HALF)
                lower = slice((2 * h + 1) * HALF, (2 * h + 2) * HALF)
                straight = jnp.where(tap_low, first[upper], second[lower])
                crossed = jnp.where(tap_low, second[upper], first[lower])
                start = pl.multiple_of((layer * 3 + tap) * LANES, LANES) + h * HALF
                grad_track[pl.ds(start, HALF), :] = straight + swap_halves(crossed)
        return carry

    lax.fori_loop(0, layers, back, 0)

    feature_grad = backward[...].astype(bf16).astype(f32)
    put_padded(mixed, feature_grad * slopes[layers])
    lifted = []
    for h in range(2):
        lanes = slice(2 * h * LANES, (2 * h + 2) * LANES)
        left = jnp.concatenate([piece for i in range(3) for piece in window(mixed, h, i)], axis=1)
        lifted.append((backward[:, lanes].astype(bf16).astype(f32) + dot(left, wt[h])).astype(bf16))
    grad_in[...] = band_diagonal(dot_tn(pixels[...], jnp.concatenate(lifted, axis=1)))

    width = grad_conv.shape[1]
    for h in range(2):
        left = jnp.concatenate(window(proj, h, 1), axis=1)
        right = jnp.concatenate(
            [mixed[(2 - i) * blocks : (2 - i) * blocks + size, 2 * h * LANES : (2 * h + 2) * LANES] for i in range(3)],
            axis=1,
        )
        full = dot_tn(left, right)
        for i in range(3):
            for j in range(3):
                parts = []
                for out_slot in range(SLOTS):
                    row = INPUT_SLOTS.index(out_slot + j - 1) * HALF
                    tile = 2 * i + out_slot // 2
                    parts.append(full[row : row + HALF, tile * LANES : (tile + 1) * LANES])
                total = parts[0] + parts[2] + swap_halves(parts[1] + parts[3])
                for g in range(2):
                    start = ((3 * i + j) * 4 + 2 * h + g) * width
                    piece = total[g * width : (g + 1) * width]
                    if g:
                        piece = pltpu.roll(piece, LANES - width, 1)
                    grad_conv[start : start + width, :] = piece[:, :width]


def replicated_step(gathered, own, weights, w_track_shape, w_conv_shape, table, dilation, rows_total, blocks):
    strips = gathered.shape[0]
    layers = w_track_shape[0]
    margin = rows_total // 4
    size = rows_total * blocks
    chan_count = w_track_shape[2]
    det_count, band_count = table.shape
    loss_scale = 1.0 / math.sqrt(rows_total * blocks * SLOTS)
    slots = jnp.eye(SLOTS, dtype=table.dtype)
    table_t = (slots[:, None, :, None] * table.T[None, :, None, :]).reshape(SLOTS * band_count, SLOTS * det_count)
    smem = pl.BlockSpec(memory_space=pltpu.SMEM)
    vmem = pl.BlockSpec(memory_space=pltpu.VMEM)
    f32, bf16 = jnp.float32, jnp.bfloat16
    taps = math.prod(w_conv_shape[:4])
    outs = pl.pallas_call(
        lambda *refs: step_kernel(rows_total, blocks, margin, loss_scale, *refs),
        out_shape=(
            jax.ShapeDtypeStruct((rows_total, LANES), bf16),
            jax.ShapeDtypeStruct((band_count, chan_count), f32),
            jax.ShapeDtypeStruct((taps, w_conv_shape[4]), f32),
            jax.ShapeDtypeStruct((layers * 3 * chan_count, chan_count), f32),
            jax.ShapeDtypeStruct((band_count, chan_count), f32),
            jax.ShapeDtypeStruct((band_count, det_count), f32),
        ),
        in_specs=[smem, smem] + [vmem] * 8,
        out_specs=tuple([vmem] * 6),
        scratch_shapes=[
            pltpu.VMEM((size, LANES), bf16),
            pltpu.VMEM((size, LANES), f32),
            pltpu.VMEM((blocks, LANES), f32),
            pltpu.VMEM((size + 2 * blocks, 6 * LANES), bf16),
            pltpu.VMEM((size + 2 * blocks, 6 * LANES), bf16),
            pltpu.VMEM((layers + 1, size + 2 * margin * blocks, 4 * LANES), bf16),
            pltpu.VMEM((size + 2 * margin * blocks, 4 * LANES), bf16),
            pltpu.VMEM((layers + 1, size, 4 * LANES), f32),
            pltpu.VMEM((size, 4 * LANES), f32),
            pltpu.VMEM((size, LANES), f32),
        ],
        interpret=INTERPRET,
        name="strip_step",
    )(own, dilation, gathered, *weights, table_t)
    prediction, grad_in, grad_conv, grad_track, grad_out_t, grad_table_t = outs
    return (
        prediction,
        grad_in,
        grad_conv.reshape(w_conv_shape),
        grad_track.reshape(w_track_shape),
        grad_out_t.T,
        grad_table_t.T,
    )


def device_payload(bands, target, detector, flags, blocks):
    cells = jnp.concatenate([detector & 255, detector >> 8, flags]).astype(jnp.bfloat16)
    line = jnp.zeros((16, LANES), jnp.bfloat16).at[0, : cells.shape[0]].set(cells)
    return jnp.concatenate([bands.reshape(bands.shape[0] * blocks, LANES), target, line], axis=0)


def gather_strip(payload, size):
    held = payload[None]
    distance = size // 2
    while distance:
        pairs = [(i, i ^ distance) for i in range(size)]
        held = jnp.concatenate([held, lax.ppermute(held, "strip", pairs)], axis=0)
        distance //= 2
    return held


def body_replicated(bands, target, w_in, w_conv, w_track, w_out, table, dilation, detector, flags):
    size = lax.axis_size("strip")
    rows_total = bands.shape[0] * size
    blocks = bands.shape[1] // LANES
    own = lax.axis_index("strip").astype(jnp.int32).reshape(1)
    weights = prepare_weights(w_in, w_conv, w_track, w_out)
    gathered = gather_strip(device_payload(bands, target, detector, flags, blocks), size)
    return replicated_step(
        gathered, own, weights, w_track.shape, w_conv.shape, table, dilation, rows_total, blocks
    )


def strip_fits(bands, target, w_in, w_conv, w_track, w_out, table, dilation, detector, flags):
    size = lax.axis_size("strip")
    band_count, chan_count = w_in.shape
    rows_local = bands.shape[0]
    rows_total = rows_local * size
    blocks = bands.shape[1] // LANES
    held = rows_total * blocks * SLOTS * chan_count * 44
    return (
        size & (size - 1) == 0
        and chan_count == 2 * HALF
        and band_count * SLOTS == LANES
        and w_conv.shape[2:] == (4, HALF // 2, HALF // 2)
        and w_out.shape[1] == band_count
        and target.shape == (rows_total, LANES)
        and blocks == size
        and blocks % 16 == 0
        and held <= VMEM_BUDGET
    )


def body(*args):
    return body_replicated(*args) if strip_fits(*args) else body_distributed(*args)


def solution(mesh):
    placed = (
        P(("groups", "strip"), None),
        P("groups", "strip"),
        P(),
        P(),
        P(),
        P(),
        P(),
        P(),
        P(("groups", "strip")),
        P(("groups", "strip")),
    )
    return jax.shard_map(
        body,
        mesh=mesh,
        in_specs=placed,
        out_specs=(
            P("groups", "strip"),
            P("groups", None),
            P("groups", None, None, None, None),
            P("groups", None, None, None),
            P("groups", None),
            P("groups", None),
        ),
        check_vma=False,
    )
```

```python
import math

import jax
import jax.numpy as jnp
from jax import lax
from jax.experimental import pallas as pl
from jax.experimental.pallas import tpu as pltpu
from jax.sharding import PartitionSpec as P

INTERPRET = False


def with_halo(x, sides, width):
    for axis, dim in sides:
        size, length = (lax.axis_size(axis), x.shape[dim])
        up = [(i, (i + 1) % size) for i in range(size - 1)]
        down = [(j, i) for i, j in up]
        last = lax.slice_in_dim(x, length - width, length, axis=dim)
        initial = lax.slice_in_dim(x, 0, width, axis=dim)
        before = lax.ppermute(last, axis, up)
        after = lax.ppermute(initial, axis, down)
        x = jnp.concatenate([before, x, after], axis=dim)
    return x


def silu_slope(preact):
    sigmoid_val = jax.nn.sigmoid(preact)
    return sigmoid_val * (1.0 + preact * (1.0 - sigmoid_val))


def block_diagonal(weight):
    groups = weight.shape[2]
    width = weight.shape[3]
    identity = jnp.eye(groups, dtype=weight.dtype)
    spread = weight[:, :, :, :, None, :] * identity[None, None, :, None, :, None]
    return spread.reshape(3, 3, groups * width, groups * width)


def conv_forward(padded, dense_weight):
    row_count = padded.shape[0] - 2
    col_count = padded.shape[1] - 2
    chan_count = padded.shape[2]
    summed = jnp.zeros((row_count * col_count, dense_weight.shape[3]), jnp.float32)
    for i in range(3):
        for j in range(3):
            window = padded[i : i + row_count, j : j + col_count].reshape(-1, chan_count)
            summed = summed + jnp.dot(
                window, dense_weight[i, j], preferred_element_type=jnp.float32
            )
    return summed.reshape(row_count, col_count, -1)


def conv_transpose(padded_grad, dense_weight):
    row_count = padded_grad.shape[0] - 2
    col_count = padded_grad.shape[1] - 2
    chan_count = padded_grad.shape[2]
    summed = jnp.zeros((row_count * col_count, dense_weight.shape[2]), jnp.float32)
    for i in range(3):
        for j in range(3):
            window = padded_grad[2 - i : 2 - i + row_count, 2 - j : 2 - j + col_count].reshape(
                -1, chan_count
            )
            summed = summed + jnp.dot(
                window, dense_weight[i, j].T, preferred_element_type=jnp.float32
            )
    return summed.reshape(row_count, col_count, -1)


def conv_weight_grad(padded, gradient, groups):
    row_count = gradient.shape[0]
    col_count = gradient.shape[1]
    chan_count = gradient.shape[2]
    width = chan_count // groups
    contract = (((0,), (0,)), ((), ()))
    flat_out = gradient.reshape(-1, chan_count)
    rows_of_taps = []
    for i in range(3):
        taps = []
        for j in range(3):
            window = padded[i : i + row_count, j : j + col_count].reshape(-1, chan_count)
            full = lax.dot_general(window, flat_out, contract, preferred_element_type=jnp.float32)
            taps.append(
                jnp.stack(
                    [
                        full[g * width : (g + 1) * width, g * width : (g + 1) * width]
                        for g in range(groups)
                    ]
                )
            )
        rows_of_taps.append(jnp.stack(taps))
    return jnp.stack(rows_of_taps)


def shifted(source, offset, margin):
    padded = jnp.pad(source, ((margin, margin), (0, 0), (0, 0)))
    return lax.dynamic_slice_in_dim(padded, margin + offset, source.shape[0], 0)


def project_pixels(pixels, w_in):
    flat = jnp.dot(pixels.reshape(-1, pixels.shape[2]), w_in, preferred_element_type=jnp.float32)
    return flat.astype(jnp.bfloat16).reshape(pixels.shape[0], pixels.shape[1], w_in.shape[1])


def column_work(
    features, target_block, w_track, w_out, table, dilation, detector, flags, loss_scale
):
    row_count, col_count, chan_count = features.shape
    band_count = w_out.shape[1]
    layers = w_track.shape[0]
    margin = row_count // 4
    contract = (((0,), (0,)), ((), ()))
    selector = (detector[:, None] == jnp.arange(table.shape[0], dtype=jnp.int32)[None, :]).astype(
        jnp.float32
    )
    flag_values = flags.astype(jnp.float32)
    offsets = flag_values[:, None] * jnp.dot(selector, table, precision=lax.Precision.HIGHEST)
    activations = [features]
    preacts = []
    current = features
    for layer_index in range(layers):
        spacing = dilation[layer_index]
        preact = jnp.zeros((row_count * col_count, chan_count), jnp.float32)
        for tap_index in range(3):
            moved_rows = shifted(current, (tap_index - 1) * spacing, margin)
            preact = preact + jnp.dot(
                moved_rows.reshape(-1, chan_count),
                w_track[layer_index, tap_index],
                preferred_element_type=jnp.float32,
            )
        preact = preact.reshape(row_count, col_count, chan_count)
        current = (current.astype(jnp.float32) + jax.nn.silu(preact)).astype(jnp.bfloat16)
        preacts.append(preact)
        activations.append(current)
    raw_output = (
        jnp.dot(current.reshape(-1, chan_count), w_out, preferred_element_type=jnp.float32).reshape(
            row_count, col_count, band_count
        )
        + offsets[None]
    )
    prediction = raw_output.astype(jnp.bfloat16)
    residue = (
        prediction.astype(jnp.float32)
        - target_block.reshape(row_count, col_count, band_count).astype(jnp.float32)
    ) * loss_scale
    residue_b = residue.astype(jnp.bfloat16)
    grad_out = lax.dot_general(
        current.reshape(-1, chan_count),
        residue_b.reshape(-1, band_count),
        contract,
        preferred_element_type=jnp.float32,
    )
    column_sums = jnp.sum(residue, axis=0) * flag_values[:, None]
    grad_table = jnp.dot(selector.T, column_sums, precision=lax.Precision.HIGHEST)
    backward = jnp.dot(
        residue_b.reshape(-1, band_count), w_out.T, preferred_element_type=jnp.float32
    ).reshape(row_count, col_count, chan_count)
    track_grads = [None] * layers
    for layer_index in reversed(range(layers)):
        spacing = dilation[layer_index]
        gate_grad = (backward * silu_slope(preacts[layer_index])).astype(jnp.bfloat16)
        flat_grad = gate_grad.reshape(-1, chan_count)
        tap_grads = []
        for tap_index in range(3):
            moved_rows = shifted(activations[layer_index], (tap_index - 1) * spacing, margin)
            tap_grads.append(
                lax.dot_general(
                    moved_rows.reshape(-1, chan_count),
                    flat_grad,
                    contract,
                    preferred_element_type=jnp.float32,
                )
            )
            pulled = jnp.dot(
                flat_grad, w_track[layer_index, tap_index].T, preferred_element_type=jnp.float32
            ).reshape(row_count, col_count, chan_count)
            backward = backward + shifted(pulled, (1 - tap_index) * spacing, margin)
        track_grads[layer_index] = jnp.stack(tap_grads)
    return (
        backward.astype(jnp.bfloat16),
        prediction.reshape(row_count, col_count * band_count),
        jnp.stack(track_grads),
        grad_out,
        grad_table,
    )


def body_distributed(bands, target, w_in, w_conv, w_track, w_out, table, dilation, detector, flags):
    band_count = w_in.shape[0]
    chan_count = w_in.shape[1]
    groups = w_conv.shape[2]
    device_count = lax.axis_size("strip")
    dense_conv = block_diagonal(w_conv)
    row_count = bands.shape[0]
    col_count = bands.shape[1] // band_count
    pixels = bands.reshape(row_count, col_count, band_count)
    projected = project_pixels(pixels, w_in)
    padded = with_halo(projected, (("strip", 0),), 1)
    padded = jnp.pad(padded, ((0, 0), (1, 1), (0, 0)))
    spatial = conv_forward(padded, dense_conv)
    features = (projected.astype(jnp.float32) + jax.nn.silu(spatial)).astype(jnp.bfloat16)
    feature_cols = lax.all_to_all(features, "strip", split_axis=1, concat_axis=0, tiled=True)
    loss_scale = 1.0 / math.sqrt(feature_cols.shape[0] * feature_cols.shape[1] * device_count)
    feature_grad, prediction, grad_track, grad_out, grad_table = column_work(
        feature_cols, target, w_track, w_out, table, dilation, detector, flags, loss_scale
    )
    local_grad = lax.all_to_all(feature_grad, "strip", split_axis=0, concat_axis=1, tiled=True)
    mixed_grad = (local_grad.astype(jnp.float32) * silu_slope(spatial)).astype(jnp.bfloat16)
    grad_pad = with_halo(mixed_grad, (("strip", 0),), 1)
    grad_pad = jnp.pad(grad_pad, ((0, 0), (1, 1), (0, 0)))
    lifted = (local_grad.astype(jnp.float32) + conv_transpose(grad_pad, dense_conv)).astype(
        jnp.bfloat16
    )
    grad_conv = conv_weight_grad(padded, mixed_grad, groups)
    contract = (((0,), (0,)), ((), ()))
    grad_in = lax.dot_general(
        pixels.reshape(-1, band_count),
        lifted.reshape(-1, chan_count),
        contract,
        preferred_element_type=jnp.float32,
    )
    grad_in, grad_conv, grad_track, grad_out, grad_table = lax.psum(
        (grad_in, grad_conv, grad_track, grad_out, grad_table), "strip"
    )
    return (prediction, grad_in, grad_conv, grad_track, grad_out, grad_table)


LANES = 128
HALF = 64
SLOTS = 4
VMEM_BUDGET = 48 * 1024 * 1024
PREPARE_VMEM = 16 * 1024 * 1024
STEP_VMEM = 32 * 1024 * 1024


def low_half(shape):
    return lax.broadcasted_iota(jnp.int32, shape, len(shape) - 1) % LANES < HALF


def swap_halves(x):
    return pltpu.roll(x, HALF, 1)


def expand_tap(weight):
    turned = swap_halves(weight)
    low = low_half((HALF, LANES))
    zero = jnp.zeros((HALF, LANES), jnp.float32)
    blocks = []
    for h in range(2):
        own = weight[h * HALF : (h + 1) * HALF]
        other = turned[h * HALF : (h + 1) * HALF]
        blocks.append(jnp.concatenate([jnp.where(low, own, zero), jnp.where(low, other, zero)], axis=1))
        blocks.append(jnp.concatenate([jnp.where(low, zero, other), jnp.where(low, zero, own)], axis=1))
    return jnp.concatenate(blocks, axis=0)


def expand_band(weight):
    band_count = weight.shape[0]
    turned = swap_halves(weight)
    low = low_half((band_count, LANES))
    zero = jnp.zeros((band_count, LANES), jnp.float32)
    columns = []
    for h in range(2):
        first, second = (weight, turned) if h == 0 else (turned, weight)
        for pair in range(2):
            rows = [zero] * SLOTS
            rows[2 * pair] = jnp.where(low, first, zero)
            rows[2 * pair + 1] = jnp.where(low, zero, second)
            columns.append(jnp.concatenate(rows, axis=0))
    return jnp.concatenate(columns, axis=1)


INPUT_SLOTS = (0, 1, 2, 3, 4, -1)


def expand_conv(taps, ref, transposed):
    width = taps[0].shape[0]
    low = low_half((HALF, LANES))
    zero = jnp.zeros((HALF, LANES), jnp.float32)
    row = lax.broadcasted_iota(jnp.int32, (HALF, LANES), 0) // width
    lane = lax.broadcasted_iota(jnp.int32, (HALF, LANES), 1) // width % 2
    same = row == lane
    for i in range(3):
        for h in range(2):
            values = []
            for j in range(3):
                tap = taps[3 * i + j]
                turned = swap_halves(tap)
                spread = jnp.where(low[:width], tap, turned) if h == 0 else jnp.where(low[:width], turned, tap)
                values.append(jnp.where(same, jnp.concatenate([spread, spread], axis=0), zero))
            place = 2 - i if transposed else i
            for position, slot in enumerate(INPUT_SLOTS):
                tiles = []
                for pair in range(2):
                    pieces = []
                    for half in range(2):
                        out_slot = 2 * pair + half
                        j = out_slot + 1 - slot if transposed else slot - out_slot + 1
                        pieces.append(values[j] if 0 <= j <= 2 else zero)
                    tiles.append(jnp.where(low, pieces[0], pieces[1]))
                start = (place * len(INPUT_SLOTS) + position) * HALF
                ref[h, start : start + HALF, :] = jnp.concatenate(tiles, axis=1).astype(ref.dtype)


def stay(x):
    return x if INTERPRET else pltpu.with_memory_space_constraint(x, pltpu.HBM)


def fetch(sources, targets, semaphores):
    copies = [pltpu.make_async_copy(a, b, semaphores.at[n]) for n, (a, b) in enumerate(zip(sources, targets))]
    for copy in copies:
        copy.start()
    return copies


def prepare_kernel(*refs):
    sources, (w4, wo4, wc, wt, wf, wb, tt), held, semaphores = refs[:5], refs[5:12], refs[12:17], refs[17]
    w_track, w_conv, w_in, w_out_t, table_t = held
    copies = fetch(sources, held, semaphores)
    for copy in copies:
        copy.wait()
    f32 = jnp.float32
    w4[...] = expand_band(w_in[...].astype(f32)).astype(w4.dtype)
    wo4[...] = expand_band(w_out_t[...].astype(f32)).astype(wo4.dtype)
    width = w_conv.shape[1]
    groups = LANES // width
    taps, taps_t = [], []
    for tap in range(9):
        block = w_conv[tap * LANES : (tap + 1) * LANES, :].astype(f32)
        taps.append(jnp.concatenate([block[g * width : (g + 1) * width] for g in range(groups)], axis=1))
        taps_t.append(block.T)
    expand_conv(taps, wc, False)
    expand_conv(taps_t, wt, True)
    for layer in range(w_track.shape[0]):
        for tap in range(3):
            weight = w_track[layer, tap].astype(f32)
            rows = pl.ds(tap * 2 * LANES, 2 * LANES)
            wf[layer, rows, :] = expand_tap(weight).astype(wf.dtype)
            wb[layer, rows, :] = expand_tap(weight.T).astype(wb.dtype)
    rows, columns = table_t.shape
    for place, part in enumerate(thirds(table_t[...])):
        part = part.astype(f32)
        zero = jnp.zeros_like(part)
        for k in range(SLOTS):
            line = jnp.concatenate([part if k == other else zero for other in range(SLOTS)], axis=1)
            tt[k * rows : (k + 1) * rows, place * SLOTS * columns : (place + 1) * SLOTS * columns] = line.astype(tt.dtype)


def prepare_weights(w_in, w_conv, w_track, w_out, table):
    chan_count = w_in.shape[1]
    width = w_conv.shape[4]
    layers = w_track.shape[0]
    sources = (w_track, w_conv.reshape(-1, width), w_in, w_out.T, table.T)
    shapes = (
        (SLOTS * w_in.shape[0], SLOTS * chan_count),
        (SLOTS * w_out.shape[1], SLOTS * chan_count),
        (2, 18 * HALF, 2 * LANES),
        (2, 18 * HALF, 2 * LANES),
        (layers, 6 * LANES, 2 * LANES),
        (layers, 6 * LANES, 2 * LANES),
        (SLOTS * table.shape[1], 3 * SLOTS * table.shape[0]),
    )
    return pl.pallas_call(
        prepare_kernel,
        out_shape=tuple(jax.ShapeDtypeStruct(s, jnp.bfloat16) for s in shapes),
        in_specs=[pl.BlockSpec(memory_space=pltpu.HBM)] * len(sources),
        scratch_shapes=[pltpu.VMEM(a.shape, a.dtype) for a in sources] + [pltpu.SemaphoreType.DMA((len(sources),))],
        compiler_params=pltpu.CompilerParams(vmem_limit_bytes=PREPARE_VMEM),
        interpret=INTERPRET,
        name="prepare_weights",
    )(*[stay(a) for a in sources])


def silu_and_slope(v):
    s = 0.5 * jnp.tanh(0.5 * v) + 0.5
    return v * s, s * (1.0 + v * (1.0 - s))


def dot(a, b):
    return jnp.dot(a, b, preferred_element_type=jnp.float32)


def dot_tn(a, b):
    return lax.dot_general(a, b, (((0,), (0,)), ((), ())), preferred_element_type=jnp.float32)


def dot_nt(a, b):
    return lax.dot_general(a, b, (((1,), (1,)), ((), ())), preferred_element_type=jnp.float32)


def thirds(x):
    first = x.astype(jnp.bfloat16)
    rest = x - first.astype(jnp.float32)
    second = rest.astype(jnp.bfloat16)
    third = (rest - second.astype(jnp.float32)).astype(jnp.bfloat16)
    return first, second, third


def band_diagonal(full):
    rows = full.shape[0] // SLOTS
    low = low_half((rows, LANES))
    straight, crossed = None, None
    for pair in range(2):
        even = [full[2 * pair * rows : (2 * pair + 1) * rows, (2 * h + pair) * LANES : (2 * h + pair + 1) * LANES] for h in range(2)]
        odd = [full[(2 * pair + 1) * rows : (2 * pair + 2) * rows, (2 * h + pair) * LANES : (2 * h + pair + 1) * LANES] for h in range(2)]
        direct = jnp.where(low, even[0], odd[1])
        swapped = jnp.where(low, even[1], odd[0])
        straight = direct if straight is None else straight + direct
        crossed = swapped if crossed is None else crossed + swapped
    return straight + swap_halves(crossed)


def step_kernel(
    rows_total,
    blocks,
    margin,
    loss_scale,
    own,
    dilation,
    gathered,
    w4,
    wo4,
    wc,
    wt,
    wf,
    wb,
    table_t,
    prediction,
    grad_in,
    grad_conv,
    grad_track,
    grad_out_t,
    grad_table_t,
    pixels,
    target,
    meta,
    proj,
    mixed,
    acts,
    gates,
    slopes,
    backward,
    shown,
):
    size = rows_total * blocks
    strips = gathered.shape[0]
    rows_local = rows_total // strips
    layers = wf.shape[0]
    bf16 = jnp.bfloat16
    f32 = jnp.float32
    mine = own[0]
    bits = strips.bit_length() - 1
    local = rows_local * blocks
    middle = pl.ds(margin * blocks, size)

    for s in range(strips):
        apart = mine ^ s
        place = 0
        for b in range(bits):
            place = place * 2 + ((apart >> b) & 1)
        pixels[s * local : (s + 1) * local, :] = gathered[place, 0:local, :]
        target[pl.ds(s, rows_total, stride=blocks), :] = gathered[place, local : local + rows_total, :].astype(f32)
        meta[s : s + 1, :] = gathered[place, local + rows_total : local + rows_total + 8, :].astype(f32)[0:1]

    for ref in (proj, mixed):
        ref[0:blocks, :] = jnp.zeros((blocks, ref.shape[1]), bf16)
        ref[size + blocks : size + 2 * blocks, :] = jnp.zeros((blocks, ref.shape[1]), bf16)
    edge = jnp.zeros((margin * blocks, acts.shape[2]), bf16)
    for layer in range(layers):
        acts[layer, 0 : margin * blocks, :] = edge
        acts[layer, margin * blocks + size :, :] = edge
    gates[0 : margin * blocks, :] = edge
    gates[margin * blocks + size :, :] = edge

    low = low_half((size, LANES))
    position = lax.broadcasted_iota(jnp.int32, (size, LANES), 0) % blocks
    outside = jnp.where(low, blocks - 1, 0)
    keep = position != outside

    def put_padded(ref, value):
        rounded = value.astype(bf16)
        ref[blocks : blocks + size, 0 : 4 * LANES] = rounded
        wide = rounded.astype(f32)
        for h in range(2):
            following = pltpu.roll(wide[:, 2 * h * LANES : (2 * h + 1) * LANES], size - 1, 0)
            previous = pltpu.roll(wide[:, (2 * h + 1) * LANES : (2 * h + 2) * LANES], 1, 0)
            side = jnp.where(keep, jnp.where(low, following, previous), 0.0)
            ref[blocks : blocks + size, (4 + h) * LANES : (5 + h) * LANES] = side.astype(bf16)

    def window(ref, h, i):
        rows = slice(i * blocks, i * blocks + size)
        return [ref[rows, 2 * h * LANES : (2 * h + 2) * LANES], ref[rows, (4 + h) * LANES : (5 + h) * LANES]]

    put_padded(proj, dot(pixels[...], w4[...]))
    for h in range(2):
        lanes = slice(2 * h * LANES, (2 * h + 2) * LANES)
        left = jnp.concatenate([piece for i in range(3) for piece in window(proj, h, i)], axis=1)
        silu, slope = silu_and_slope(dot(left, wc[h]))
        slopes[layers, :, lanes] = slope
        centre = proj[blocks : blocks + size, lanes].astype(f32)
        acts[0, middle, lanes] = (centre + silu).astype(bf16)

    def tap_window(ref, spacing, sign, pair):
        pieces = []
        for tap in range(3):
            start = pl.multiple_of((margin + sign * (tap - 1) * spacing) * blocks, 16)
            for h in range(2):
                pieces.append(ref[pl.ds(start, size), (2 * h + pair) * LANES : (2 * h + pair + 1) * LANES])
        return jnp.concatenate(pieces, axis=1)

    def forward(layer, carry):
        spacing = dilation[layer]
        for pair in range(2):
            silu, slope = silu_and_slope(dot(tap_window(acts.at[layer], spacing, 1, pair), wf[layer]))
            for h in range(2):
                lanes = slice((2 * h + pair) * LANES, (2 * h + pair + 1) * LANES)
                part = slice(h * LANES, (h + 1) * LANES)
                slopes[layer, :, lanes] = slope[:, part]
                centre = acts[layer, middle, lanes].astype(f32)
                acts[layer + 1, middle, lanes] = (centre + silu[:, part]).astype(bf16)
        return carry

    lax.fori_loop(0, layers, forward, 0)

    det_count = table_t.shape[1] // (3 * SLOTS)
    meta_b = meta[...].astype(bf16)
    source = lax.broadcasted_iota(jnp.int32, (LANES, SLOTS * det_count), 0)
    slot_of = lax.broadcasted_iota(jnp.int32, (LANES, SLOTS * det_count), 1) // det_count
    spread = jnp.where(source == slot_of, 1.0, jnp.where(source == slot_of + SLOTS, 256.0, 0.0)).astype(bf16)
    element = (lax.broadcasted_iota(jnp.int32, (blocks, SLOTS * det_count), 1) % det_count).astype(f32)
    selector = jnp.where(dot(meta_b, spread) == element, 1.0, 0.0).astype(bf16)
    source = lax.broadcasted_iota(jnp.int32, (LANES, LANES), 0)
    slot_of = lax.broadcasted_iota(jnp.int32, (LANES, LANES), 1) // (LANES // SLOTS)
    flag = dot(meta_b, jnp.where(source == slot_of + 2 * SLOTS, 1.0, 0.0).astype(bf16))
    offsets = dot_nt(jnp.concatenate([selector] * 3, axis=1), table_t[...]) * flag

    raw = dot_nt(acts[layers, middle, :], wo4[...]).reshape(rows_total, blocks, LANES) + offsets[None]
    rounded = raw.astype(bf16).astype(f32)
    shown[...] = rounded.reshape(size, LANES)
    prediction[...] = shown[pl.ds(mine, rows_total, stride=blocks), :].astype(bf16)
    residue = (rounded - target[...].reshape(rows_total, blocks, LANES)) * loss_scale
    column_sums = jnp.sum(residue, axis=0) * flag
    residue_b = residue.reshape(size, LANES).astype(bf16)
    backward[...] = dot(residue_b, wo4[...])
    grad_out_t[...] = band_diagonal(dot_tn(residue_b, acts[layers, middle, :]))
    sums = jnp.concatenate(thirds(column_sums), axis=0)
    full = dot_tn(sums, jnp.concatenate([selector] * 3, axis=0))
    band_count = LANES // SLOTS
    grad_table_t[...] = sum(
        full[k * band_count : (k + 1) * band_count, k * det_count : (k + 1) * det_count] for k in range(SLOTS)
    )

    tap_low = low_half((HALF, LANES))

    def back(step, carry):
        layer = layers - 1 - step
        spacing = dilation[layer]
        gates[middle, :] = (backward[...] * slopes[layer]).astype(bf16)
        moved = []
        for pair in range(2):
            right = tap_window(gates, spacing, -1, pair)
            moved.append(right)
            update = dot(right, wb[layer])
            for h in range(2):
                lanes = slice((2 * h + pair) * LANES, (2 * h + pair + 1) * LANES)
                backward[:, lanes] = backward[:, lanes] + update[:, h * LANES : (h + 1) * LANES]
        left = [
            jnp.concatenate(
                [acts[layer, middle, (2 * h + pair) * LANES : (2 * h + pair + 1) * LANES] for h in range(2)], axis=1
            )
            for pair in range(2)
        ]
        full = dot_tn(jnp.concatenate(left, axis=0), jnp.concatenate(moved, axis=0))
        for tap in range(3):
            first = full[:, 2 * tap * LANES : (2 * tap + 1) * LANES]
            second = full[:, (2 * tap + 1) * LANES : (2 * tap + 2) * LANES]
            for h in range(2):
                upper = slice(2 * h * HALF, (2 * h + 1) * HALF)
                lower = slice((2 * h + 1) * HALF, (2 * h + 2) * HALF)
                straight = jnp.where(tap_low, first[upper], second[lower])
                crossed = jnp.where(tap_low, second[upper], first[lower])
                start = pl.multiple_of((layer * 3 + tap) * LANES, LANES) + h * HALF
                grad_track[pl.ds(start, HALF), :] = straight + swap_halves(crossed)
        return carry

    lax.fori_loop(0, layers, back, 0)

    feature_grad = backward[...].astype(bf16).astype(f32)
    put_padded(mixed, feature_grad * slopes[layers])
    lifted = []
    for h in range(2):
        lanes = slice(2 * h * LANES, (2 * h + 2) * LANES)
        left = jnp.concatenate([piece for i in range(3) for piece in window(mixed, h, i)], axis=1)
        lifted.append((backward[:, lanes].astype(bf16).astype(f32) + dot(left, wt[h])).astype(bf16))
    grad_in[...] = band_diagonal(dot_tn(pixels[...], jnp.concatenate(lifted, axis=1)))

    width = grad_conv.shape[1]
    for h in range(2):
        left = jnp.concatenate(window(proj, h, 1), axis=1)
        right = jnp.concatenate(
            [mixed[(2 - i) * blocks : (2 - i) * blocks + size, 2 * h * LANES : (2 * h + 2) * LANES] for i in range(3)],
            axis=1,
        )
        full = dot_tn(left, right)
        for i in range(3):
            for j in range(3):
                parts = []
                for out_slot in range(SLOTS):
                    row = INPUT_SLOTS.index(out_slot + j - 1) * HALF
                    tile = 2 * i + out_slot // 2
                    parts.append(full[row : row + HALF, tile * LANES : (tile + 1) * LANES])
                total = parts[0] + parts[2] + swap_halves(parts[1] + parts[3])
                for g in range(2):
                    start = ((3 * i + j) * 4 + 2 * h + g) * width
                    piece = total[g * width : (g + 1) * width]
                    if g:
                        piece = pltpu.roll(piece, LANES - width, 1)
                    grad_conv[start : start + width, :] = piece[:, :width]


def replicated_step(gathered, own, weights, w_track_shape, w_conv_shape, table_shape, dilation, rows_total, blocks):
    strips = gathered.shape[0]
    layers = w_track_shape[0]
    margin = rows_total // 4
    size = rows_total * blocks
    chan_count = w_track_shape[2]
    det_count, band_count = table_shape
    loss_scale = 1.0 / math.sqrt(rows_total * blocks * SLOTS)
    smem = pl.BlockSpec(memory_space=pltpu.SMEM)
    vmem = pl.BlockSpec(memory_space=pltpu.VMEM)
    f32, bf16 = jnp.float32, jnp.bfloat16
    taps = math.prod(w_conv_shape[:4])
    outs = pl.pallas_call(
        lambda *refs: step_kernel(rows_total, blocks, margin, loss_scale, *refs),
        out_shape=(
            jax.ShapeDtypeStruct((rows_total, LANES), bf16),
            jax.ShapeDtypeStruct((band_count, chan_count), f32),
            jax.ShapeDtypeStruct((taps, w_conv_shape[4]), f32),
            jax.ShapeDtypeStruct((layers * 3 * chan_count, chan_count), f32),
            jax.ShapeDtypeStruct((band_count, chan_count), f32),
            jax.ShapeDtypeStruct((band_count, det_count), f32),
        ),
        in_specs=[smem, smem] + [vmem] * 8,
        out_specs=tuple([vmem] * 6),
        scratch_shapes=[
            pltpu.VMEM((size, LANES), bf16),
            pltpu.VMEM((size, LANES), f32),
            pltpu.VMEM((blocks, LANES), f32),
            pltpu.VMEM((size + 2 * blocks, 6 * LANES), bf16),
            pltpu.VMEM((size + 2 * blocks, 6 * LANES), bf16),
            pltpu.VMEM((layers + 1, size + 2 * margin * blocks, 4 * LANES), bf16),
            pltpu.VMEM((size + 2 * margin * blocks, 4 * LANES), bf16),
            pltpu.VMEM((layers + 1, size, 4 * LANES), f32),
            pltpu.VMEM((size, 4 * LANES), f32),
            pltpu.VMEM((size, LANES), f32),
        ],
        compiler_params=pltpu.CompilerParams(vmem_limit_bytes=STEP_VMEM),
        interpret=INTERPRET,
        name="strip_step",
    )(own, dilation, gathered, *weights)
    prediction, grad_in, grad_conv, grad_track, grad_out_t, grad_table_t = outs
    return (
        prediction,
        grad_in,
        grad_conv.reshape(w_conv_shape),
        grad_track.reshape(w_track_shape),
        grad_out_t.T,
        grad_table_t.T,
    )


def payload_kernel(*refs):
    sources, payload, held, rows, semaphores = refs[:4], refs[4], refs[5:9], refs[9], refs[10]
    bands, target, detector, flags = held
    for copy in fetch(sources, held, semaphores):
        copy.wait()
    blocks = bands.shape[1] // LANES
    rows_local = bands.shape[0]
    local = rows_local * blocks
    wide = bands[...].astype(jnp.float32)
    for block in range(blocks):
        rows[pl.ds(block, rows_local, stride=blocks), :] = wide[:, block * LANES : (block + 1) * LANES]
    payload[0:local, :] = rows[...].astype(payload.dtype)
    payload[local : local + target.shape[0], :] = target[...]
    shape = (8, LANES)
    lane = lax.broadcasted_iota(jnp.int32, shape, 1)
    line = jnp.zeros(shape, jnp.int32)
    for k in range(SLOTS):
        line = jnp.where(lane == k, detector[k] & 255, line)
        line = jnp.where(lane == SLOTS + k, detector[k] >> 8, line)
        line = jnp.where(lane == 2 * SLOTS + k, flags[k], line)
    payload[local + target.shape[0] :, :] = line.astype(jnp.float32).astype(payload.dtype)


def device_payload(bands, target, detector, flags, blocks):
    local = bands.shape[0] * blocks
    return pl.pallas_call(
        payload_kernel,
        out_shape=jax.ShapeDtypeStruct((local + target.shape[0] + 8, LANES), jnp.bfloat16),
        in_specs=[pl.BlockSpec(memory_space=pltpu.HBM)] * 4,
        out_specs=pl.BlockSpec(memory_space=pltpu.VMEM),
        scratch_shapes=[
            pltpu.VMEM(bands.shape, bands.dtype),
            pltpu.VMEM(target.shape, target.dtype),
            pltpu.SMEM(detector.shape, detector.dtype),
            pltpu.SMEM(flags.shape, flags.dtype),
            pltpu.VMEM((local, LANES), jnp.float32),
            pltpu.SemaphoreType.DMA((4,)),
        ],
        compiler_params=pltpu.CompilerParams(vmem_limit_bytes=PREPARE_VMEM),
        interpret=INTERPRET,
        name="payload",
    )(*[stay(a) for a in (bands, target, detector, flags)])


def gather_strip(payload, size):
    held = payload[None]
    distance = size // 2
    while distance:
        pairs = [(i, i ^ distance) for i in range(size)]
        held = jnp.concatenate([held, lax.ppermute(held, "strip", pairs)], axis=0)
        distance //= 2
    return held


def body_replicated(bands, target, w_in, w_conv, w_track, w_out, table, dilation, detector, flags):
    size = lax.axis_size("strip")
    rows_total = bands.shape[0] * size
    blocks = bands.shape[1] // LANES
    own = lax.axis_index("strip").astype(jnp.int32).reshape(1)
    weights = prepare_weights(w_in, w_conv, w_track, w_out, table)
    gathered = gather_strip(device_payload(bands, target, detector, flags, blocks), size)
    return replicated_step(
        gathered, own, weights, w_track.shape, w_conv.shape, table.shape, dilation, rows_total, blocks
    )


def strip_fits(bands, target, w_in, w_conv, w_track, w_out, table, dilation, detector, flags):
    size = lax.axis_size("strip")
    band_count, chan_count = w_in.shape
    rows_local = bands.shape[0]
    rows_total = rows_local * size
    blocks = bands.shape[1] // LANES
    held = rows_total * blocks * SLOTS * chan_count * 44
    return (
        size & (size - 1) == 0
        and chan_count == 2 * HALF
        and band_count * SLOTS == LANES
        and w_conv.shape[2:] == (4, HALF // 2, HALF // 2)
        and w_out.shape[1] == band_count
        and target.shape == (rows_total, LANES)
        and blocks == size
        and blocks % 16 == 0
        and held <= VMEM_BUDGET
    )


def body(*args):
    return body_replicated(*args) if strip_fits(*args) else body_distributed(*args)


def solution(mesh):
    placed = (
        P(("groups", "strip"), None),
        P("groups", "strip"),
        P(),
        P(),
        P(),
        P(),
        P(),
        P(),
        P(("groups", "strip")),
        P(("groups", "strip")),
    )
    return jax.shard_map(
        body,
        mesh=mesh,
        in_specs=placed,
        out_specs=(
            P("groups", "strip"),
            P("groups", None),
            P("groups", None, None, None, None),
            P("groups", None, None, None),
            P("groups", None),
            P("groups", None),
        ),
        check_vma=False,
    )
```

```python
import math

import jax
import jax.numpy as jnp
from jax import lax
from jax.experimental import pallas as pl
from jax.experimental.pallas import tpu as pltpu
from jax.sharding import PartitionSpec as P

INTERPRET = False


def with_halo(x, sides, width):
    for axis, dim in sides:
        size, length = (lax.axis_size(axis), x.shape[dim])
        up = [(i, (i + 1) % size) for i in range(size - 1)]
        down = [(j, i) for i, j in up]
        last = lax.slice_in_dim(x, length - width, length, axis=dim)
        initial = lax.slice_in_dim(x, 0, width, axis=dim)
        before = lax.ppermute(last, axis, up)
        after = lax.ppermute(initial, axis, down)
        x = jnp.concatenate([before, x, after], axis=dim)
    return x


def silu_slope(preact):
    sigmoid_val = jax.nn.sigmoid(preact)
    return sigmoid_val * (1.0 + preact * (1.0 - sigmoid_val))


def block_diagonal(weight):
    groups = weight.shape[2]
    width = weight.shape[3]
    identity = jnp.eye(groups, dtype=weight.dtype)
    spread = weight[:, :, :, :, None, :] * identity[None, None, :, None, :, None]
    return spread.reshape(3, 3, groups * width, groups * width)


def conv_forward(padded, dense_weight):
    row_count = padded.shape[0] - 2
    col_count = padded.shape[1] - 2
    chan_count = padded.shape[2]
    summed = jnp.zeros((row_count * col_count, dense_weight.shape[3]), jnp.float32)
    for i in range(3):
        for j in range(3):
            window = padded[i : i + row_count, j : j + col_count].reshape(-1, chan_count)
            summed = summed + jnp.dot(
                window, dense_weight[i, j], preferred_element_type=jnp.float32
            )
    return summed.reshape(row_count, col_count, -1)


def conv_transpose(padded_grad, dense_weight):
    row_count = padded_grad.shape[0] - 2
    col_count = padded_grad.shape[1] - 2
    chan_count = padded_grad.shape[2]
    summed = jnp.zeros((row_count * col_count, dense_weight.shape[2]), jnp.float32)
    for i in range(3):
        for j in range(3):
            window = padded_grad[2 - i : 2 - i + row_count, 2 - j : 2 - j + col_count].reshape(
                -1, chan_count
            )
            summed = summed + jnp.dot(
                window, dense_weight[i, j].T, preferred_element_type=jnp.float32
            )
    return summed.reshape(row_count, col_count, -1)


def conv_weight_grad(padded, gradient, groups):
    row_count = gradient.shape[0]
    col_count = gradient.shape[1]
    chan_count = gradient.shape[2]
    width = chan_count // groups
    contract = (((0,), (0,)), ((), ()))
    flat_out = gradient.reshape(-1, chan_count)
    rows_of_taps = []
    for i in range(3):
        taps = []
        for j in range(3):
            window = padded[i : i + row_count, j : j + col_count].reshape(-1, chan_count)
            full = lax.dot_general(window, flat_out, contract, preferred_element_type=jnp.float32)
            taps.append(
                jnp.stack(
                    [
                        full[g * width : (g + 1) * width, g * width : (g + 1) * width]
                        for g in range(groups)
                    ]
                )
            )
        rows_of_taps.append(jnp.stack(taps))
    return jnp.stack(rows_of_taps)


def shifted(source, offset, margin):
    padded = jnp.pad(source, ((margin, margin), (0, 0), (0, 0)))
    return lax.dynamic_slice_in_dim(padded, margin + offset, source.shape[0], 0)


def project_pixels(pixels, w_in):
    flat = jnp.dot(pixels.reshape(-1, pixels.shape[2]), w_in, preferred_element_type=jnp.float32)
    return flat.astype(jnp.bfloat16).reshape(pixels.shape[0], pixels.shape[1], w_in.shape[1])


def column_work(
    features, target_block, w_track, w_out, table, dilation, detector, flags, loss_scale
):
    row_count, col_count, chan_count = features.shape
    band_count = w_out.shape[1]
    layers = w_track.shape[0]
    margin = row_count // 4
    contract = (((0,), (0,)), ((), ()))
    selector = (detector[:, None] == jnp.arange(table.shape[0], dtype=jnp.int32)[None, :]).astype(
        jnp.float32
    )
    flag_values = flags.astype(jnp.float32)
    offsets = flag_values[:, None] * jnp.dot(selector, table, precision=lax.Precision.HIGHEST)
    activations = [features]
    preacts = []
    current = features
    for layer_index in range(layers):
        spacing = dilation[layer_index]
        preact = jnp.zeros((row_count * col_count, chan_count), jnp.float32)
        for tap_index in range(3):
            moved_rows = shifted(current, (tap_index - 1) * spacing, margin)
            preact = preact + jnp.dot(
                moved_rows.reshape(-1, chan_count),
                w_track[layer_index, tap_index],
                preferred_element_type=jnp.float32,
            )
        preact = preact.reshape(row_count, col_count, chan_count)
        current = (current.astype(jnp.float32) + jax.nn.silu(preact)).astype(jnp.bfloat16)
        preacts.append(preact)
        activations.append(current)
    raw_output = (
        jnp.dot(current.reshape(-1, chan_count), w_out, preferred_element_type=jnp.float32).reshape(
            row_count, col_count, band_count
        )
        + offsets[None]
    )
    prediction = raw_output.astype(jnp.bfloat16)
    residue = (
        prediction.astype(jnp.float32)
        - target_block.reshape(row_count, col_count, band_count).astype(jnp.float32)
    ) * loss_scale
    residue_b = residue.astype(jnp.bfloat16)
    grad_out = lax.dot_general(
        current.reshape(-1, chan_count),
        residue_b.reshape(-1, band_count),
        contract,
        preferred_element_type=jnp.float32,
    )
    column_sums = jnp.sum(residue, axis=0) * flag_values[:, None]
    grad_table = jnp.dot(selector.T, column_sums, precision=lax.Precision.HIGHEST)
    backward = jnp.dot(
        residue_b.reshape(-1, band_count), w_out.T, preferred_element_type=jnp.float32
    ).reshape(row_count, col_count, chan_count)
    track_grads = [None] * layers
    for layer_index in reversed(range(layers)):
        spacing = dilation[layer_index]
        gate_grad = (backward * silu_slope(preacts[layer_index])).astype(jnp.bfloat16)
        flat_grad = gate_grad.reshape(-1, chan_count)
        tap_grads = []
        for tap_index in range(3):
            moved_rows = shifted(activations[layer_index], (tap_index - 1) * spacing, margin)
            tap_grads.append(
                lax.dot_general(
                    moved_rows.reshape(-1, chan_count),
                    flat_grad,
                    contract,
                    preferred_element_type=jnp.float32,
                )
            )
            pulled = jnp.dot(
                flat_grad, w_track[layer_index, tap_index].T, preferred_element_type=jnp.float32
            ).reshape(row_count, col_count, chan_count)
            backward = backward + shifted(pulled, (1 - tap_index) * spacing, margin)
        track_grads[layer_index] = jnp.stack(tap_grads)
    return (
        backward.astype(jnp.bfloat16),
        prediction.reshape(row_count, col_count * band_count),
        jnp.stack(track_grads),
        grad_out,
        grad_table,
    )


def body_distributed(bands, target, w_in, w_conv, w_track, w_out, table, dilation, detector, flags):
    band_count = w_in.shape[0]
    chan_count = w_in.shape[1]
    groups = w_conv.shape[2]
    device_count = lax.axis_size("strip")
    dense_conv = block_diagonal(w_conv)
    row_count = bands.shape[0]
    col_count = bands.shape[1] // band_count
    pixels = bands.reshape(row_count, col_count, band_count)
    projected = project_pixels(pixels, w_in)
    padded = with_halo(projected, (("strip", 0),), 1)
    padded = jnp.pad(padded, ((0, 0), (1, 1), (0, 0)))
    spatial = conv_forward(padded, dense_conv)
    features = (projected.astype(jnp.float32) + jax.nn.silu(spatial)).astype(jnp.bfloat16)
    feature_cols = lax.all_to_all(features, "strip", split_axis=1, concat_axis=0, tiled=True)
    loss_scale = 1.0 / math.sqrt(feature_cols.shape[0] * feature_cols.shape[1] * device_count)
    feature_grad, prediction, grad_track, grad_out, grad_table = column_work(
        feature_cols, target, w_track, w_out, table, dilation, detector, flags, loss_scale
    )
    local_grad = lax.all_to_all(feature_grad, "strip", split_axis=0, concat_axis=1, tiled=True)
    mixed_grad = (local_grad.astype(jnp.float32) * silu_slope(spatial)).astype(jnp.bfloat16)
    grad_pad = with_halo(mixed_grad, (("strip", 0),), 1)
    grad_pad = jnp.pad(grad_pad, ((0, 0), (1, 1), (0, 0)))
    lifted = (local_grad.astype(jnp.float32) + conv_transpose(grad_pad, dense_conv)).astype(
        jnp.bfloat16
    )
    grad_conv = conv_weight_grad(padded, mixed_grad, groups)
    contract = (((0,), (0,)), ((), ()))
    grad_in = lax.dot_general(
        pixels.reshape(-1, band_count),
        lifted.reshape(-1, chan_count),
        contract,
        preferred_element_type=jnp.float32,
    )
    grad_in, grad_conv, grad_track, grad_out, grad_table = lax.psum(
        (grad_in, grad_conv, grad_track, grad_out, grad_table), "strip"
    )
    return (prediction, grad_in, grad_conv, grad_track, grad_out, grad_table)


LANES = 128
HALF = 64
SLOTS = 4
VMEM_BUDGET = 48 * 1024 * 1024
PREPARE_VMEM = 16 * 1024 * 1024
STEP_VMEM = 32 * 1024 * 1024


def low_half(shape):
    return lax.broadcasted_iota(jnp.int32, shape, len(shape) - 1) % LANES < HALF


def swap_halves(x):
    return pltpu.roll(x, HALF, 1)


def expand_tap(weight):
    turned = swap_halves(weight)
    low = low_half((HALF, LANES))
    zero = jnp.zeros((HALF, LANES), jnp.float32)
    blocks = []
    for h in range(2):
        own = weight[h * HALF : (h + 1) * HALF]
        other = turned[h * HALF : (h + 1) * HALF]
        blocks.append(jnp.concatenate([jnp.where(low, own, zero), jnp.where(low, other, zero)], axis=1))
        blocks.append(jnp.concatenate([jnp.where(low, zero, other), jnp.where(low, zero, own)], axis=1))
    return jnp.concatenate(blocks, axis=0)


def expand_band(weight):
    band_count = weight.shape[0]
    turned = swap_halves(weight)
    low = low_half((band_count, LANES))
    zero = jnp.zeros((band_count, LANES), jnp.float32)
    columns = []
    for pair in range(2):
        for h in range(2):
            first, second = (weight, turned) if h == 0 else (turned, weight)
            rows = [zero] * SLOTS
            rows[2 * pair] = jnp.where(low, first, zero)
            rows[2 * pair + 1] = jnp.where(low, zero, second)
            columns.append(jnp.concatenate(rows, axis=0))
    return jnp.concatenate(columns, axis=1)


INPUT_SLOTS = (0, 1, 2, 3, 4, -1)


def expand_conv(taps, ref, transposed):
    width = taps[0].shape[0]
    low = low_half((HALF, LANES))
    zero = jnp.zeros((HALF, LANES), jnp.float32)
    row = lax.broadcasted_iota(jnp.int32, (HALF, LANES), 0) // width
    lane = lax.broadcasted_iota(jnp.int32, (HALF, LANES), 1) // width % 2
    same = row == lane
    for i in range(3):
        for h in range(2):
            values = []
            for j in range(3):
                tap = taps[3 * i + j]
                turned = swap_halves(tap)
                spread = jnp.where(low[:width], tap, turned) if h == 0 else jnp.where(low[:width], turned, tap)
                values.append(jnp.where(same, jnp.concatenate([spread, spread], axis=0), zero))
            place = 2 - i if transposed else i
            for position, slot in enumerate(INPUT_SLOTS):
                tiles = []
                for pair in range(2):
                    pieces = []
                    for half in range(2):
                        out_slot = 2 * pair + half
                        j = out_slot + 1 - slot if transposed else slot - out_slot + 1
                        pieces.append(values[j] if 0 <= j <= 2 else zero)
                    tiles.append(jnp.where(low, pieces[0], pieces[1]))
                start = (place * len(INPUT_SLOTS) + position) * HALF
                ref[h, start : start + HALF, :] = (0.5 * jnp.concatenate(tiles, axis=1)).astype(ref.dtype)


def stay(x):
    return x if INTERPRET else pltpu.with_memory_space_constraint(x, pltpu.HBM)


def fetch(sources, targets, semaphores):
    copies = [pltpu.make_async_copy(a, b, semaphores.at[n]) for n, (a, b) in enumerate(zip(sources, targets))]
    for copy in copies:
        copy.start()
    return copies


def prepare_kernel(*refs):
    sources, (w4, wo4, wc, wt, wf, wb, tt), held, semaphores = refs[:5], refs[5:12], refs[12:17], refs[17]
    w_track, w_conv, w_in, w_out_t, table_t = held
    copies = fetch(sources, held, semaphores)
    for copy in copies:
        copy.wait()
    f32 = jnp.float32
    w4[...] = expand_band(w_in[...].astype(f32)).astype(w4.dtype)
    wo4[...] = expand_band(w_out_t[...].astype(f32)).astype(wo4.dtype)
    width = w_conv.shape[1]
    groups = LANES // width
    taps, taps_t = [], []
    for tap in range(9):
        block = w_conv[tap * LANES : (tap + 1) * LANES, :].astype(f32)
        taps.append(jnp.concatenate([block[g * width : (g + 1) * width] for g in range(groups)], axis=1))
        taps_t.append(block.T)
    expand_conv(taps, wc, False)
    expand_conv(taps_t, wt, True)
    for layer in range(w_track.shape[0]):
        for tap in range(3):
            weight = 0.5 * w_track[layer, tap].astype(f32)
            rows = pl.ds(tap * 2 * LANES, 2 * LANES)
            wf[layer, rows, :] = expand_tap(weight).astype(wf.dtype)
            wb[layer, rows, :] = expand_tap(weight.T).astype(wb.dtype)
    rows, columns = table_t.shape
    for place, part in enumerate(thirds(table_t[...])):
        part = part.astype(f32)
        zero = jnp.zeros_like(part)
        for k in range(SLOTS):
            line = jnp.concatenate([part if k == other else zero for other in range(SLOTS)], axis=1)
            tt[k * rows : (k + 1) * rows, place * SLOTS * columns : (place + 1) * SLOTS * columns] = line.astype(tt.dtype)


def prepare_weights(w_in, w_conv, w_track, w_out, table):
    chan_count = w_in.shape[1]
    width = w_conv.shape[4]
    layers = w_track.shape[0]
    sources = (w_track, w_conv.reshape(-1, width), w_in, w_out.T, table.T)
    shapes = (
        (SLOTS * w_in.shape[0], SLOTS * chan_count),
        (SLOTS * w_out.shape[1], SLOTS * chan_count),
        (2, 18 * HALF, 2 * LANES),
        (2, 18 * HALF, 2 * LANES),
        (layers, 6 * LANES, 2 * LANES),
        (layers, 6 * LANES, 2 * LANES),
        (SLOTS * table.shape[1], 3 * SLOTS * table.shape[0]),
    )
    return pl.pallas_call(
        prepare_kernel,
        out_shape=tuple(jax.ShapeDtypeStruct(s, jnp.bfloat16) for s in shapes),
        in_specs=[pl.BlockSpec(memory_space=pltpu.HBM)] * len(sources),
        scratch_shapes=[pltpu.VMEM(a.shape, a.dtype) for a in sources] + [pltpu.SemaphoreType.DMA((len(sources),))],
        compiler_params=pltpu.CompilerParams(vmem_limit_bytes=PREPARE_VMEM),
        interpret=INTERPRET,
        name="prepare_weights",
    )(*[stay(a) for a in sources])


def silu_and_slope(u):
    t = jnp.tanh(u)
    double = 1.0 + t
    silu = u * double
    return silu, double + silu * (1.0 - t)


def dot(a, b):
    return jnp.dot(a, b, preferred_element_type=jnp.float32)


def dot_tn(a, b):
    return lax.dot_general(a, b, (((0,), (0,)), ((), ())), preferred_element_type=jnp.float32)


def dot_nt(a, b):
    return lax.dot_general(a, b, (((1,), (1,)), ((), ())), preferred_element_type=jnp.float32)


def thirds(x):
    first = x.astype(jnp.bfloat16)
    rest = x - first.astype(jnp.float32)
    second = rest.astype(jnp.bfloat16)
    third = (rest - second.astype(jnp.float32)).astype(jnp.bfloat16)
    return first, second, third


def band_diagonal(full):
    rows = full.shape[0] // SLOTS
    low = low_half((rows, LANES))
    straight, crossed = None, None
    for pair in range(2):
        tiles = [slice((2 * pair + h) * LANES, (2 * pair + h + 1) * LANES) for h in range(2)]
        even = [full[2 * pair * rows : (2 * pair + 1) * rows, tile] for tile in tiles]
        odd = [full[(2 * pair + 1) * rows : (2 * pair + 2) * rows, tile] for tile in tiles]
        direct = jnp.where(low, even[0], odd[1])
        swapped = jnp.where(low, even[1], odd[0])
        straight = direct if straight is None else straight + direct
        crossed = swapped if crossed is None else crossed + swapped
    return straight + swap_halves(crossed)


TILES = tuple(slice(n * LANES, (n + 1) * LANES) for n in range(4))


def step_kernel(rows_total, blocks, margin, loss_scale, layers, *refs):
    own, dilation, gathered, w4, wo4, wc, wt, wf, wb, table_t = refs[:10]
    prediction, grad_in, grad_conv, grad_track, grad_out_t, grad_table_t = refs[10:16]
    pixels, target, meta, shown, side = refs[16:21]
    rest = list(refs[21:])

    def take(count):
        taken = rest[:count]
        del rest[:count]
        return taken

    proj, proj_side = take(2), take(1)[0]
    mixed, mixed_side = take(2), take(1)[0]
    acts = [take(2) for _ in range(layers + 1)]
    gates = [take(2) for _ in range(layers)]
    slopes = [take(2) for _ in range(layers + 1)]
    backward = [take(2) for _ in range(layers + 1)]

    size = rows_total * blocks
    strips = gathered.shape[0]
    rows_local = rows_total // strips
    bf16 = jnp.bfloat16
    f32 = jnp.float32
    mine = own[0]
    bits = strips.bit_length() - 1
    local = rows_local * blocks
    inner = slice(blocks, blocks + size)
    middle = slice(margin * blocks, margin * blocks + size)

    for s in range(strips):
        apart = mine ^ s
        place = 0
        for b in range(bits):
            place = place * 2 + ((apart >> b) & 1)
        pixels[s * local : (s + 1) * local, :] = gathered[place, 0:local, :]
        target[pl.ds(s, rows_total, stride=blocks), :] = gathered[place, local : local + rows_total, :].astype(f32)
        meta[s : s + 1, :] = gathered[place, local + rows_total : local + rows_total + 8, :].astype(f32)[0:1]

    for ref in (*proj, proj_side, *mixed, mixed_side):
        ref[0:blocks, :] = jnp.zeros((blocks, ref.shape[1]), bf16)
        ref[size + blocks :, :] = jnp.zeros((blocks, ref.shape[1]), bf16)
    edge = jnp.zeros((margin * blocks, 2 * LANES), bf16)
    for ref in [ref for pair in acts[:layers] + gates for ref in pair]:
        ref[0 : margin * blocks, :] = edge
        ref[margin * blocks + size :, :] = edge
    gap = jnp.zeros((rows_total, 8, LANES), f32)
    side[:, :, 0:8, :] = jnp.broadcast_to(gap[None], (4, rows_total, 8, LANES))
    side[:, :, 8 + blocks : 16 + blocks, :] = jnp.broadcast_to(gap[None], (4, rows_total, 8, LANES))

    side_low = low_half((rows_total, blocks, LANES))

    def put_side(ref, values):
        for h in range(2):
            for pair in range(2):
                side[2 * h + pair, :, 8 : 8 + blocks, :] = values[pair][:, TILES[h]].reshape(rows_total, blocks, LANES)
            following = side[2 * h, :, 9 : 9 + blocks, :]
            previous = side[2 * h + 1, :, 7 : 7 + blocks, :]
            ref[inner, TILES[h]] = jnp.where(side_low, following, previous).reshape(size, LANES).astype(bf16)

    def window(pairs, beside, h, i):
        rows = slice(i * blocks, i * blocks + size)
        return [pairs[0][rows, TILES[h]], pairs[1][rows, TILES[h]], beside[rows, TILES[h]]]

    def windows(pairs, beside, h):
        return jnp.concatenate([piece for i in range(3) for piece in window(pairs, beside, h, i)], axis=1)

    projected = dot(pixels[...], w4[...])
    projected = [projected[:, 0 : 2 * LANES], projected[:, 2 * LANES :]]
    for pair in range(2):
        proj[pair][inner, :] = projected[pair].astype(bf16)
    put_side(proj_side, projected)
    for h in range(2):
        silu, slope = silu_and_slope(dot(windows(proj, proj_side, h), wc[h]))
        for pair in range(2):
            slopes[layers][pair][:, TILES[h]] = slope[:, TILES[pair]]
            centre = proj[pair][inner, TILES[h]].astype(f32)
            acts[0][pair][middle, TILES[h]] = (centre + silu[:, TILES[pair]]).astype(bf16)

    def tap_rows(ref, layer, sign):
        pieces = []
        for tap in range(3):
            if tap == 1:
                pieces.append(ref[middle, :])
            else:
                start = pl.multiple_of((margin + sign * (tap - 1) * dilation[layer]) * blocks, 16)
                pieces.append(ref[pl.ds(start, size), :])
        return jnp.concatenate(pieces, axis=1)

    def track(layer, pair):
        return dot(tap_rows(acts[layer][pair], layer, 1), wf[layer])

    sums = [track(0, pair) for pair in range(2)]
    for layer in range(layers):
        for pair in range(2):
            silu, slope = silu_and_slope(sums[pair])
            slopes[layer][pair][...] = slope
            centre = acts[layer][pair][middle, :].astype(f32)
            rows = middle if layer + 1 < layers else slice(0, size)
            acts[layer + 1][pair][rows, :] = (centre + silu).astype(bf16)
            if layer + 1 < layers:
                sums[pair] = track(layer + 1, pair)

    det_count = table_t.shape[1] // (3 * SLOTS)
    meta_b = meta[...].astype(bf16)
    source = lax.broadcasted_iota(jnp.int32, (LANES, SLOTS * det_count), 0)
    slot_of = lax.broadcasted_iota(jnp.int32, (LANES, SLOTS * det_count), 1) // det_count
    spread = jnp.where(source == slot_of, 1.0, jnp.where(source == slot_of + SLOTS, 256.0, 0.0)).astype(bf16)
    element = (lax.broadcasted_iota(jnp.int32, (blocks, SLOTS * det_count), 1) % det_count).astype(f32)
    selector = jnp.where(dot(meta_b, spread) == element, 1.0, 0.0).astype(bf16)
    source = lax.broadcasted_iota(jnp.int32, (LANES, LANES), 0)
    slot_of = lax.broadcasted_iota(jnp.int32, (LANES, LANES), 1) // (LANES // SLOTS)
    flag = dot(meta_b, jnp.where(source == slot_of + 2 * SLOTS, 1.0, 0.0).astype(bf16))
    offsets = dot_nt(jnp.concatenate([selector] * 3, axis=1), table_t[...]) * flag

    last = jnp.concatenate([ref[...] for ref in acts[layers]], axis=1)
    raw = dot_nt(last, wo4[...]).reshape(rows_total, blocks, LANES) + offsets[None]
    rounded = raw.astype(bf16).astype(f32)
    shown[...] = rounded.reshape(size, LANES)
    prediction[...] = shown[pl.ds(mine, rows_total, stride=blocks), :].astype(bf16)
    residue = (rounded - target[...].reshape(rows_total, blocks, LANES)) * loss_scale
    column_sums = jnp.sum(residue, axis=0) * flag
    residue_b = residue.reshape(size, LANES).astype(bf16)
    for pair in range(2):
        backward[layers][pair][...] = dot(residue_b, wo4[:, 2 * pair * LANES : (2 * pair + 2) * LANES])
    grad_out_t[...] = band_diagonal(dot_tn(residue_b, last))
    sums = jnp.concatenate(thirds(column_sums), axis=0)
    full = dot_tn(sums, jnp.concatenate([selector] * 3, axis=0))
    band_count = LANES // SLOTS
    grad_table_t[...] = sum(
        full[k * band_count : (k + 1) * band_count, k * det_count : (k + 1) * det_count] for k in range(SLOTS)
    )

    tap_low = low_half((HALF, LANES))
    for layer in reversed(range(layers)):
        moved = []
        for pair in range(2):
            gates[layer][pair][middle, :] = (backward[layer + 1][pair][...] * slopes[layer][pair][...]).astype(bf16)
            right = tap_rows(gates[layer][pair], layer, -1)
            moved.append(right)
            backward[layer][pair][...] = backward[layer + 1][pair][...] + dot(right, wb[layer])
        left = jnp.concatenate([acts[layer][pair][middle, :] for pair in range(2)], axis=0)
        full = dot_tn(left, jnp.concatenate(moved, axis=0))
        for tap in range(3):
            first = full[:, 2 * tap * LANES : (2 * tap + 1) * LANES]
            second = full[:, (2 * tap + 1) * LANES : (2 * tap + 2) * LANES]
            for h in range(2):
                upper = slice(2 * h * HALF, (2 * h + 1) * HALF)
                lower = slice((2 * h + 1) * HALF, (2 * h + 2) * HALF)
                straight = jnp.where(tap_low, first[upper], second[lower])
                crossed = jnp.where(tap_low, second[upper], first[lower])
                start = (layer * 3 + tap) * LANES + h * HALF
                grad_track[start : start + HALF, :] = 0.5 * (straight + swap_halves(crossed))

    gradients = [backward[0][pair][...].astype(bf16).astype(f32) for pair in range(2)]
    values = [gradients[pair] * slopes[layers][pair][...] for pair in range(2)]
    for pair in range(2):
        mixed[pair][inner, :] = values[pair].astype(bf16)
    put_side(mixed_side, values)
    lifted = [[None, None], [None, None]]
    for h in range(2):
        pulled = dot(windows(mixed, mixed_side, h), wt[h])
        for pair in range(2):
            centre = backward[0][pair][:, TILES[h]].astype(bf16).astype(f32)
            lifted[pair][h] = (centre + pulled[:, TILES[pair]]).astype(bf16)
    grad_in[...] = band_diagonal(dot_tn(pixels[...], jnp.concatenate(lifted[0] + lifted[1], axis=1)))

    width = grad_conv.shape[1]
    for h in range(2):
        left = jnp.concatenate(window(proj, proj_side, h, 1), axis=1)
        right = jnp.concatenate(
            [
                mixed[pair][(2 - i) * blocks : (2 - i) * blocks + size, TILES[h]]
                for i in range(3)
                for pair in range(2)
            ],
            axis=1,
        )
        full = dot_tn(left, right)
        for i in range(3):
            for j in range(3):
                parts = []
                for out_slot in range(SLOTS):
                    row = INPUT_SLOTS.index(out_slot + j - 1) * HALF
                    tile = 2 * i + out_slot // 2
                    parts.append(full[row : row + HALF, tile * LANES : (tile + 1) * LANES])
                total = 0.5 * (parts[0] + parts[2] + swap_halves(parts[1] + parts[3]))
                for g in range(2):
                    start = ((3 * i + j) * 4 + 2 * h + g) * width
                    piece = total[g * width : (g + 1) * width]
                    if g:
                        piece = pltpu.roll(piece, LANES - width, 1)
                    grad_conv[start : start + width, :] = piece[:, :width]


def replicated_step(gathered, own, weights, w_track_shape, w_conv_shape, table_shape, dilation, rows_total, blocks):
    layers = w_track_shape[0]
    margin = rows_total // 4
    size = rows_total * blocks
    chan_count = w_track_shape[2]
    det_count, band_count = table_shape
    loss_scale = 1.0 / math.sqrt(rows_total * blocks * SLOTS)
    smem = pl.BlockSpec(memory_space=pltpu.SMEM)
    vmem = pl.BlockSpec(memory_space=pltpu.VMEM)
    f32, bf16 = jnp.float32, jnp.bfloat16
    taps = math.prod(w_conv_shape[:4])
    wide = 2 * LANES
    ringed = pltpu.VMEM((size + 2 * blocks, wide), bf16)
    spaced = pltpu.VMEM((size + 2 * margin * blocks, wide), bf16)
    outs = pl.pallas_call(
        lambda *refs: step_kernel(rows_total, blocks, margin, loss_scale, layers, *refs),
        out_shape=(
            jax.ShapeDtypeStruct((rows_total, LANES), bf16),
            jax.ShapeDtypeStruct((band_count, chan_count), f32),
            jax.ShapeDtypeStruct((taps, w_conv_shape[4]), f32),
            jax.ShapeDtypeStruct((layers * 3 * chan_count, chan_count), f32),
            jax.ShapeDtypeStruct((band_count, chan_count), f32),
            jax.ShapeDtypeStruct((band_count, det_count), f32),
        ),
        in_specs=[smem, smem] + [vmem] * 8,
        out_specs=tuple([vmem] * 6),
        scratch_shapes=[
            pltpu.VMEM((size, LANES), bf16),
            pltpu.VMEM((size, LANES), f32),
            pltpu.VMEM((blocks, LANES), f32),
            pltpu.VMEM((size, LANES), f32),
            pltpu.VMEM((4, rows_total, blocks + 16, LANES), f32),
        ]
        + [ringed] * 6
        + [spaced] * (2 * layers)
        + [pltpu.VMEM((size, wide), bf16)] * 2
        + [spaced] * (2 * layers)
        + [pltpu.VMEM((size, wide), f32)] * (4 * (layers + 1)),
        compiler_params=pltpu.CompilerParams(vmem_limit_bytes=STEP_VMEM),
        interpret=INTERPRET,
        name="strip_step",
    )(own, dilation, gathered, *weights)
    prediction, grad_in, grad_conv, grad_track, grad_out_t, grad_table_t = outs
    return (
        prediction,
        grad_in,
        grad_conv.reshape(w_conv_shape),
        grad_track.reshape(w_track_shape),
        grad_out_t.T,
        grad_table_t.T,
    )


def payload_kernel(*refs):
    sources, payload, held, rows, semaphores = refs[:4], refs[4], refs[5:9], refs[9], refs[10]
    bands, target, detector, flags = held
    for copy in fetch(sources, held, semaphores):
        copy.wait()
    blocks = bands.shape[1] // LANES
    rows_local = bands.shape[0]
    local = rows_local * blocks
    wide = bands[...].astype(jnp.float32)
    for block in range(blocks):
        rows[pl.ds(block, rows_local, stride=blocks), :] = wide[:, block * LANES : (block + 1) * LANES]
    payload[0:local, :] = rows[...].astype(payload.dtype)
    payload[local : local + target.shape[0], :] = target[...]
    shape = (8, LANES)
    lane = lax.broadcasted_iota(jnp.int32, shape, 1)
    line = jnp.zeros(shape, jnp.int32)
    for k in range(SLOTS):
        line = jnp.where(lane == k, detector[k] & 255, line)
        line = jnp.where(lane == SLOTS + k, detector[k] >> 8, line)
        line = jnp.where(lane == 2 * SLOTS + k, flags[k], line)
    payload[local + target.shape[0] :, :] = line.astype(jnp.float32).astype(payload.dtype)


def device_payload(bands, target, detector, flags, blocks):
    local = bands.shape[0] * blocks
    return pl.pallas_call(
        payload_kernel,
        out_shape=jax.ShapeDtypeStruct((local + target.shape[0] + 8, LANES), jnp.bfloat16),
        in_specs=[pl.BlockSpec(memory_space=pltpu.HBM)] * 4,
        out_specs=pl.BlockSpec(memory_space=pltpu.VMEM),
        scratch_shapes=[
            pltpu.VMEM(bands.shape, bands.dtype),
            pltpu.VMEM(target.shape, target.dtype),
            pltpu.SMEM(detector.shape, detector.dtype),
            pltpu.SMEM(flags.shape, flags.dtype),
            pltpu.VMEM((local, LANES), jnp.float32),
            pltpu.SemaphoreType.DMA((4,)),
        ],
        compiler_params=pltpu.CompilerParams(vmem_limit_bytes=PREPARE_VMEM),
        interpret=INTERPRET,
        name="payload",
    )(*[stay(a) for a in (bands, target, detector, flags)])


def gather_strip(payload, size):
    held = payload[None]
    distance = size // 2
    while distance:
        pairs = [(i, i ^ distance) for i in range(size)]
        held = jnp.concatenate([held, lax.ppermute(held, "strip", pairs)], axis=0)
        distance //= 2
    return held


def body_replicated(bands, target, w_in, w_conv, w_track, w_out, table, dilation, detector, flags):
    size = lax.axis_size("strip")
    rows_total = bands.shape[0] * size
    blocks = bands.shape[1] // LANES
    own = lax.axis_index("strip").astype(jnp.int32).reshape(1)
    weights = prepare_weights(w_in, w_conv, w_track, w_out, table)
    gathered = gather_strip(device_payload(bands, target, detector, flags, blocks), size)
    return replicated_step(
        gathered, own, weights, w_track.shape, w_conv.shape, table.shape, dilation, rows_total, blocks
    )


def strip_fits(bands, target, w_in, w_conv, w_track, w_out, table, dilation, detector, flags):
    size = lax.axis_size("strip")
    band_count, chan_count = w_in.shape
    rows_local = bands.shape[0]
    rows_total = rows_local * size
    blocks = bands.shape[1] // LANES
    held = rows_total * blocks * SLOTS * chan_count * 44
    return (
        size & (size - 1) == 0
        and chan_count == 2 * HALF
        and band_count * SLOTS == LANES
        and w_conv.shape[2:] == (4, HALF // 2, HALF // 2)
        and w_out.shape[1] == band_count
        and target.shape == (rows_total, LANES)
        and blocks == size
        and blocks % 16 == 0
        and held <= VMEM_BUDGET
    )


def body(*args):
    return body_replicated(*args) if strip_fits(*args) else body_distributed(*args)


def solution(mesh):
    placed = (
        P(("groups", "strip"), None),
        P("groups", "strip"),
        P(),
        P(),
        P(),
        P(),
        P(),
        P(),
        P(("groups", "strip")),
        P(("groups", "strip")),
    )
    return jax.shard_map(
        body,
        mesh=mesh,
        in_specs=placed,
        out_specs=(
            P("groups", "strip"),
            P("groups", None),
            P("groups", None, None, None, None),
            P("groups", None, None, None),
            P("groups", None),
            P("groups", None),
        ),
        check_vma=False,
    )
```

```python
import functools
import math

import jax
import jax.numpy as jnp
from jax import lax
from jax.experimental import pallas as pl
from jax.experimental.pallas import tpu as pltpu
from jax.sharding import PartitionSpec as P

INTERPRET = False


def with_halo(x, sides, width):
    for axis, dim in sides:
        size, length = (lax.axis_size(axis), x.shape[dim])
        up = [(i, (i + 1) % size) for i in range(size - 1)]
        down = [(j, i) for i, j in up]
        last = lax.slice_in_dim(x, length - width, length, axis=dim)
        initial = lax.slice_in_dim(x, 0, width, axis=dim)
        before = lax.ppermute(last, axis, up)
        after = lax.ppermute(initial, axis, down)
        x = jnp.concatenate([before, x, after], axis=dim)
    return x


def silu_slope(preact):
    sigmoid_val = jax.nn.sigmoid(preact)
    return sigmoid_val * (1.0 + preact * (1.0 - sigmoid_val))


def block_diagonal(weight):
    groups = weight.shape[2]
    width = weight.shape[3]
    identity = jnp.eye(groups, dtype=weight.dtype)
    spread = weight[:, :, :, :, None, :] * identity[None, None, :, None, :, None]
    return spread.reshape(3, 3, groups * width, groups * width)


def conv_forward(padded, dense_weight):
    row_count = padded.shape[0] - 2
    col_count = padded.shape[1] - 2
    chan_count = padded.shape[2]
    summed = jnp.zeros((row_count * col_count, dense_weight.shape[3]), jnp.float32)
    for i in range(3):
        for j in range(3):
            window = padded[i : i + row_count, j : j + col_count].reshape(-1, chan_count)
            summed = summed + jnp.dot(
                window, dense_weight[i, j], preferred_element_type=jnp.float32
            )
    return summed.reshape(row_count, col_count, -1)


def conv_transpose(padded_grad, dense_weight):
    row_count = padded_grad.shape[0] - 2
    col_count = padded_grad.shape[1] - 2
    chan_count = padded_grad.shape[2]
    summed = jnp.zeros((row_count * col_count, dense_weight.shape[2]), jnp.float32)
    for i in range(3):
        for j in range(3):
            window = padded_grad[2 - i : 2 - i + row_count, 2 - j : 2 - j + col_count].reshape(
                -1, chan_count
            )
            summed = summed + jnp.dot(
                window, dense_weight[i, j].T, preferred_element_type=jnp.float32
            )
    return summed.reshape(row_count, col_count, -1)


def conv_weight_grad(padded, gradient, groups):
    row_count = gradient.shape[0]
    col_count = gradient.shape[1]
    chan_count = gradient.shape[2]
    width = chan_count // groups
    contract = (((0,), (0,)), ((), ()))
    flat_out = gradient.reshape(-1, chan_count)
    rows_of_taps = []
    for i in range(3):
        taps = []
        for j in range(3):
            window = padded[i : i + row_count, j : j + col_count].reshape(-1, chan_count)
            full = lax.dot_general(window, flat_out, contract, preferred_element_type=jnp.float32)
            taps.append(
                jnp.stack(
                    [
                        full[g * width : (g + 1) * width, g * width : (g + 1) * width]
                        for g in range(groups)
                    ]
                )
            )
        rows_of_taps.append(jnp.stack(taps))
    return jnp.stack(rows_of_taps)


def shifted(source, offset, margin):
    padded = jnp.pad(source, ((margin, margin), (0, 0), (0, 0)))
    return lax.dynamic_slice_in_dim(padded, margin + offset, source.shape[0], 0)


def project_pixels(pixels, w_in):
    flat = jnp.dot(pixels.reshape(-1, pixels.shape[2]), w_in, preferred_element_type=jnp.float32)
    return flat.astype(jnp.bfloat16).reshape(pixels.shape[0], pixels.shape[1], w_in.shape[1])


def column_work(
    features, target_block, w_track, w_out, table, dilation, detector, flags, loss_scale
):
    row_count, col_count, chan_count = features.shape
    band_count = w_out.shape[1]
    layers = w_track.shape[0]
    margin = row_count // 4
    contract = (((0,), (0,)), ((), ()))
    selector = (detector[:, None] == jnp.arange(table.shape[0], dtype=jnp.int32)[None, :]).astype(
        jnp.float32
    )
    flag_values = flags.astype(jnp.float32)
    offsets = flag_values[:, None] * jnp.dot(selector, table, precision=lax.Precision.HIGHEST)
    activations = [features]
    preacts = []
    current = features
    for layer_index in range(layers):
        spacing = dilation[layer_index]
        preact = jnp.zeros((row_count * col_count, chan_count), jnp.float32)
        for tap_index in range(3):
            moved_rows = shifted(current, (tap_index - 1) * spacing, margin)
            preact = preact + jnp.dot(
                moved_rows.reshape(-1, chan_count),
                w_track[layer_index, tap_index],
                preferred_element_type=jnp.float32,
            )
        preact = preact.reshape(row_count, col_count, chan_count)
        current = (current.astype(jnp.float32) + jax.nn.silu(preact)).astype(jnp.bfloat16)
        preacts.append(preact)
        activations.append(current)
    raw_output = (
        jnp.dot(current.reshape(-1, chan_count), w_out, preferred_element_type=jnp.float32).reshape(
            row_count, col_count, band_count
        )
        + offsets[None]
    )
    prediction = raw_output.astype(jnp.bfloat16)
    residue = (
        prediction.astype(jnp.float32)
        - target_block.reshape(row_count, col_count, band_count).astype(jnp.float32)
    ) * loss_scale
    residue_b = residue.astype(jnp.bfloat16)
    grad_out = lax.dot_general(
        current.reshape(-1, chan_count),
        residue_b.reshape(-1, band_count),
        contract,
        preferred_element_type=jnp.float32,
    )
    column_sums = jnp.sum(residue, axis=0) * flag_values[:, None]
    grad_table = jnp.dot(selector.T, column_sums, precision=lax.Precision.HIGHEST)
    backward = jnp.dot(
        residue_b.reshape(-1, band_count), w_out.T, preferred_element_type=jnp.float32
    ).reshape(row_count, col_count, chan_count)
    track_grads = [None] * layers
    for layer_index in reversed(range(layers)):
        spacing = dilation[layer_index]
        gate_grad = (backward * silu_slope(preacts[layer_index])).astype(jnp.bfloat16)
        flat_grad = gate_grad.reshape(-1, chan_count)
        tap_grads = []
        for tap_index in range(3):
            moved_rows = shifted(activations[layer_index], (tap_index - 1) * spacing, margin)
            tap_grads.append(
                lax.dot_general(
                    moved_rows.reshape(-1, chan_count),
                    flat_grad,
                    contract,
                    preferred_element_type=jnp.float32,
                )
            )
            pulled = jnp.dot(
                flat_grad, w_track[layer_index, tap_index].T, preferred_element_type=jnp.float32
            ).reshape(row_count, col_count, chan_count)
            backward = backward + shifted(pulled, (1 - tap_index) * spacing, margin)
        track_grads[layer_index] = jnp.stack(tap_grads)
    return (
        backward.astype(jnp.bfloat16),
        prediction.reshape(row_count, col_count * band_count),
        jnp.stack(track_grads),
        grad_out,
        grad_table,
    )


def body_distributed(bands, target, w_in, w_conv, w_track, w_out, table, dilation, detector, flags):
    band_count = w_in.shape[0]
    chan_count = w_in.shape[1]
    groups = w_conv.shape[2]
    device_count = lax.axis_size("strip")
    dense_conv = block_diagonal(w_conv)
    row_count = bands.shape[0]
    col_count = bands.shape[1] // band_count
    pixels = bands.reshape(row_count, col_count, band_count)
    projected = project_pixels(pixels, w_in)
    padded = with_halo(projected, (("strip", 0),), 1)
    padded = jnp.pad(padded, ((0, 0), (1, 1), (0, 0)))
    spatial = conv_forward(padded, dense_conv)
    features = (projected.astype(jnp.float32) + jax.nn.silu(spatial)).astype(jnp.bfloat16)
    feature_cols = lax.all_to_all(features, "strip", split_axis=1, concat_axis=0, tiled=True)
    loss_scale = 1.0 / math.sqrt(feature_cols.shape[0] * feature_cols.shape[1] * device_count)
    feature_grad, prediction, grad_track, grad_out, grad_table = column_work(
        feature_cols, target, w_track, w_out, table, dilation, detector, flags, loss_scale
    )
    local_grad = lax.all_to_all(feature_grad, "strip", split_axis=0, concat_axis=1, tiled=True)
    mixed_grad = (local_grad.astype(jnp.float32) * silu_slope(spatial)).astype(jnp.bfloat16)
    grad_pad = with_halo(mixed_grad, (("strip", 0),), 1)
    grad_pad = jnp.pad(grad_pad, ((0, 0), (1, 1), (0, 0)))
    lifted = (local_grad.astype(jnp.float32) + conv_transpose(grad_pad, dense_conv)).astype(
        jnp.bfloat16
    )
    grad_conv = conv_weight_grad(padded, mixed_grad, groups)
    contract = (((0,), (0,)), ((), ()))
    grad_in = lax.dot_general(
        pixels.reshape(-1, band_count),
        lifted.reshape(-1, chan_count),
        contract,
        preferred_element_type=jnp.float32,
    )
    grad_in, grad_conv, grad_track, grad_out, grad_table = lax.psum(
        (grad_in, grad_conv, grad_track, grad_out, grad_table), "strip"
    )
    return (prediction, grad_in, grad_conv, grad_track, grad_out, grad_table)


LANES = 128
HALF = 64
SLOTS = 4
VMEM_BUDGET = 48 * 1024 * 1024
PREPARE_VMEM = 16 * 1024 * 1024
STEP_VMEM = 32 * 1024 * 1024


def low_half(shape):
    return lax.broadcasted_iota(jnp.int32, shape, len(shape) - 1) % LANES < HALF


def swap_halves(x):
    return pltpu.roll(x, HALF, 1)


def expand_tap(weight):
    turned = swap_halves(weight)
    low = low_half((HALF, LANES))
    zero = jnp.zeros((HALF, LANES), jnp.float32)
    blocks = []
    for h in range(2):
        own = weight[h * HALF : (h + 1) * HALF]
        other = turned[h * HALF : (h + 1) * HALF]
        blocks.append(jnp.concatenate([jnp.where(low, own, zero), jnp.where(low, other, zero)], axis=1))
        blocks.append(jnp.concatenate([jnp.where(low, zero, other), jnp.where(low, zero, own)], axis=1))
    return jnp.concatenate(blocks, axis=0)


def expand_band(weight):
    band_count = weight.shape[0]
    turned = swap_halves(weight)
    low = low_half((band_count, LANES))
    zero = jnp.zeros((band_count, LANES), jnp.float32)
    columns = []
    for pair in range(2):
        for h in range(2):
            first, second = (weight, turned) if h == 0 else (turned, weight)
            rows = [zero] * SLOTS
            rows[2 * pair] = jnp.where(low, first, zero)
            rows[2 * pair + 1] = jnp.where(low, zero, second)
            columns.append(jnp.concatenate(rows, axis=0))
    return jnp.concatenate(columns, axis=1)


INPUT_SLOTS = (0, 1, 2, 3, 4, -1)


def expand_conv(taps, ref, transposed):
    width = taps[0].shape[0]
    low = low_half((HALF, LANES))
    zero = jnp.zeros((HALF, LANES), jnp.float32)
    row = lax.broadcasted_iota(jnp.int32, (HALF, LANES), 0) // width
    lane = lax.broadcasted_iota(jnp.int32, (HALF, LANES), 1) // width % 2
    same = row == lane
    for i in range(3):
        for h in range(2):
            values = []
            for j in range(3):
                tap = taps[3 * i + j]
                turned = swap_halves(tap)
                spread = jnp.where(low[:width], tap, turned) if h == 0 else jnp.where(low[:width], turned, tap)
                values.append(jnp.where(same, jnp.concatenate([spread, spread], axis=0), zero))
            place = 2 - i if transposed else i
            for position, slot in enumerate(INPUT_SLOTS):
                tiles = []
                for pair in range(2):
                    pieces = []
                    for half in range(2):
                        out_slot = 2 * pair + half
                        j = out_slot + 1 - slot if transposed else slot - out_slot + 1
                        pieces.append(values[j] if 0 <= j <= 2 else zero)
                    tiles.append(jnp.where(low, pieces[0], pieces[1]))
                start = (place * len(INPUT_SLOTS) + position) * HALF
                ref[h, start : start + HALF, :] = (0.5 * jnp.concatenate(tiles, axis=1)).astype(ref.dtype)


def stay(x):
    return x if INTERPRET else pltpu.with_memory_space_constraint(x, pltpu.HBM)


def fetch(sources, targets, semaphores):
    copies = [pltpu.make_async_copy(a, b, semaphores.at[n]) for n, (a, b) in enumerate(zip(sources, targets))]
    for copy in copies:
        copy.start()
    return copies


def prepare_kernel(*refs):
    sources, (w4, wo4, wc, wt, wf, wb, tt), held, semaphores = refs[:5], refs[5:12], refs[12:17], refs[17]
    w_track, w_conv, w_in, w_out_t, table_t = held
    copies = fetch(sources, held, semaphores)
    for copy in copies:
        copy.wait()
    f32 = jnp.float32
    w4[...] = expand_band(w_in[...].astype(f32)).astype(w4.dtype)
    wo4[...] = expand_band(w_out_t[...].astype(f32)).astype(wo4.dtype)
    width = w_conv.shape[1]
    groups = LANES // width
    taps, taps_t = [], []
    for tap in range(9):
        block = w_conv[tap * LANES : (tap + 1) * LANES, :].astype(f32)
        taps.append(jnp.concatenate([block[g * width : (g + 1) * width] for g in range(groups)], axis=1))
        taps_t.append(block.T)
    expand_conv(taps, wc, False)
    expand_conv(taps_t, wt, True)
    for layer in range(w_track.shape[0]):
        for tap in range(3):
            weight = 0.5 * w_track[layer, tap].astype(f32)
            rows = pl.ds(tap * 2 * LANES, 2 * LANES)
            wf[layer, rows, :] = expand_tap(weight).astype(wf.dtype)
            wb[layer, rows, :] = expand_tap(weight.T).astype(wb.dtype)
    rows, columns = table_t.shape
    for place, part in enumerate(thirds(table_t[...])):
        part = part.astype(f32)
        zero = jnp.zeros_like(part)
        for k in range(SLOTS):
            line = jnp.concatenate([part if k == other else zero for other in range(SLOTS)], axis=1)
            tt[k * rows : (k + 1) * rows, place * SLOTS * columns : (place + 1) * SLOTS * columns] = line.astype(tt.dtype)


def prepare_weights(w_in, w_conv, w_track, w_out, table):
    chan_count = w_in.shape[1]
    width = w_conv.shape[4]
    layers = w_track.shape[0]
    sources = (w_track, w_conv.reshape(-1, width), w_in, w_out.T, table.T)
    shapes = (
        (SLOTS * w_in.shape[0], SLOTS * chan_count),
        (SLOTS * w_out.shape[1], SLOTS * chan_count),
        (2, 18 * HALF, 2 * LANES),
        (2, 18 * HALF, 2 * LANES),
        (layers, 6 * LANES, 2 * LANES),
        (layers, 6 * LANES, 2 * LANES),
        (SLOTS * table.shape[1], 3 * SLOTS * table.shape[0]),
    )
    return pl.pallas_call(
        prepare_kernel,
        out_shape=tuple(jax.ShapeDtypeStruct(s, jnp.bfloat16) for s in shapes),
        in_specs=[pl.BlockSpec(memory_space=pltpu.HBM)] * len(sources),
        scratch_shapes=[pltpu.VMEM(a.shape, a.dtype) for a in sources] + [pltpu.SemaphoreType.DMA((len(sources),))],
        compiler_params=pltpu.CompilerParams(vmem_limit_bytes=PREPARE_VMEM),
        interpret=INTERPRET,
        name="prepare_weights",
    )(*[stay(a) for a in sources])


def silu_of(u):
    return u * (1.0 + jnp.tanh(u))


def double_slope(u):
    t = jnp.tanh(u)
    double = 1.0 + t
    return double + u * double * (1.0 - t)


def dot(a, b):
    return jnp.dot(a, b, preferred_element_type=jnp.float32)


def dot_tn(a, b):
    return lax.dot_general(a, b, (((0,), (0,)), ((), ())), preferred_element_type=jnp.float32)


def dot_nt(a, b):
    return lax.dot_general(a, b, (((1,), (1,)), ((), ())), preferred_element_type=jnp.float32)


def thirds(x):
    first = x.astype(jnp.bfloat16)
    rest = x - first.astype(jnp.float32)
    second = rest.astype(jnp.bfloat16)
    third = (rest - second.astype(jnp.float32)).astype(jnp.bfloat16)
    return first, second, third


def band_diagonal(full):
    rows = full.shape[0] // SLOTS
    low = low_half((rows, LANES))
    straight, crossed = None, None
    for pair in range(2):
        tiles = [slice((2 * pair + h) * LANES, (2 * pair + h + 1) * LANES) for h in range(2)]
        even = [full[2 * pair * rows : (2 * pair + 1) * rows, tile] for tile in tiles]
        odd = [full[(2 * pair + 1) * rows : (2 * pair + 2) * rows, tile] for tile in tiles]
        direct = jnp.where(low, even[0], odd[1])
        swapped = jnp.where(low, even[1], odd[0])
        straight = direct if straight is None else straight + direct
        crossed = swapped if crossed is None else crossed + swapped
    return straight + swap_halves(crossed)


TILES = tuple(slice(n * LANES, (n + 1) * LANES) for n in range(4))


def step_kernel(rows_total, blocks, margin, loss_scale, layers, position, *refs):
    spacing_in, gathered, w4, wo4, wc, wt, wf, wb, table_t = refs[:9]
    prediction, grad_in, grad_conv, grad_track, grad_out_t, grad_table_t = refs[9:15]
    pixels, target, meta, shown, side, dilation, arrived = refs[15:22]
    rest = list(refs[22:])

    def take(count):
        taken = rest[:count]
        del rest[:count]
        return taken

    proj, proj_side = take(2), take(1)[0]
    mixed, mixed_side = take(2), take(1)[0]
    acts = [take(2) for _ in range(layers + 1)]
    gates = [take(2) for _ in range(layers)]
    halves = [take(2) for _ in range(layers + 1)]
    backward = [take(2) for _ in range(layers + 1)]

    size = rows_total * blocks
    strips = gathered.shape[0]
    rows_local = rows_total // strips
    bf16 = jnp.bfloat16
    f32 = jnp.float32
    mine = position if INTERPRET else lax.axis_index("strip")
    scalars = pltpu.make_async_copy(spacing_in, dilation, arrived)
    scalars.start()
    bits = strips.bit_length() - 1
    local = rows_local * blocks
    inner = slice(blocks, blocks + size)
    middle = slice(margin * blocks, margin * blocks + size)

    for s in range(strips):
        apart = mine ^ s
        place = 0
        for b in range(bits):
            place = place * 2 + ((apart >> b) & 1)
        pixels[s * local : (s + 1) * local, :] = gathered[place, 0:local, :]
        target[pl.ds(s, rows_total, stride=blocks), :] = gathered[place, local : local + rows_total, :].astype(f32)
        meta[s : s + 1, :] = gathered[place, local + rows_total : local + rows_total + 8, :].astype(f32)[0:1]

    for ref in (*proj, proj_side, *mixed, mixed_side):
        ref[0:blocks, :] = jnp.zeros((blocks, ref.shape[1]), bf16)
        ref[size + blocks :, :] = jnp.zeros((blocks, ref.shape[1]), bf16)
    edge = jnp.zeros((margin * blocks, 2 * LANES), bf16)
    for ref in [ref for pair in acts[:layers] + gates for ref in pair]:
        ref[0 : margin * blocks, :] = edge
        ref[margin * blocks + size :, :] = edge
    gap = jnp.zeros((rows_total, 8, LANES), f32)
    side[:, :, 0:8, :] = jnp.broadcast_to(gap[None], (4, rows_total, 8, LANES))
    side[:, :, 8 + blocks : 16 + blocks, :] = jnp.broadcast_to(gap[None], (4, rows_total, 8, LANES))

    scalars.wait()
    zero = pl.multiple_of((dilation[0] >> 16) * 8, 8)
    side_low = low_half((rows_total, blocks, LANES))

    def put_side(ref, values):
        for h in range(2):
            for pair in range(2):
                side[2 * h + pair, :, 8 : 8 + blocks, :] = values[pair][:, TILES[h]].reshape(rows_total, blocks, LANES)
            following = side[2 * h, :, 9 : 9 + blocks, :]
            previous = side[2 * h + 1, :, 7 : 7 + blocks, :]
            ref[inner, TILES[h]] = jnp.where(side_low, following, previous).reshape(size, LANES).astype(bf16)

    def window(pairs, beside, h, i):
        rows = slice(i * blocks, i * blocks + size)
        return [pairs[0][rows, TILES[h]], pairs[1][rows, TILES[h]], beside[rows, TILES[h]]]

    def windows(pairs, beside, h):
        return jnp.concatenate([piece for i in range(3) for piece in window(pairs, beside, h, i)], axis=1)

    projected = dot(pixels[...], w4[...])
    projected = [projected[:, 0 : 2 * LANES], projected[:, 2 * LANES :]]
    for pair in range(2):
        proj[pair][inner, :] = projected[pair].astype(bf16)
    put_side(proj_side, projected)
    for h in range(2):
        left = windows(proj, proj_side, h)
        u = jnp.concatenate([dot(left[: size // 2], wc[h]), dot(left[size // 2 :], wc[h])], axis=0)
        silu = silu_of(u)
        for pair in range(2):
            halves[layers][pair][pl.ds(zero, size), TILES[h]] = u[:, TILES[pair]]
            centre = proj[pair][inner, TILES[h]].astype(f32)
            acts[0][pair][middle, TILES[h]] = (centre + silu[:, TILES[pair]]).astype(bf16)

    def tap_rows(ref, layer, sign):
        pieces = []
        for tap in range(3):
            if tap == 1:
                pieces.append(ref[middle, :])
            else:
                start = pl.multiple_of((margin + sign * (tap - 1) * dilation[layer]) * blocks, 16)
                pieces.append(ref[pl.ds(start, size), :])
        return jnp.concatenate(pieces, axis=1)

    def forward(layer):
        rows = middle if layer + 1 < layers else slice(0, size)
        for pair in range(2):
            part = sums[pair]
            halves[layer][pair][pl.ds(zero, size), :] = part
            centre = acts[layer][pair][middle, :].astype(f32)
            acts[layer + 1][pair][rows, :] = (centre + silu_of(part)).astype(bf16)
            if layer + 1 < layers:
                sums[pair] = track(layer + 1, pair)

    def track(layer, pair):
        left = tap_rows(acts[layer][pair], layer, 1)
        return jnp.concatenate([dot(left[: size // 2], wf[layer]), dot(left[size // 2 :], wf[layer])], axis=0)

    sums = [track(0, pair) for pair in range(2)]
    for layer in range(layers):
        forward(layer)

    det_count = table_t.shape[1] // (3 * SLOTS)
    meta_b = meta[...].astype(bf16)
    source = lax.broadcasted_iota(jnp.int32, (LANES, SLOTS * det_count), 0)
    slot_of = lax.broadcasted_iota(jnp.int32, (LANES, SLOTS * det_count), 1) // det_count
    spread = jnp.where(source == slot_of, 1.0, jnp.where(source == slot_of + SLOTS, 256.0, 0.0)).astype(bf16)
    element = (lax.broadcasted_iota(jnp.int32, (blocks, SLOTS * det_count), 1) % det_count).astype(f32)
    selector = jnp.where(dot(meta_b, spread) == element, 1.0, 0.0).astype(bf16)
    source = lax.broadcasted_iota(jnp.int32, (LANES, LANES), 0)
    slot_of = lax.broadcasted_iota(jnp.int32, (LANES, LANES), 1) // (LANES // SLOTS)
    flag = dot(meta_b, jnp.where(source == slot_of + 2 * SLOTS, 1.0, 0.0).astype(bf16))
    offsets = dot_nt(jnp.concatenate([selector] * 3, axis=1), table_t[...]) * flag

    last = jnp.concatenate([ref[...] for ref in acts[layers]], axis=1)
    raw = dot_nt(last, wo4[...]).reshape(rows_total, blocks, LANES) + offsets[None]
    rounded = raw.astype(bf16).astype(f32)
    shown[...] = rounded.reshape(size, LANES)
    prediction[...] = shown[pl.ds(mine, rows_total, stride=blocks), :].astype(bf16)
    residue = (rounded - target[...].reshape(rows_total, blocks, LANES)) * loss_scale
    column_sums = jnp.sum(residue, axis=0) * flag
    residue_b = residue.reshape(size, LANES).astype(bf16)
    for pair in range(2):
        backward[layers][pair][...] = dot(residue_b, wo4[:, 2 * pair * LANES : (2 * pair + 2) * LANES])
    grad_out_t[...] = band_diagonal(dot_tn(residue_b, last))
    parts = jnp.concatenate(thirds(column_sums), axis=0)
    full = dot_tn(parts, jnp.concatenate([selector] * 3, axis=0))
    band_count = LANES // SLOTS
    grad_table_t[...] = sum(
        full[k * band_count : (k + 1) * band_count, k * det_count : (k + 1) * det_count] for k in range(SLOTS)
    )

    tap_low = low_half((HALF, LANES))

    def hold(layer, above):
        for pair in range(2):
            halves[layer][pair][pl.ds(zero + size, 8), 0:LANES] = backward[above][pair][0:8, 0:LANES]

    def back(layer):
        hold(layer, layer + 1)
        moved = []
        for pair in range(2):
            gates[layer][pair][middle, :] = (backward[layer + 1][pair][...] * double_slope(halves[layer][pair][0:size, :])).astype(bf16)
            right = tap_rows(gates[layer][pair], layer, -1)
            moved.append(right)
        both = jnp.concatenate(moved, axis=0)
        update = dot(both, wb[layer])
        for pair in range(2):
            backward[layer][pair][...] = backward[layer + 1][pair][...] + update[pair * size : (pair + 1) * size]
        left = jnp.concatenate([acts[layer][pair][middle, :] for pair in range(2)], axis=0)
        full = dot_tn(left, both)
        for tap in range(3):
            first = full[:, 2 * tap * LANES : (2 * tap + 1) * LANES]
            second = full[:, (2 * tap + 1) * LANES : (2 * tap + 2) * LANES]
            for h in range(2):
                upper = slice(2 * h * HALF, (2 * h + 1) * HALF)
                lower = slice((2 * h + 1) * HALF, (2 * h + 2) * HALF)
                straight = jnp.where(tap_low, first[upper], second[lower])
                crossed = jnp.where(tap_low, second[upper], first[lower])
                start = (layer * 3 + tap) * LANES + h * HALF
                grad_track[start : start + HALF, :] = 0.5 * (straight + swap_halves(crossed))

    for layer in reversed(range(layers)):
        back(layer)

    hold(layers, 0)
    gradients = [backward[0][pair][...].astype(bf16).astype(f32) for pair in range(2)]
    values = [gradients[pair] * double_slope(halves[layers][pair][0:size, :]) for pair in range(2)]
    for pair in range(2):
        mixed[pair][inner, :] = values[pair].astype(bf16)
    put_side(mixed_side, values)
    lifted = [[None, None], [None, None]]
    for h in range(2):
        pulled = dot(windows(mixed, mixed_side, h), wt[h])
        for pair in range(2):
            centre = backward[0][pair][:, TILES[h]].astype(bf16).astype(f32)
            lifted[pair][h] = (centre + pulled[:, TILES[pair]]).astype(bf16)
    grad_in[...] = band_diagonal(dot_tn(pixels[...], jnp.concatenate(lifted[0] + lifted[1], axis=1)))

    width = grad_conv.shape[1]
    for h in range(2):
        left = jnp.concatenate(window(proj, proj_side, h, 1), axis=1)
        right = jnp.concatenate(
            [
                mixed[pair][(2 - i) * blocks : (2 - i) * blocks + size, TILES[h]]
                for i in range(3)
                for pair in range(2)
            ],
            axis=1,
        )
        full = dot_tn(left, right)
        for i in range(3):
            for j in range(3):
                parts = []
                for out_slot in range(SLOTS):
                    row = INPUT_SLOTS.index(out_slot + j - 1) * HALF
                    tile = 2 * i + out_slot // 2
                    parts.append(full[row : row + HALF, tile * LANES : (tile + 1) * LANES])
                total = 0.5 * (parts[0] + parts[2] + swap_halves(parts[1] + parts[3]))
                for g in range(2):
                    start = ((3 * i + j) * 4 + 2 * h + g) * width
                    piece = total[g * width : (g + 1) * width]
                    if g:
                        piece = pltpu.roll(piece, LANES - width, 1)
                    grad_conv[start : start + width, :] = piece[:, :width]


def replicated_step(gathered, weights, w_track_shape, w_conv_shape, table_shape, dilation, rows_total, blocks, position=None):
    layers = w_track_shape[0]
    margin = rows_total // 4
    size = rows_total * blocks
    chan_count = w_track_shape[2]
    det_count, band_count = table_shape
    loss_scale = 1.0 / math.sqrt(rows_total * blocks * SLOTS)
    vmem = pl.BlockSpec(memory_space=pltpu.VMEM)
    hbm = pl.BlockSpec(memory_space=pltpu.HBM)
    f32, bf16 = jnp.float32, jnp.bfloat16
    taps = math.prod(w_conv_shape[:4])
    wide = 2 * LANES
    ringed = pltpu.VMEM((size + 2 * blocks, wide), bf16)
    spaced = pltpu.VMEM((size + 2 * margin * blocks, wide), bf16)
    outs = pl.pallas_call(
        lambda *refs: step_kernel(rows_total, blocks, margin, loss_scale, layers, position, *refs),
        out_shape=(
            jax.ShapeDtypeStruct((rows_total, LANES), bf16),
            jax.ShapeDtypeStruct((band_count, chan_count), f32),
            jax.ShapeDtypeStruct((taps, w_conv_shape[4]), f32),
            jax.ShapeDtypeStruct((layers * 3 * chan_count, chan_count), f32),
            jax.ShapeDtypeStruct((band_count, chan_count), f32),
            jax.ShapeDtypeStruct((band_count, det_count), f32),
        ),
        in_specs=[hbm] + [vmem] * 8,
        out_specs=tuple([vmem] * 6),
        scratch_shapes=[
            pltpu.VMEM((size, LANES), bf16),
            pltpu.VMEM((size, LANES), f32),
            pltpu.VMEM((blocks, LANES), f32),
            pltpu.VMEM((size, LANES), f32),
            pltpu.VMEM((4, rows_total, blocks + 16, LANES), f32),
            pltpu.SMEM(dilation.shape, dilation.dtype),
            pltpu.SemaphoreType.DMA,
        ]
        + [ringed] * 6
        + [spaced] * (2 * layers)
        + [pltpu.VMEM((size, wide), bf16)] * 2
        + [spaced] * (2 * layers)
        + [pltpu.VMEM((size + 8, wide), f32)] * (2 * (layers + 1))
        + [pltpu.VMEM((size, wide), f32)] * (2 * (layers + 1)),
        compiler_params=pltpu.CompilerParams(vmem_limit_bytes=STEP_VMEM),
        interpret=INTERPRET,
        name="strip_step",
    )(stay(dilation), gathered, *weights)
    prediction, grad_in, grad_conv, grad_track, grad_out_t, grad_table_t = outs
    return (
        prediction,
        grad_in,
        grad_conv.reshape(w_conv_shape),
        grad_track.reshape(w_track_shape),
        grad_out_t.T,
        grad_table_t.T,
    )


def payload_kernel(*refs):
    sources, payload, held, rows, semaphores = refs[:4], refs[4], refs[5:9], refs[9], refs[10]
    bands, target, detector, flags = held
    for copy in fetch(sources, held, semaphores):
        copy.wait()
    blocks = bands.shape[1] // LANES
    rows_local = bands.shape[0]
    local = rows_local * blocks
    wide = bands[...].astype(jnp.float32)
    for block in range(blocks):
        rows[pl.ds(block, rows_local, stride=blocks), :] = wide[:, block * LANES : (block + 1) * LANES]
    payload[0:local, :] = rows[...].astype(payload.dtype)
    payload[local : local + target.shape[0], :] = target[...]
    shape = (8, LANES)
    lane = lax.broadcasted_iota(jnp.int32, shape, 1)
    line = jnp.zeros(shape, jnp.int32)
    for k in range(SLOTS):
        line = jnp.where(lane == k, detector[k] & 255, line)
        line = jnp.where(lane == SLOTS + k, detector[k] >> 8, line)
        line = jnp.where(lane == 2 * SLOTS + k, flags[k], line)
    payload[local + target.shape[0] :, :] = line.astype(jnp.float32).astype(payload.dtype)


def device_payload(bands, target, detector, flags, blocks):
    local = bands.shape[0] * blocks
    return pl.pallas_call(
        payload_kernel,
        out_shape=jax.ShapeDtypeStruct((local + target.shape[0] + 8, LANES), jnp.bfloat16),
        in_specs=[pl.BlockSpec(memory_space=pltpu.HBM)] * 4,
        out_specs=pl.BlockSpec(memory_space=pltpu.VMEM),
        scratch_shapes=[
            pltpu.VMEM(bands.shape, bands.dtype),
            pltpu.VMEM(target.shape, target.dtype),
            pltpu.SMEM(detector.shape, detector.dtype),
            pltpu.SMEM(flags.shape, flags.dtype),
            pltpu.VMEM((local, LANES), jnp.float32),
            pltpu.SemaphoreType.DMA((4,)),
        ],
        compiler_params=pltpu.CompilerParams(vmem_limit_bytes=PREPARE_VMEM),
        interpret=INTERPRET,
        name="payload",
    )(*[stay(a) for a in (bands, target, detector, flags)])


def gather_strip(payload, size):
    held = payload[None]
    distance = size // 2
    while distance:
        pairs = [(i, i ^ distance) for i in range(size)]
        held = jnp.concatenate([held, lax.ppermute(held, "strip", pairs)], axis=0)
        distance //= 2
    return held


def body_replicated(bands, target, w_in, w_conv, w_track, w_out, table, dilation, detector, flags):
    size = lax.axis_size("strip")
    rows_total = bands.shape[0] * size
    blocks = bands.shape[1] // LANES
    weights = prepare_weights(w_in, w_conv, w_track, w_out, table)
    gathered = gather_strip(device_payload(bands, target, detector, flags, blocks), size)
    return replicated_step(
        gathered, weights, w_track.shape, w_conv.shape, table.shape, dilation, rows_total, blocks
    )


def strip_fits(bands, target, w_in, w_conv, w_track, w_out, table, dilation, detector, flags):
    size = lax.axis_size("strip")
    band_count, chan_count = w_in.shape
    rows_local = bands.shape[0]
    rows_total = rows_local * size
    blocks = bands.shape[1] // LANES
    held = rows_total * blocks * SLOTS * chan_count * 44
    return (
        size & (size - 1) == 0
        and chan_count == 2 * HALF
        and band_count * SLOTS == LANES
        and w_conv.shape[2:] == (4, HALF // 2, HALF // 2)
        and w_out.shape[1] == band_count
        and target.shape == (rows_total, LANES)
        and blocks == size
        and blocks % 16 == 0
        and held <= VMEM_BUDGET
    )


def body(*args):
    return body_replicated(*args) if strip_fits(*args) else body_distributed(*args)


def solution(mesh):
    placed = (
        P(("groups", "strip"), None),
        P("groups", "strip"),
        P(),
        P(),
        P(),
        P(),
        P(),
        P(),
        P(("groups", "strip")),
        P(("groups", "strip")),
    )
    return jax.shard_map(
        body,
        mesh=mesh,
        in_specs=placed,
        out_specs=(
            P("groups", "strip"),
            P("groups", None),
            P("groups", None, None, None, None),
            P("groups", None, None, None),
            P("groups", None),
            P("groups", None),
        ),
        check_vma=False,
    )
```

```python
import functools
import math

import jax
import jax.numpy as jnp
from jax import lax
from jax.experimental import pallas as pl
from jax.experimental.pallas import tpu as pltpu
from jax.sharding import PartitionSpec as P

INTERPRET = False


def with_halo(x, sides, width):
    for axis, dim in sides:
        size, length = (lax.axis_size(axis), x.shape[dim])
        up = [(i, (i + 1) % size) for i in range(size - 1)]
        down = [(j, i) for i, j in up]
        last = lax.slice_in_dim(x, length - width, length, axis=dim)
        initial = lax.slice_in_dim(x, 0, width, axis=dim)
        before = lax.ppermute(last, axis, up)
        after = lax.ppermute(initial, axis, down)
        x = jnp.concatenate([before, x, after], axis=dim)
    return x


def silu_slope(preact):
    sigmoid_val = jax.nn.sigmoid(preact)
    return sigmoid_val * (1.0 + preact * (1.0 - sigmoid_val))


def block_diagonal(weight):
    groups = weight.shape[2]
    width = weight.shape[3]
    identity = jnp.eye(groups, dtype=weight.dtype)
    spread = weight[:, :, :, :, None, :] * identity[None, None, :, None, :, None]
    return spread.reshape(3, 3, groups * width, groups * width)


def conv_forward(padded, dense_weight):
    row_count = padded.shape[0] - 2
    col_count = padded.shape[1] - 2
    chan_count = padded.shape[2]
    summed = jnp.zeros((row_count * col_count, dense_weight.shape[3]), jnp.float32)
    for i in range(3):
        for j in range(3):
            window = padded[i : i + row_count, j : j + col_count].reshape(-1, chan_count)
            summed = summed + jnp.dot(
                window, dense_weight[i, j], preferred_element_type=jnp.float32
            )
    return summed.reshape(row_count, col_count, -1)


def conv_transpose(padded_grad, dense_weight):
    row_count = padded_grad.shape[0] - 2
    col_count = padded_grad.shape[1] - 2
    chan_count = padded_grad.shape[2]
    summed = jnp.zeros((row_count * col_count, dense_weight.shape[2]), jnp.float32)
    for i in range(3):
        for j in range(3):
            window = padded_grad[2 - i : 2 - i + row_count, 2 - j : 2 - j + col_count].reshape(
                -1, chan_count
            )
            summed = summed + jnp.dot(
                window, dense_weight[i, j].T, preferred_element_type=jnp.float32
            )
    return summed.reshape(row_count, col_count, -1)


def conv_weight_grad(padded, gradient, groups):
    row_count = gradient.shape[0]
    col_count = gradient.shape[1]
    chan_count = gradient.shape[2]
    width = chan_count // groups
    contract = (((0,), (0,)), ((), ()))
    flat_out = gradient.reshape(-1, chan_count)
    rows_of_taps = []
    for i in range(3):
        taps = []
        for j in range(3):
            window = padded[i : i + row_count, j : j + col_count].reshape(-1, chan_count)
            full = lax.dot_general(window, flat_out, contract, preferred_element_type=jnp.float32)
            taps.append(
                jnp.stack(
                    [
                        full[g * width : (g + 1) * width, g * width : (g + 1) * width]
                        for g in range(groups)
                    ]
                )
            )
        rows_of_taps.append(jnp.stack(taps))
    return jnp.stack(rows_of_taps)


def shifted(source, offset, margin):
    padded = jnp.pad(source, ((margin, margin), (0, 0), (0, 0)))
    return lax.dynamic_slice_in_dim(padded, margin + offset, source.shape[0], 0)


def project_pixels(pixels, w_in):
    flat = jnp.dot(pixels.reshape(-1, pixels.shape[2]), w_in, preferred_element_type=jnp.float32)
    return flat.astype(jnp.bfloat16).reshape(pixels.shape[0], pixels.shape[1], w_in.shape[1])


def column_work(
    features, target_block, w_track, w_out, table, dilation, detector, flags, loss_scale
):
    row_count, col_count, chan_count = features.shape
    band_count = w_out.shape[1]
    layers = w_track.shape[0]
    margin = row_count // 4
    contract = (((0,), (0,)), ((), ()))
    selector = (detector[:, None] == jnp.arange(table.shape[0], dtype=jnp.int32)[None, :]).astype(
        jnp.float32
    )
    flag_values = flags.astype(jnp.float32)
    offsets = flag_values[:, None] * jnp.dot(selector, table, precision=lax.Precision.HIGHEST)
    activations = [features]
    preacts = []
    current = features
    for layer_index in range(layers):
        spacing = dilation[layer_index]
        preact = jnp.zeros((row_count * col_count, chan_count), jnp.float32)
        for tap_index in range(3):
            moved_rows = shifted(current, (tap_index - 1) * spacing, margin)
            preact = preact + jnp.dot(
                moved_rows.reshape(-1, chan_count),
                w_track[layer_index, tap_index],
                preferred_element_type=jnp.float32,
            )
        preact = preact.reshape(row_count, col_count, chan_count)
        current = (current.astype(jnp.float32) + jax.nn.silu(preact)).astype(jnp.bfloat16)
        preacts.append(preact)
        activations.append(current)
    raw_output = (
        jnp.dot(current.reshape(-1, chan_count), w_out, preferred_element_type=jnp.float32).reshape(
            row_count, col_count, band_count
        )
        + offsets[None]
    )
    prediction = raw_output.astype(jnp.bfloat16)
    residue = (
        prediction.astype(jnp.float32)
        - target_block.reshape(row_count, col_count, band_count).astype(jnp.float32)
    ) * loss_scale
    residue_b = residue.astype(jnp.bfloat16)
    grad_out = lax.dot_general(
        current.reshape(-1, chan_count),
        residue_b.reshape(-1, band_count),
        contract,
        preferred_element_type=jnp.float32,
    )
    column_sums = jnp.sum(residue, axis=0) * flag_values[:, None]
    grad_table = jnp.dot(selector.T, column_sums, precision=lax.Precision.HIGHEST)
    backward = jnp.dot(
        residue_b.reshape(-1, band_count), w_out.T, preferred_element_type=jnp.float32
    ).reshape(row_count, col_count, chan_count)
    track_grads = [None] * layers
    for layer_index in reversed(range(layers)):
        spacing = dilation[layer_index]
        gate_grad = (backward * silu_slope(preacts[layer_index])).astype(jnp.bfloat16)
        flat_grad = gate_grad.reshape(-1, chan_count)
        tap_grads = []
        for tap_index in range(3):
            moved_rows = shifted(activations[layer_index], (tap_index - 1) * spacing, margin)
            tap_grads.append(
                lax.dot_general(
                    moved_rows.reshape(-1, chan_count),
                    flat_grad,
                    contract,
                    preferred_element_type=jnp.float32,
                )
            )
            pulled = jnp.dot(
                flat_grad, w_track[layer_index, tap_index].T, preferred_element_type=jnp.float32
            ).reshape(row_count, col_count, chan_count)
            backward = backward + shifted(pulled, (1 - tap_index) * spacing, margin)
        track_grads[layer_index] = jnp.stack(tap_grads)
    return (
        backward.astype(jnp.bfloat16),
        prediction.reshape(row_count, col_count * band_count),
        jnp.stack(track_grads),
        grad_out,
        grad_table,
    )


def body_distributed(bands, target, w_in, w_conv, w_track, w_out, table, dilation, detector, flags):
    band_count = w_in.shape[0]
    chan_count = w_in.shape[1]
    groups = w_conv.shape[2]
    device_count = lax.axis_size("strip")
    dense_conv = block_diagonal(w_conv)
    row_count = bands.shape[0]
    col_count = bands.shape[1] // band_count
    pixels = bands.reshape(row_count, col_count, band_count)
    projected = project_pixels(pixels, w_in)
    padded = with_halo(projected, (("strip", 0),), 1)
    padded = jnp.pad(padded, ((0, 0), (1, 1), (0, 0)))
    spatial = conv_forward(padded, dense_conv)
    features = (projected.astype(jnp.float32) + jax.nn.silu(spatial)).astype(jnp.bfloat16)
    feature_cols = lax.all_to_all(features, "strip", split_axis=1, concat_axis=0, tiled=True)
    loss_scale = 1.0 / math.sqrt(feature_cols.shape[0] * feature_cols.shape[1] * device_count)
    feature_grad, prediction, grad_track, grad_out, grad_table = column_work(
        feature_cols, target, w_track, w_out, table, dilation, detector, flags, loss_scale
    )
    local_grad = lax.all_to_all(feature_grad, "strip", split_axis=0, concat_axis=1, tiled=True)
    mixed_grad = (local_grad.astype(jnp.float32) * silu_slope(spatial)).astype(jnp.bfloat16)
    grad_pad = with_halo(mixed_grad, (("strip", 0),), 1)
    grad_pad = jnp.pad(grad_pad, ((0, 0), (1, 1), (0, 0)))
    lifted = (local_grad.astype(jnp.float32) + conv_transpose(grad_pad, dense_conv)).astype(
        jnp.bfloat16
    )
    grad_conv = conv_weight_grad(padded, mixed_grad, groups)
    contract = (((0,), (0,)), ((), ()))
    grad_in = lax.dot_general(
        pixels.reshape(-1, band_count),
        lifted.reshape(-1, chan_count),
        contract,
        preferred_element_type=jnp.float32,
    )
    grad_in, grad_conv, grad_track, grad_out, grad_table = lax.psum(
        (grad_in, grad_conv, grad_track, grad_out, grad_table), "strip"
    )
    return (prediction, grad_in, grad_conv, grad_track, grad_out, grad_table)


LANES = 128
HALF = 64
SLOTS = 4
VMEM_BUDGET = 48 * 1024 * 1024
PREPARE_VMEM = 16 * 1024 * 1024
STEP_VMEM = 32 * 1024 * 1024


def low_half(shape):
    return lax.broadcasted_iota(jnp.int32, shape, len(shape) - 1) % LANES < HALF


def swap_halves(x):
    return pltpu.roll(x, HALF, 1)


def expand_tap(weight):
    turned = swap_halves(weight)
    low = low_half((HALF, LANES))
    zero = jnp.zeros((HALF, LANES), jnp.float32)
    blocks = []
    for h in range(2):
        own = weight[h * HALF : (h + 1) * HALF]
        other = turned[h * HALF : (h + 1) * HALF]
        blocks.append(jnp.concatenate([jnp.where(low, own, zero), jnp.where(low, other, zero)], axis=1))
        blocks.append(jnp.concatenate([jnp.where(low, zero, other), jnp.where(low, zero, own)], axis=1))
    return jnp.concatenate(blocks, axis=0)


def expand_band(weight):
    band_count = weight.shape[0]
    turned = swap_halves(weight)
    low = low_half((band_count, LANES))
    zero = jnp.zeros((band_count, LANES), jnp.float32)
    columns = []
    for pair in range(2):
        for h in range(2):
            first, second = (weight, turned) if h == 0 else (turned, weight)
            rows = [zero] * SLOTS
            rows[2 * pair] = jnp.where(low, first, zero)
            rows[2 * pair + 1] = jnp.where(low, zero, second)
            columns.append(jnp.concatenate(rows, axis=0))
    return jnp.concatenate(columns, axis=1)


INPUT_SLOTS = (0, 1, 2, 3, 4, -1)


def expand_conv(taps, ref, transposed):
    width = taps[0].shape[0]
    low = low_half((HALF, LANES))
    zero = jnp.zeros((HALF, LANES), jnp.float32)
    row = lax.broadcasted_iota(jnp.int32, (HALF, LANES), 0) // width
    lane = lax.broadcasted_iota(jnp.int32, (HALF, LANES), 1) // width % 2
    same = row == lane
    for i in range(3):
        for h in range(2):
            values = []
            for j in range(3):
                tap = taps[3 * i + j]
                turned = swap_halves(tap)
                spread = jnp.where(low[:width], tap, turned) if h == 0 else jnp.where(low[:width], turned, tap)
                values.append(jnp.where(same, jnp.concatenate([spread, spread], axis=0), zero))
            place = 2 - i if transposed else i
            for position, slot in enumerate(INPUT_SLOTS):
                tiles = []
                for pair in range(2):
                    pieces = []
                    for half in range(2):
                        out_slot = 2 * pair + half
                        j = out_slot + 1 - slot if transposed else slot - out_slot + 1
                        pieces.append(values[j] if 0 <= j <= 2 else zero)
                    tiles.append(jnp.where(low, pieces[0], pieces[1]))
                start = (place * len(INPUT_SLOTS) + position) * HALF
                ref[h, start : start + HALF, :] = (0.5 * jnp.concatenate(tiles, axis=1)).astype(ref.dtype)


def stay(x):
    return x if INTERPRET else pltpu.with_memory_space_constraint(x, pltpu.HBM)


def fetch(sources, targets, semaphores):
    copies = [pltpu.make_async_copy(a, b, semaphores.at[n]) for n, (a, b) in enumerate(zip(sources, targets))]
    for copy in copies:
        copy.start()
    return copies


def prepare_kernel(*refs):
    sources, (w4, wo4, wc, wt, wf, wb, tt), held, semaphores = refs[:5], refs[5:12], refs[12:17], refs[17]
    w_track, w_conv, w_in, w_out_t, table_t = held
    copies = fetch(sources, held, semaphores)
    for copy in copies:
        copy.wait()
    f32 = jnp.float32
    w4[...] = expand_band(w_in[...].astype(f32)).astype(w4.dtype)
    wo4[...] = expand_band(w_out_t[...].astype(f32)).astype(wo4.dtype)
    width = w_conv.shape[1]
    groups = LANES // width
    taps, taps_t = [], []
    for tap in range(9):
        block = w_conv[tap * LANES : (tap + 1) * LANES, :].astype(f32)
        taps.append(jnp.concatenate([block[g * width : (g + 1) * width] for g in range(groups)], axis=1))
        taps_t.append(block.T)
    expand_conv(taps, wc, False)
    expand_conv(taps_t, wt, True)
    for layer in range(w_track.shape[0]):
        for tap in range(3):
            weight = 0.5 * w_track[layer, tap].astype(f32)
            rows = pl.ds(tap * 2 * LANES, 2 * LANES)
            wf[layer, rows, :] = expand_tap(weight).astype(wf.dtype)
            wb[layer, rows, :] = expand_tap(weight.T).astype(wb.dtype)
    rows, columns = table_t.shape
    for place, part in enumerate(thirds(table_t[...])):
        part = part.astype(f32)
        zero = jnp.zeros_like(part)
        for k in range(SLOTS):
            line = jnp.concatenate([part if k == other else zero for other in range(SLOTS)], axis=1)
            tt[k * rows : (k + 1) * rows, place * SLOTS * columns : (place + 1) * SLOTS * columns] = line.astype(tt.dtype)


def prepare_weights(w_in, w_conv, w_track, w_out, table):
    chan_count = w_in.shape[1]
    width = w_conv.shape[4]
    layers = w_track.shape[0]
    sources = (w_track, w_conv.reshape(-1, width), w_in, w_out.T, table.T)
    shapes = (
        (SLOTS * w_in.shape[0], SLOTS * chan_count),
        (SLOTS * w_out.shape[1], SLOTS * chan_count),
        (2, 18 * HALF, 2 * LANES),
        (2, 18 * HALF, 2 * LANES),
        (layers, 6 * LANES, 2 * LANES),
        (layers, 6 * LANES, 2 * LANES),
        (SLOTS * table.shape[1], 3 * SLOTS * table.shape[0]),
    )
    return pl.pallas_call(
        prepare_kernel,
        out_shape=tuple(jax.ShapeDtypeStruct(s, jnp.bfloat16) for s in shapes),
        in_specs=[pl.BlockSpec(memory_space=pltpu.HBM)] * len(sources),
        scratch_shapes=[pltpu.VMEM(a.shape, a.dtype) for a in sources] + [pltpu.SemaphoreType.DMA((len(sources),))],
        compiler_params=pltpu.CompilerParams(vmem_limit_bytes=PREPARE_VMEM),
        interpret=INTERPRET,
        name="prepare_weights",
    )(*[stay(a) for a in sources])


def silu_of(u):
    return u * (1.0 + jnp.tanh(u))


def double_slope(u):
    t = jnp.tanh(u)
    double = 1.0 + t
    return double + u * double * (1.0 - t)


def dot(a, b):
    return jnp.dot(a, b, preferred_element_type=jnp.float32)


def dot_tn(a, b):
    return lax.dot_general(a, b, (((0,), (0,)), ((), ())), preferred_element_type=jnp.float32)


def dot_nt(a, b):
    return lax.dot_general(a, b, (((1,), (1,)), ((), ())), preferred_element_type=jnp.float32)


def thirds(x):
    first = x.astype(jnp.bfloat16)
    rest = x - first.astype(jnp.float32)
    second = rest.astype(jnp.bfloat16)
    third = (rest - second.astype(jnp.float32)).astype(jnp.bfloat16)
    return first, second, third


def band_diagonal(full):
    rows = full.shape[0] // SLOTS
    low = low_half((rows, LANES))
    straight, crossed = None, None
    for pair in range(2):
        tiles = [slice((2 * pair + h) * LANES, (2 * pair + h + 1) * LANES) for h in range(2)]
        even = [full[2 * pair * rows : (2 * pair + 1) * rows, tile] for tile in tiles]
        odd = [full[(2 * pair + 1) * rows : (2 * pair + 2) * rows, tile] for tile in tiles]
        direct = jnp.where(low, even[0], odd[1])
        swapped = jnp.where(low, even[1], odd[0])
        straight = direct if straight is None else straight + direct
        crossed = swapped if crossed is None else crossed + swapped
    return straight + swap_halves(crossed)


TILES = tuple(slice(n * LANES, (n + 1) * LANES) for n in range(4))


def step_kernel(rows_total, blocks, margin, loss_scale, layers, position, *refs):
    spacing_in, gathered, w4, wo4, wc, wt, wf, wb, table_t = refs[:9]
    prediction, grad_in, grad_conv, grad_track, grad_out_t, grad_table_t = refs[9:15]
    pixels, target, meta, shown, side, dilation, arrived = refs[15:22]
    rest = list(refs[22:])

    def take(count):
        taken = rest[:count]
        del rest[:count]
        return taken

    proj, proj_side = take(2), take(1)[0]
    mixed, mixed_side = take(2), take(1)[0]
    acts = [take(2) for _ in range(layers + 1)]
    gates = [take(2) for _ in range(layers)]
    halves = [take(2) for _ in range(layers + 1)]
    backward = [take(2) for _ in range(layers + 1)]

    size = rows_total * blocks
    strips = gathered.shape[0]
    rows_local = rows_total // strips
    bf16 = jnp.bfloat16
    f32 = jnp.float32
    mine = position if INTERPRET else lax.axis_index("strip")
    scalars = pltpu.make_async_copy(spacing_in, dilation, arrived)
    scalars.start()
    bits = strips.bit_length() - 1
    local = rows_local * blocks
    inner = slice(blocks, blocks + size)
    middle = slice(margin * blocks, margin * blocks + size)

    for s in range(strips):
        apart = mine ^ s
        place = 0
        for b in range(bits):
            place = place * 2 + ((apart >> b) & 1)
        pixels[s * local : (s + 1) * local, :] = gathered[place, 0:local, :]
        target[pl.ds(s, rows_total, stride=blocks), :] = gathered[place, local : local + rows_total, :].astype(f32)
        meta[s : s + 1, :] = gathered[place, local + rows_total : local + rows_total + 8, :].astype(f32)[0:1]

    for ref in (*proj, proj_side, *mixed, mixed_side):
        ref[0:blocks, :] = jnp.zeros((blocks, ref.shape[1]), bf16)
        ref[size + blocks :, :] = jnp.zeros((blocks, ref.shape[1]), bf16)
    edge = jnp.zeros((margin * blocks, 2 * LANES), bf16)
    for ref in [ref for pair in acts[:layers] + gates for ref in pair]:
        ref[0 : margin * blocks, :] = edge
        ref[margin * blocks + size :, :] = edge
    gap = jnp.zeros((rows_total, 8, LANES), f32)
    for n in range(4):
        start = 0 if n % 2 else 8 + blocks
        side[n, :, start : start + 8, :] = gap

    scalars.wait()
    zero = pl.multiple_of((dilation[0] >> 16) * 8, 8)
    side_low = low_half((rows_total, blocks, LANES))

    def put_side(ref, values):
        for h in range(2):
            for pair in range(2):
                side[2 * h + pair, :, 8 : 8 + blocks, :] = values[pair][:, TILES[h]].reshape(rows_total, blocks, LANES)
            following = side[2 * h, :, 9 : 9 + blocks, :]
            previous = side[2 * h + 1, :, 7 : 7 + blocks, :]
            ref[inner, TILES[h]] = jnp.where(side_low, following, previous).reshape(size, LANES).astype(bf16)

    def window(pairs, beside, h, i):
        rows = slice(i * blocks, i * blocks + size)
        return [pairs[0][rows, TILES[h]], pairs[1][rows, TILES[h]], beside[rows, TILES[h]]]

    def windows(pairs, beside, h):
        return jnp.concatenate([piece for i in range(3) for piece in window(pairs, beside, h, i)], axis=1)

    projected = dot(pixels[...], w4[...])
    projected = [projected[:, 0 : 2 * LANES], projected[:, 2 * LANES :]]
    for pair in range(2):
        proj[pair][inner, :] = projected[pair].astype(bf16)
    put_side(proj_side, projected)
    for h in range(2):
        left = windows(proj, proj_side, h)
        u = jnp.concatenate([dot(left[: size // 2], wc[h]), dot(left[size // 2 :], wc[h])], axis=0)
        silu = silu_of(u)
        for pair in range(2):
            halves[layers][pair][pl.ds(zero, size), TILES[h]] = u[:, TILES[pair]]
            centre = proj[pair][inner, TILES[h]].astype(f32)
            acts[0][pair][middle, TILES[h]] = (centre + silu[:, TILES[pair]]).astype(bf16)

    def tap_rows(ref, layer, sign):
        pieces = []
        for tap in range(3):
            if tap == 1:
                pieces.append(ref[middle, :])
            else:
                start = pl.multiple_of((margin + sign * (tap - 1) * dilation[layer]) * blocks, 16)
                pieces.append(ref[pl.ds(start, size), :])
        return jnp.concatenate(pieces, axis=1)

    def forward(layer):
        rows = middle if layer + 1 < layers else slice(0, size)
        for pair in range(2):
            part = sums[pair]
            halves[layer][pair][pl.ds(zero, size), :] = part
            centre = acts[layer][pair][middle, :].astype(f32)
            acts[layer + 1][pair][rows, :] = (centre + silu_of(part)).astype(bf16)
            if layer + 1 < layers:
                sums[pair] = track(layer + 1, pair)

    def track(layer, pair):
        left = tap_rows(acts[layer][pair], layer, 1)
        return jnp.concatenate([dot(left[: size // 2], wf[layer]), dot(left[size // 2 :], wf[layer])], axis=0)

    sums = [track(0, pair) for pair in range(2)]
    for layer in range(layers):
        forward(layer)

    det_count = table_t.shape[1] // (3 * SLOTS)
    meta_b = meta[...].astype(bf16)
    source = lax.broadcasted_iota(jnp.int32, (LANES, SLOTS * det_count), 0)
    slot_of = lax.broadcasted_iota(jnp.int32, (LANES, SLOTS * det_count), 1) // det_count
    spread = jnp.where(source == slot_of, 1.0, jnp.where(source == slot_of + SLOTS, 256.0, 0.0)).astype(bf16)
    element = (lax.broadcasted_iota(jnp.int32, (blocks, SLOTS * det_count), 1) % det_count).astype(f32)
    selector = jnp.where(dot(meta_b, spread) == element, 1.0, 0.0).astype(bf16)
    source = lax.broadcasted_iota(jnp.int32, (LANES, LANES), 0)
    slot_of = lax.broadcasted_iota(jnp.int32, (LANES, LANES), 1) // (LANES // SLOTS)
    flag = dot(meta_b, jnp.where(source == slot_of + 2 * SLOTS, 1.0, 0.0).astype(bf16))
    offsets = dot_nt(jnp.concatenate([selector] * 3, axis=1), table_t[...]) * flag

    last = jnp.concatenate([ref[...] for ref in acts[layers]], axis=1)
    raw = dot_nt(last, wo4[...]).reshape(rows_total, blocks, LANES) + offsets[None]
    rounded = raw.astype(bf16).astype(f32)
    shown[...] = rounded.reshape(size, LANES)
    prediction[...] = shown[pl.ds(mine, rows_total, stride=blocks), :].astype(bf16)
    residue = (rounded - target[...].reshape(rows_total, blocks, LANES)) * loss_scale
    column_sums = jnp.sum(residue, axis=0) * flag
    residue_b = residue.reshape(size, LANES).astype(bf16)
    for pair in range(2):
        backward[layers][pair][...] = dot(residue_b, wo4[:, 2 * pair * LANES : (2 * pair + 2) * LANES])
    grad_out_t[...] = band_diagonal(dot_tn(residue_b, last))
    parts = jnp.concatenate(thirds(column_sums), axis=0)
    full = dot_tn(parts, jnp.concatenate([selector] * 3, axis=0))
    band_count = LANES // SLOTS
    grad_table_t[...] = sum(
        full[k * band_count : (k + 1) * band_count, k * det_count : (k + 1) * det_count] for k in range(SLOTS)
    )

    tap_low = low_half((HALF, LANES))

    def hold(layer, above):
        for pair in range(2):
            halves[layer][pair][pl.ds(zero + size, 8), 0:LANES] = backward[above][pair][0:8, 0:LANES]

    def back(layer):
        hold(layer, layer + 1)
        moved = []
        for pair in range(2):
            gates[layer][pair][middle, :] = (backward[layer + 1][pair][...] * double_slope(halves[layer][pair][0:size, :])).astype(bf16)
            right = tap_rows(gates[layer][pair], layer, -1)
            moved.append(right)
        both = jnp.concatenate(moved, axis=0)
        update = dot(both, wb[layer])
        for pair in range(2):
            backward[layer][pair][...] = backward[layer + 1][pair][...] + update[pair * size : (pair + 1) * size]
        left = jnp.concatenate([acts[layer][pair][middle, :] for pair in range(2)], axis=0)
        full = dot_tn(left, both)
        for tap in range(3):
            first = full[:, 2 * tap * LANES : (2 * tap + 1) * LANES]
            second = full[:, (2 * tap + 1) * LANES : (2 * tap + 2) * LANES]
            for h in range(2):
                upper = slice(2 * h * HALF, (2 * h + 1) * HALF)
                lower = slice((2 * h + 1) * HALF, (2 * h + 2) * HALF)
                straight = jnp.where(tap_low, first[upper], second[lower])
                crossed = jnp.where(tap_low, second[upper], first[lower])
                start = (layer * 3 + tap) * LANES + h * HALF
                grad_track[start : start + HALF, :] = 0.5 * (straight + swap_halves(crossed))

    for layer in reversed(range(layers)):
        back(layer)

    hold(layers, 0)
    gradients = [backward[0][pair][...].astype(bf16).astype(f32) for pair in range(2)]
    values = [gradients[pair] * double_slope(halves[layers][pair][0:size, :]) for pair in range(2)]
    for pair in range(2):
        mixed[pair][inner, :] = values[pair].astype(bf16)
    put_side(mixed_side, values)
    lifted = [[None, None], [None, None]]
    for h in range(2):
        pulled = dot(windows(mixed, mixed_side, h), wt[h])
        for pair in range(2):
            centre = backward[0][pair][:, TILES[h]].astype(bf16).astype(f32)
            lifted[pair][h] = (centre + pulled[:, TILES[pair]]).astype(bf16)
    grad_in[...] = band_diagonal(dot_tn(pixels[...], jnp.concatenate(lifted[0] + lifted[1], axis=1)))

    width = grad_conv.shape[1]
    for h in range(2):
        left = jnp.concatenate(window(proj, proj_side, h, 1), axis=1)
        right = jnp.concatenate(
            [
                mixed[pair][(2 - i) * blocks : (2 - i) * blocks + size, TILES[h]]
                for i in range(3)
                for pair in range(2)
            ],
            axis=1,
        )
        full = dot_tn(left, right)
        for i in range(3):
            for j in range(3):
                parts = []
                for out_slot in range(SLOTS):
                    row = INPUT_SLOTS.index(out_slot + j - 1) * HALF
                    tile = 2 * i + out_slot // 2
                    parts.append(full[row : row + HALF, tile * LANES : (tile + 1) * LANES])
                total = 0.5 * (parts[0] + parts[2] + swap_halves(parts[1] + parts[3]))
                for g in range(2):
                    start = ((3 * i + j) * 4 + 2 * h + g) * width
                    piece = total[g * width : (g + 1) * width]
                    if g:
                        piece = pltpu.roll(piece, LANES - width, 1)
                    grad_conv[start : start + width, :] = piece[:, :width]


def replicated_step(gathered, weights, w_track_shape, w_conv_shape, table_shape, dilation, rows_total, blocks, position=None):
    layers = w_track_shape[0]
    margin = rows_total // 4
    size = rows_total * blocks
    chan_count = w_track_shape[2]
    det_count, band_count = table_shape
    loss_scale = 1.0 / math.sqrt(rows_total * blocks * SLOTS)
    vmem = pl.BlockSpec(memory_space=pltpu.VMEM)
    hbm = pl.BlockSpec(memory_space=pltpu.HBM)
    f32, bf16 = jnp.float32, jnp.bfloat16
    taps = math.prod(w_conv_shape[:4])
    wide = 2 * LANES
    ringed = pltpu.VMEM((size + 2 * blocks, wide), bf16)
    spaced = pltpu.VMEM((size + 2 * margin * blocks, wide), bf16)
    outs = pl.pallas_call(
        lambda *refs: step_kernel(rows_total, blocks, margin, loss_scale, layers, position, *refs),
        out_shape=(
            jax.ShapeDtypeStruct((rows_total, LANES), bf16),
            jax.ShapeDtypeStruct((band_count, chan_count), f32),
            jax.ShapeDtypeStruct((taps, w_conv_shape[4]), f32),
            jax.ShapeDtypeStruct((layers * 3 * chan_count, chan_count), f32),
            jax.ShapeDtypeStruct((band_count, chan_count), f32),
            jax.ShapeDtypeStruct((band_count, det_count), f32),
        ),
        in_specs=[hbm] + [vmem] * 8,
        out_specs=tuple([vmem] * 6),
        scratch_shapes=[
            pltpu.VMEM((size, LANES), bf16),
            pltpu.VMEM((size, LANES), f32),
            pltpu.VMEM((blocks, LANES), f32),
            pltpu.VMEM((size, LANES), f32),
            pltpu.VMEM((4, rows_total, blocks + 16, LANES), f32),
            pltpu.SMEM(dilation.shape, dilation.dtype),
            pltpu.SemaphoreType.DMA,
        ]
        + [ringed] * 6
        + [spaced] * (2 * layers)
        + [pltpu.VMEM((size, wide), bf16)] * 2
        + [spaced] * (2 * layers)
        + [pltpu.VMEM((size + 8, wide), f32)] * (2 * (layers + 1))
        + [pltpu.VMEM((size, wide), f32)] * (2 * (layers + 1)),
        compiler_params=pltpu.CompilerParams(vmem_limit_bytes=STEP_VMEM),
        interpret=INTERPRET,
        name="strip_step",
    )(stay(dilation), gathered, *weights)
    prediction, grad_in, grad_conv, grad_track, grad_out_t, grad_table_t = outs
    return (
        prediction,
        grad_in,
        grad_conv.reshape(w_conv_shape),
        grad_track.reshape(w_track_shape),
        grad_out_t.T,
        grad_table_t.T,
    )


def payload_kernel(*refs):
    sources, payload, held, rows, semaphores = refs[:4], refs[4], refs[5:9], refs[9], refs[10]
    bands, target, detector, flags = held
    for copy in fetch(sources, held, semaphores):
        copy.wait()
    blocks = bands.shape[1] // LANES
    rows_local = bands.shape[0]
    local = rows_local * blocks
    wide = bands[...].astype(jnp.float32)
    for block in range(blocks):
        rows[pl.ds(block, rows_local, stride=blocks), :] = wide[:, block * LANES : (block + 1) * LANES]
    payload[0:local, :] = rows[...].astype(payload.dtype)
    payload[local : local + target.shape[0], :] = target[...]
    shape = (8, LANES)
    lane = lax.broadcasted_iota(jnp.int32, shape, 1)
    line = jnp.zeros(shape, jnp.int32)
    for k in range(SLOTS):
        line = jnp.where(lane == k, detector[k] & 255, line)
        line = jnp.where(lane == SLOTS + k, detector[k] >> 8, line)
        line = jnp.where(lane == 2 * SLOTS + k, flags[k], line)
    payload[local + target.shape[0] :, :] = line.astype(jnp.float32).astype(payload.dtype)


def device_payload(bands, target, detector, flags, blocks):
    local = bands.shape[0] * blocks
    return pl.pallas_call(
        payload_kernel,
        out_shape=jax.ShapeDtypeStruct((local + target.shape[0] + 8, LANES), jnp.bfloat16),
        in_specs=[pl.BlockSpec(memory_space=pltpu.HBM)] * 4,
        out_specs=pl.BlockSpec(memory_space=pltpu.VMEM),
        scratch_shapes=[
            pltpu.VMEM(bands.shape, bands.dtype),
            pltpu.VMEM(target.shape, target.dtype),
            pltpu.SMEM(detector.shape, detector.dtype),
            pltpu.SMEM(flags.shape, flags.dtype),
            pltpu.VMEM((local, LANES), jnp.float32),
            pltpu.SemaphoreType.DMA((4,)),
        ],
        compiler_params=pltpu.CompilerParams(vmem_limit_bytes=PREPARE_VMEM),
        interpret=INTERPRET,
        name="payload",
    )(*[stay(a) for a in (bands, target, detector, flags)])


def gather_strip(payload, size):
    held = payload[None]
    distance = size // 2
    while distance:
        pairs = [(i, i ^ distance) for i in range(size)]
        held = jnp.concatenate([held, lax.ppermute(held, "strip", pairs)], axis=0)
        distance //= 2
    return held


def body_replicated(bands, target, w_in, w_conv, w_track, w_out, table, dilation, detector, flags):
    size = lax.axis_size("strip")
    rows_total = bands.shape[0] * size
    blocks = bands.shape[1] // LANES
    weights = prepare_weights(w_in, w_conv, w_track, w_out, table)
    gathered = gather_strip(device_payload(bands, target, detector, flags, blocks), size)
    return replicated_step(
        gathered, weights, w_track.shape, w_conv.shape, table.shape, dilation, rows_total, blocks
    )


def strip_fits(bands, target, w_in, w_conv, w_track, w_out, table, dilation, detector, flags):
    size = lax.axis_size("strip")
    band_count, chan_count = w_in.shape
    rows_local = bands.shape[0]
    rows_total = rows_local * size
    blocks = bands.shape[1] // LANES
    held = rows_total * blocks * SLOTS * chan_count * 44
    return (
        size & (size - 1) == 0
        and chan_count == 2 * HALF
        and band_count * SLOTS == LANES
        and w_conv.shape[2:] == (4, HALF // 2, HALF // 2)
        and w_out.shape[1] == band_count
        and target.shape == (rows_total, LANES)
        and blocks == size
        and blocks % 16 == 0
        and held <= VMEM_BUDGET
    )


def body(*args):
    return body_replicated(*args) if strip_fits(*args) else body_distributed(*args)


def solution(mesh):
    placed = (
        P(("groups", "strip"), None),
        P("groups", "strip"),
        P(),
        P(),
        P(),
        P(),
        P(),
        P(),
        P(("groups", "strip")),
        P(("groups", "strip")),
    )
    return jax.shard_map(
        body,
        mesh=mesh,
        in_specs=placed,
        out_specs=(
            P("groups", "strip"),
            P("groups", None),
            P("groups", None, None, None, None),
            P("groups", None, None, None),
            P("groups", None),
            P("groups", None),
        ),
        check_vma=False,
    )
```

```python
import functools
import math

import jax
import jax.numpy as jnp
from jax import lax
from jax.experimental import pallas as pl
from jax.experimental.pallas import tpu as pltpu
from jax.sharding import PartitionSpec as P

INTERPRET = False


def with_halo(x, sides, width):
    for axis, dim in sides:
        size, length = (lax.axis_size(axis), x.shape[dim])
        up = [(i, (i + 1) % size) for i in range(size - 1)]
        down = [(j, i) for i, j in up]
        last = lax.slice_in_dim(x, length - width, length, axis=dim)
        initial = lax.slice_in_dim(x, 0, width, axis=dim)
        before = lax.ppermute(last, axis, up)
        after = lax.ppermute(initial, axis, down)
        x = jnp.concatenate([before, x, after], axis=dim)
    return x


def silu_slope(preact):
    sigmoid_val = jax.nn.sigmoid(preact)
    return sigmoid_val * (1.0 + preact * (1.0 - sigmoid_val))


def block_diagonal(weight):
    groups = weight.shape[2]
    width = weight.shape[3]
    identity = jnp.eye(groups, dtype=weight.dtype)
    spread = weight[:, :, :, :, None, :] * identity[None, None, :, None, :, None]
    return spread.reshape(3, 3, groups * width, groups * width)


def conv_forward(padded, dense_weight):
    row_count = padded.shape[0] - 2
    col_count = padded.shape[1] - 2
    chan_count = padded.shape[2]
    summed = jnp.zeros((row_count * col_count, dense_weight.shape[3]), jnp.float32)
    for i in range(3):
        for j in range(3):
            window = padded[i : i + row_count, j : j + col_count].reshape(-1, chan_count)
            summed = summed + jnp.dot(
                window, dense_weight[i, j], preferred_element_type=jnp.float32
            )
    return summed.reshape(row_count, col_count, -1)


def conv_transpose(padded_grad, dense_weight):
    row_count = padded_grad.shape[0] - 2
    col_count = padded_grad.shape[1] - 2
    chan_count = padded_grad.shape[2]
    summed = jnp.zeros((row_count * col_count, dense_weight.shape[2]), jnp.float32)
    for i in range(3):
        for j in range(3):
            window = padded_grad[2 - i : 2 - i + row_count, 2 - j : 2 - j + col_count].reshape(
                -1, chan_count
            )
            summed = summed + jnp.dot(
                window, dense_weight[i, j].T, preferred_element_type=jnp.float32
            )
    return summed.reshape(row_count, col_count, -1)


def conv_weight_grad(padded, gradient, groups):
    row_count = gradient.shape[0]
    col_count = gradient.shape[1]
    chan_count = gradient.shape[2]
    width = chan_count // groups
    contract = (((0,), (0,)), ((), ()))
    flat_out = gradient.reshape(-1, chan_count)
    rows_of_taps = []
    for i in range(3):
        taps = []
        for j in range(3):
            window = padded[i : i + row_count, j : j + col_count].reshape(-1, chan_count)
            full = lax.dot_general(window, flat_out, contract, preferred_element_type=jnp.float32)
            taps.append(
                jnp.stack(
                    [
                        full[g * width : (g + 1) * width, g * width : (g + 1) * width]
                        for g in range(groups)
                    ]
                )
            )
        rows_of_taps.append(jnp.stack(taps))
    return jnp.stack(rows_of_taps)


def shifted(source, offset, margin):
    padded = jnp.pad(source, ((margin, margin), (0, 0), (0, 0)))
    return lax.dynamic_slice_in_dim(padded, margin + offset, source.shape[0], 0)


def project_pixels(pixels, w_in):
    flat = jnp.dot(pixels.reshape(-1, pixels.shape[2]), w_in, preferred_element_type=jnp.float32)
    return flat.astype(jnp.bfloat16).reshape(pixels.shape[0], pixels.shape[1], w_in.shape[1])


def column_work(
    features, target_block, w_track, w_out, table, dilation, detector, flags, loss_scale
):
    row_count, col_count, chan_count = features.shape
    band_count = w_out.shape[1]
    layers = w_track.shape[0]
    margin = row_count // 4
    contract = (((0,), (0,)), ((), ()))
    selector = (detector[:, None] == jnp.arange(table.shape[0], dtype=jnp.int32)[None, :]).astype(
        jnp.float32
    )
    flag_values = flags.astype(jnp.float32)
    offsets = flag_values[:, None] * jnp.dot(selector, table, precision=lax.Precision.HIGHEST)
    activations = [features]
    preacts = []
    current = features
    for layer_index in range(layers):
        spacing = dilation[layer_index]
        preact = jnp.zeros((row_count * col_count, chan_count), jnp.float32)
        for tap_index in range(3):
            moved_rows = shifted(current, (tap_index - 1) * spacing, margin)
            preact = preact + jnp.dot(
                moved_rows.reshape(-1, chan_count),
                w_track[layer_index, tap_index],
                preferred_element_type=jnp.float32,
            )
        preact = preact.reshape(row_count, col_count, chan_count)
        current = (current.astype(jnp.float32) + jax.nn.silu(preact)).astype(jnp.bfloat16)
        preacts.append(preact)
        activations.append(current)
    raw_output = (
        jnp.dot(current.reshape(-1, chan_count), w_out, preferred_element_type=jnp.float32).reshape(
            row_count, col_count, band_count
        )
        + offsets[None]
    )
    prediction = raw_output.astype(jnp.bfloat16)
    residue = (
        prediction.astype(jnp.float32)
        - target_block.reshape(row_count, col_count, band_count).astype(jnp.float32)
    ) * loss_scale
    residue_b = residue.astype(jnp.bfloat16)
    grad_out = lax.dot_general(
        current.reshape(-1, chan_count),
        residue_b.reshape(-1, band_count),
        contract,
        preferred_element_type=jnp.float32,
    )
    column_sums = jnp.sum(residue, axis=0) * flag_values[:, None]
    grad_table = jnp.dot(selector.T, column_sums, precision=lax.Precision.HIGHEST)
    backward = jnp.dot(
        residue_b.reshape(-1, band_count), w_out.T, preferred_element_type=jnp.float32
    ).reshape(row_count, col_count, chan_count)
    track_grads = [None] * layers
    for layer_index in reversed(range(layers)):
        spacing = dilation[layer_index]
        gate_grad = (backward * silu_slope(preacts[layer_index])).astype(jnp.bfloat16)
        flat_grad = gate_grad.reshape(-1, chan_count)
        tap_grads = []
        for tap_index in range(3):
            moved_rows = shifted(activations[layer_index], (tap_index - 1) * spacing, margin)
            tap_grads.append(
                lax.dot_general(
                    moved_rows.reshape(-1, chan_count),
                    flat_grad,
                    contract,
                    preferred_element_type=jnp.float32,
                )
            )
            pulled = jnp.dot(
                flat_grad, w_track[layer_index, tap_index].T, preferred_element_type=jnp.float32
            ).reshape(row_count, col_count, chan_count)
            backward = backward + shifted(pulled, (1 - tap_index) * spacing, margin)
        track_grads[layer_index] = jnp.stack(tap_grads)
    return (
        backward.astype(jnp.bfloat16),
        prediction.reshape(row_count, col_count * band_count),
        jnp.stack(track_grads),
        grad_out,
        grad_table,
    )


def body_distributed(bands, target, w_in, w_conv, w_track, w_out, table, dilation, detector, flags):
    band_count = w_in.shape[0]
    chan_count = w_in.shape[1]
    groups = w_conv.shape[2]
    device_count = lax.axis_size("strip")
    dense_conv = block_diagonal(w_conv)
    row_count = bands.shape[0]
    col_count = bands.shape[1] // band_count
    pixels = bands.reshape(row_count, col_count, band_count)
    projected = project_pixels(pixels, w_in)
    padded = with_halo(projected, (("strip", 0),), 1)
    padded = jnp.pad(padded, ((0, 0), (1, 1), (0, 0)))
    spatial = conv_forward(padded, dense_conv)
    features = (projected.astype(jnp.float32) + jax.nn.silu(spatial)).astype(jnp.bfloat16)
    feature_cols = lax.all_to_all(features, "strip", split_axis=1, concat_axis=0, tiled=True)
    loss_scale = 1.0 / math.sqrt(feature_cols.shape[0] * feature_cols.shape[1] * device_count)
    feature_grad, prediction, grad_track, grad_out, grad_table = column_work(
        feature_cols, target, w_track, w_out, table, dilation, detector, flags, loss_scale
    )
    local_grad = lax.all_to_all(feature_grad, "strip", split_axis=0, concat_axis=1, tiled=True)
    mixed_grad = (local_grad.astype(jnp.float32) * silu_slope(spatial)).astype(jnp.bfloat16)
    grad_pad = with_halo(mixed_grad, (("strip", 0),), 1)
    grad_pad = jnp.pad(grad_pad, ((0, 0), (1, 1), (0, 0)))
    lifted = (local_grad.astype(jnp.float32) + conv_transpose(grad_pad, dense_conv)).astype(
        jnp.bfloat16
    )
    grad_conv = conv_weight_grad(padded, mixed_grad, groups)
    contract = (((0,), (0,)), ((), ()))
    grad_in = lax.dot_general(
        pixels.reshape(-1, band_count),
        lifted.reshape(-1, chan_count),
        contract,
        preferred_element_type=jnp.float32,
    )
    grad_in, grad_conv, grad_track, grad_out, grad_table = lax.psum(
        (grad_in, grad_conv, grad_track, grad_out, grad_table), "strip"
    )
    return (prediction, grad_in, grad_conv, grad_track, grad_out, grad_table)


LANES = 128
HALF = 64
SLOTS = 4
VMEM_BUDGET = 48 * 1024 * 1024
PREPARE_VMEM = 16 * 1024 * 1024
STEP_VMEM = 32 * 1024 * 1024


def low_half(shape):
    return lax.broadcasted_iota(jnp.int32, shape, len(shape) - 1) % LANES < HALF


def swap_halves(x):
    return pltpu.roll(x, HALF, 1)


def expand_tap(weight):
    turned = swap_halves(weight)
    low = low_half((HALF, LANES))
    zero = jnp.zeros((HALF, LANES), jnp.float32)
    blocks = []
    for h in range(2):
        own = weight[h * HALF : (h + 1) * HALF]
        other = turned[h * HALF : (h + 1) * HALF]
        blocks.append(jnp.concatenate([jnp.where(low, own, zero), jnp.where(low, other, zero)], axis=1))
        blocks.append(jnp.concatenate([jnp.where(low, zero, other), jnp.where(low, zero, own)], axis=1))
    return jnp.concatenate(blocks, axis=0)


def expand_band(weight):
    band_count = weight.shape[0]
    turned = swap_halves(weight)
    low = low_half((band_count, LANES))
    zero = jnp.zeros((band_count, LANES), jnp.float32)
    columns = []
    for pair in range(2):
        for h in range(2):
            first, second = (weight, turned) if h == 0 else (turned, weight)
            rows = [zero] * SLOTS
            rows[2 * pair] = jnp.where(low, first, zero)
            rows[2 * pair + 1] = jnp.where(low, zero, second)
            columns.append(jnp.concatenate(rows, axis=0))
    return jnp.concatenate(columns, axis=1)


INPUT_SLOTS = (0, 1, 2, 3, 4, -1)


def expand_conv(taps, ref, transposed):
    width = taps[0].shape[0]
    low = low_half((HALF, LANES))
    zero = jnp.zeros((HALF, LANES), jnp.float32)
    row = lax.broadcasted_iota(jnp.int32, (HALF, LANES), 0) // width
    lane = lax.broadcasted_iota(jnp.int32, (HALF, LANES), 1) // width % 2
    same = row == lane
    for i in range(3):
        for h in range(2):
            values = []
            for j in range(3):
                tap = taps[3 * i + j]
                turned = swap_halves(tap)
                spread = jnp.where(low[:width], tap, turned) if h == 0 else jnp.where(low[:width], turned, tap)
                values.append(jnp.where(same, jnp.concatenate([spread, spread], axis=0), zero))
            place = 2 - i if transposed else i
            for position, slot in enumerate(INPUT_SLOTS):
                tiles = []
                for pair in range(2):
                    pieces = []
                    for half in range(2):
                        out_slot = 2 * pair + half
                        j = out_slot + 1 - slot if transposed else slot - out_slot + 1
                        pieces.append(values[j] if 0 <= j <= 2 else zero)
                    tiles.append(jnp.where(low, pieces[0], pieces[1]))
                start = (place * len(INPUT_SLOTS) + position) * HALF
                ref[h, start : start + HALF, :] = (0.5 * jnp.concatenate(tiles, axis=1)).astype(ref.dtype)


def stay(x):
    return x if INTERPRET else pltpu.with_memory_space_constraint(x, pltpu.HBM)


def fetch(sources, targets, semaphores):
    copies = [pltpu.make_async_copy(a, b, semaphores.at[n]) for n, (a, b) in enumerate(zip(sources, targets))]
    for copy in copies:
        copy.start()
    return copies


def prepare_kernel(*refs):
    sources, (w4, wo4, wc, wt, wf, wb, tt), held, semaphores = refs[:5], refs[5:12], refs[12:17], refs[17]
    w_track, w_conv, w_in, w_out_t, table_t = held
    copies = fetch(sources, held, semaphores)
    for copy in copies:
        copy.wait()
    f32 = jnp.float32
    w4[...] = expand_band(w_in[...].astype(f32)).astype(w4.dtype)
    wo4[...] = expand_band(w_out_t[...].astype(f32)).astype(wo4.dtype)
    width = w_conv.shape[1]
    groups = LANES // width
    taps, taps_t = [], []
    for tap in range(9):
        block = w_conv[tap * LANES : (tap + 1) * LANES, :].astype(f32)
        taps.append(jnp.concatenate([block[g * width : (g + 1) * width] for g in range(groups)], axis=1))
        taps_t.append(block.T)
    expand_conv(taps, wc, False)
    expand_conv(taps_t, wt, True)
    for layer in range(w_track.shape[0]):
        for tap in range(3):
            weight = 0.5 * w_track[layer, tap].astype(f32)
            rows = pl.ds(tap * 2 * LANES, 2 * LANES)
            wf[layer, rows, :] = expand_tap(weight).astype(wf.dtype)
            wb[layer, rows, :] = expand_tap(weight.T).astype(wb.dtype)
    rows, columns = table_t.shape
    for place, part in enumerate(thirds(table_t[...])):
        part = part.astype(f32)
        zero = jnp.zeros_like(part)
        for k in range(SLOTS):
            line = jnp.concatenate([part if k == other else zero for other in range(SLOTS)], axis=1)
            tt[k * rows : (k + 1) * rows, place * SLOTS * columns : (place + 1) * SLOTS * columns] = line.astype(tt.dtype)


def prepare_weights(w_in, w_conv, w_track, w_out, table):
    chan_count = w_in.shape[1]
    width = w_conv.shape[4]
    layers = w_track.shape[0]
    sources = (w_track, w_conv.reshape(-1, width), w_in, w_out.T, table.T)
    shapes = (
        (SLOTS * w_in.shape[0], SLOTS * chan_count),
        (SLOTS * w_out.shape[1], SLOTS * chan_count),
        (2, 18 * HALF, 2 * LANES),
        (2, 18 * HALF, 2 * LANES),
        (layers, 6 * LANES, 2 * LANES),
        (layers, 6 * LANES, 2 * LANES),
        (SLOTS * table.shape[1], 3 * SLOTS * table.shape[0]),
    )
    return pl.pallas_call(
        prepare_kernel,
        out_shape=tuple(jax.ShapeDtypeStruct(s, jnp.bfloat16) for s in shapes),
        in_specs=[pl.BlockSpec(memory_space=pltpu.HBM)] * len(sources),
        scratch_shapes=[pltpu.VMEM(a.shape, a.dtype) for a in sources] + [pltpu.SemaphoreType.DMA((len(sources),))],
        compiler_params=pltpu.CompilerParams(vmem_limit_bytes=PREPARE_VMEM),
        interpret=INTERPRET,
        name="prepare_weights",
    )(*[stay(a) for a in sources])


def silu_of(u):
    return u * (1.0 + jnp.tanh(u))


def double_slope(u):
    t = jnp.tanh(u)
    double = 1.0 + t
    return double + u * double * (1.0 - t)


def dot(a, b):
    return jnp.dot(a, b, preferred_element_type=jnp.float32)


def dot_tn(a, b):
    return lax.dot_general(a, b, (((0,), (0,)), ((), ())), preferred_element_type=jnp.float32)


def dot_nt(a, b):
    return lax.dot_general(a, b, (((1,), (1,)), ((), ())), preferred_element_type=jnp.float32)


def thirds(x):
    first = x.astype(jnp.bfloat16)
    rest = x - first.astype(jnp.float32)
    second = rest.astype(jnp.bfloat16)
    third = (rest - second.astype(jnp.float32)).astype(jnp.bfloat16)
    return first, second, third


def band_diagonal(full):
    rows = full.shape[0] // SLOTS
    low = low_half((rows, LANES))
    straight, crossed = None, None
    for pair in range(2):
        tiles = [slice((2 * pair + h) * LANES, (2 * pair + h + 1) * LANES) for h in range(2)]
        even = [full[2 * pair * rows : (2 * pair + 1) * rows, tile] for tile in tiles]
        odd = [full[(2 * pair + 1) * rows : (2 * pair + 2) * rows, tile] for tile in tiles]
        direct = jnp.where(low, even[0], odd[1])
        swapped = jnp.where(low, even[1], odd[0])
        straight = direct if straight is None else straight + direct
        crossed = swapped if crossed is None else crossed + swapped
    return straight + swap_halves(crossed)


TILES = tuple(slice(n * LANES, (n + 1) * LANES) for n in range(4))


def step_kernel(rows_total, blocks, margin, loss_scale, layers, position, *refs):
    spacing_in, gathered, w4, wo4, wc, wt, wf, wb, table_t = refs[:9]
    prediction, grad_in, grad_conv, track_out, grad_out_t, grad_table_t = refs[9:15]
    pixels, target, meta, shown, side, dilation, arrived = refs[15:22]
    rest = list(refs[22:])

    def take(count):
        taken = rest[:count]
        del rest[:count]
        return taken

    proj, proj_side = take(2), take(1)[0]
    mixed, mixed_side = take(2), take(1)[0]
    acts = [take(2) for _ in range(layers + 1)]
    gates = [take(2) for _ in range(layers)]
    halves = [take(2) for _ in range(layers + 1)]
    backward = [take(2) for _ in range(layers + 1)]
    grad_track, sent = take(2)
    leaving = []

    def send(source, target, part):
        copy = pltpu.make_async_copy(source, target, sent.at[part])
        copy.start()
        leaving.append(copy)

    size = rows_total * blocks
    strips = gathered.shape[0]
    rows_local = rows_total // strips
    bf16 = jnp.bfloat16
    f32 = jnp.float32
    mine = position if INTERPRET else lax.axis_index("strip")
    scalars = pltpu.make_async_copy(spacing_in, dilation, arrived)
    scalars.start()
    bits = strips.bit_length() - 1
    local = rows_local * blocks
    inner = slice(blocks, blocks + size)
    middle = slice(margin * blocks, margin * blocks + size)

    for s in range(strips):
        apart = mine ^ s
        place = 0
        for b in range(bits):
            place = place * 2 + ((apart >> b) & 1)
        pixels[s * local : (s + 1) * local, :] = gathered[place, 0:local, :]
        target[pl.ds(s, rows_total, stride=blocks), :] = gathered[place, local : local + rows_total, :].astype(f32)
        meta[s : s + 1, :] = gathered[place, local + rows_total : local + rows_total + 8, :].astype(f32)[0:1]

    for ref in (*proj, proj_side, *mixed, mixed_side):
        ref[0:blocks, :] = jnp.zeros((blocks, ref.shape[1]), bf16)
        ref[size + blocks :, :] = jnp.zeros((blocks, ref.shape[1]), bf16)
    edge = jnp.zeros((margin * blocks, 2 * LANES), bf16)
    for ref in [ref for pair in acts[:layers] + gates for ref in pair]:
        ref[0 : margin * blocks, :] = edge
        ref[margin * blocks + size :, :] = edge
    gap = jnp.zeros((rows_total, 8, LANES), f32)
    side[:, :, 0:8, :] = jnp.broadcast_to(gap[None], (4, rows_total, 8, LANES))
    side[:, :, 8 + blocks : 16 + blocks, :] = jnp.broadcast_to(gap[None], (4, rows_total, 8, LANES))

    scalars.wait()
    zero = pl.multiple_of((dilation[0] >> 16) * 8, 8)
    side_low = low_half((rows_total, blocks, LANES))

    def put_side(ref, values):
        for h in range(2):
            for pair in range(2):
                side[2 * h + pair, :, 8 : 8 + blocks, :] = values[pair][:, TILES[h]].reshape(rows_total, blocks, LANES)
            following = side[2 * h, :, 9 : 9 + blocks, :]
            previous = side[2 * h + 1, :, 7 : 7 + blocks, :]
            ref[inner, TILES[h]] = jnp.where(side_low, following, previous).reshape(size, LANES).astype(bf16)

    def window(pairs, beside, h, i):
        rows = slice(i * blocks, i * blocks + size)
        return [pairs[0][rows, TILES[h]], pairs[1][rows, TILES[h]], beside[rows, TILES[h]]]

    def windows(pairs, beside, h):
        return jnp.concatenate([piece for i in range(3) for piece in window(pairs, beside, h, i)], axis=1)

    projected = dot(pixels[...], w4[...])
    projected = [projected[:, 0 : 2 * LANES], projected[:, 2 * LANES :]]
    for pair in range(2):
        proj[pair][inner, :] = projected[pair].astype(bf16)
    put_side(proj_side, projected)
    for h in range(2):
        left = windows(proj, proj_side, h)
        u = jnp.concatenate([dot(left[: size // 2], wc[h]), dot(left[size // 2 :], wc[h])], axis=0)
        silu = silu_of(u)
        for pair in range(2):
            halves[layers][pair][pl.ds(zero, size), TILES[h]] = u[:, TILES[pair]]
            centre = proj[pair][inner, TILES[h]].astype(f32)
            acts[0][pair][middle, TILES[h]] = (centre + silu[:, TILES[pair]]).astype(bf16)

    def tap_rows(ref, layer, sign):
        pieces = []
        for tap in range(3):
            if tap == 1:
                pieces.append(ref[middle, :])
            else:
                start = pl.multiple_of((margin + sign * (tap - 1) * dilation[layer]) * blocks, 16)
                pieces.append(ref[pl.ds(start, size), :])
        return jnp.concatenate(pieces, axis=1)

    def forward(layer):
        rows = middle if layer + 1 < layers else slice(0, size)
        for pair in range(2):
            part = sums[pair]
            halves[layer][pair][pl.ds(zero, size), :] = part
            centre = acts[layer][pair][middle, :].astype(f32)
            acts[layer + 1][pair][rows, :] = (centre + silu_of(part)).astype(bf16)
            if layer + 1 < layers:
                sums[pair] = track(layer + 1, pair)

    def track(layer, pair):
        left = tap_rows(acts[layer][pair], layer, 1)
        return jnp.concatenate([dot(left[: size // 2], wf[layer]), dot(left[size // 2 :], wf[layer])], axis=0)

    sums = [track(0, pair) for pair in range(2)]
    for layer in range(layers):
        forward(layer)

    det_count = table_t.shape[1] // (3 * SLOTS)
    meta_b = meta[...].astype(bf16)
    source = lax.broadcasted_iota(jnp.int32, (LANES, SLOTS * det_count), 0)
    slot_of = lax.broadcasted_iota(jnp.int32, (LANES, SLOTS * det_count), 1) // det_count
    spread = jnp.where(source == slot_of, 1.0, jnp.where(source == slot_of + SLOTS, 256.0, 0.0)).astype(bf16)
    element = (lax.broadcasted_iota(jnp.int32, (blocks, SLOTS * det_count), 1) % det_count).astype(f32)
    selector = jnp.where(dot(meta_b, spread) == element, 1.0, 0.0).astype(bf16)
    source = lax.broadcasted_iota(jnp.int32, (LANES, LANES), 0)
    slot_of = lax.broadcasted_iota(jnp.int32, (LANES, LANES), 1) // (LANES // SLOTS)
    flag = dot(meta_b, jnp.where(source == slot_of + 2 * SLOTS, 1.0, 0.0).astype(bf16))
    offsets = dot_nt(jnp.concatenate([selector] * 3, axis=1), table_t[...]) * flag

    last = jnp.concatenate([ref[...] for ref in acts[layers]], axis=1)
    raw = dot_nt(last, wo4[...]).reshape(rows_total, blocks, LANES) + offsets[None]
    rounded = raw.astype(bf16).astype(f32)
    shown[...] = rounded.reshape(size, LANES)
    prediction[...] = shown[pl.ds(mine, rows_total, stride=blocks), :].astype(bf16)
    residue = (rounded - target[...].reshape(rows_total, blocks, LANES)) * loss_scale
    column_sums = jnp.sum(residue, axis=0) * flag
    residue_b = residue.reshape(size, LANES).astype(bf16)
    for pair in range(2):
        backward[layers][pair][...] = dot(residue_b, wo4[:, 2 * pair * LANES : (2 * pair + 2) * LANES])
    grad_out_t[...] = band_diagonal(dot_tn(residue_b, last))
    parts = jnp.concatenate(thirds(column_sums), axis=0)
    full = dot_tn(parts, jnp.concatenate([selector] * 3, axis=0))
    band_count = LANES // SLOTS
    grad_table_t[...] = sum(
        full[k * band_count : (k + 1) * band_count, k * det_count : (k + 1) * det_count] for k in range(SLOTS)
    )

    tap_low = low_half((HALF, LANES))

    def hold(layer, above):
        for pair in range(2):
            halves[layer][pair][pl.ds(zero + size, 8), 0:LANES] = backward[above][pair][0:8, 0:LANES]

    def back(layer):
        hold(layer, layer + 1)
        moved = []
        for pair in range(2):
            gates[layer][pair][middle, :] = (backward[layer + 1][pair][...] * double_slope(halves[layer][pair][0:size, :])).astype(bf16)
            right = tap_rows(gates[layer][pair], layer, -1)
            moved.append(right)
        both = jnp.concatenate(moved, axis=0)
        update = dot(both, wb[layer])
        for pair in range(2):
            backward[layer][pair][...] = backward[layer + 1][pair][...] + update[pair * size : (pair + 1) * size]
        left = jnp.concatenate([acts[layer][pair][middle, :] for pair in range(2)], axis=0)
        full = dot_tn(left, both)
        for tap in range(3):
            first = full[:, 2 * tap * LANES : (2 * tap + 1) * LANES]
            second = full[:, (2 * tap + 1) * LANES : (2 * tap + 2) * LANES]
            for h in range(2):
                upper = slice(2 * h * HALF, (2 * h + 1) * HALF)
                lower = slice((2 * h + 1) * HALF, (2 * h + 2) * HALF)
                straight = jnp.where(tap_low, first[upper], second[lower])
                crossed = jnp.where(tap_low, second[upper], first[lower])
                start = (layer * 3 + tap) * LANES + h * HALF
                grad_track[start : start + HALF, :] = 0.5 * (straight + swap_halves(crossed))
        rows = slice(layer * 3 * LANES, (layer + 1) * 3 * LANES)
        send(grad_track.at[rows], track_out.at[rows], layer)

    for layer in reversed(range(layers)):
        back(layer)

    hold(layers, 0)
    gradients = [backward[0][pair][...].astype(bf16).astype(f32) for pair in range(2)]
    values = [gradients[pair] * double_slope(halves[layers][pair][0:size, :]) for pair in range(2)]
    for pair in range(2):
        mixed[pair][inner, :] = values[pair].astype(bf16)
    put_side(mixed_side, values)
    lifted = [[None, None], [None, None]]
    for h in range(2):
        pulled = dot(windows(mixed, mixed_side, h), wt[h])
        for pair in range(2):
            centre = backward[0][pair][:, TILES[h]].astype(bf16).astype(f32)
            lifted[pair][h] = (centre + pulled[:, TILES[pair]]).astype(bf16)
    grad_in[...] = band_diagonal(dot_tn(pixels[...], jnp.concatenate(lifted[0] + lifted[1], axis=1)))

    width = grad_conv.shape[1]
    for h in range(2):
        left = jnp.concatenate(window(proj, proj_side, h, 1), axis=1)
        right = jnp.concatenate(
            [
                mixed[pair][(2 - i) * blocks : (2 - i) * blocks + size, TILES[h]]
                for i in range(3)
                for pair in range(2)
            ],
            axis=1,
        )
        full = dot_tn(left, right)
        for i in range(3):
            for j in range(3):
                parts = []
                for out_slot in range(SLOTS):
                    row = INPUT_SLOTS.index(out_slot + j - 1) * HALF
                    tile = 2 * i + out_slot // 2
                    parts.append(full[row : row + HALF, tile * LANES : (tile + 1) * LANES])
                total = 0.5 * (parts[0] + parts[2] + swap_halves(parts[1] + parts[3]))
                for g in range(2):
                    start = ((3 * i + j) * 4 + 2 * h + g) * width
                    piece = total[g * width : (g + 1) * width]
                    if g:
                        piece = pltpu.roll(piece, LANES - width, 1)
                    grad_conv[start : start + width, :] = piece[:, :width]
    for copy in leaving:
        copy.wait()


def replicated_step(gathered, weights, w_track_shape, w_conv_shape, table_shape, dilation, rows_total, blocks, position=None):
    layers = w_track_shape[0]
    margin = rows_total // 4
    size = rows_total * blocks
    chan_count = w_track_shape[2]
    det_count, band_count = table_shape
    loss_scale = 1.0 / math.sqrt(rows_total * blocks * SLOTS)
    vmem = pl.BlockSpec(memory_space=pltpu.VMEM)
    hbm = pl.BlockSpec(memory_space=pltpu.HBM)
    f32, bf16 = jnp.float32, jnp.bfloat16
    taps = math.prod(w_conv_shape[:4])
    wide = 2 * LANES
    ringed = pltpu.VMEM((size + 2 * blocks, wide), bf16)
    spaced = pltpu.VMEM((size + 2 * margin * blocks, wide), bf16)
    outs = pl.pallas_call(
        lambda *refs: step_kernel(rows_total, blocks, margin, loss_scale, layers, position, *refs),
        out_shape=(
            jax.ShapeDtypeStruct((rows_total, LANES), bf16),
            jax.ShapeDtypeStruct((band_count, chan_count), f32),
            jax.ShapeDtypeStruct((taps, w_conv_shape[4]), f32),
            jax.ShapeDtypeStruct((layers * 3 * chan_count, chan_count), f32),
            jax.ShapeDtypeStruct((band_count, chan_count), f32),
            jax.ShapeDtypeStruct((band_count, det_count), f32),
        ),
        in_specs=[hbm] + [vmem] * 8,
        out_specs=(vmem, vmem, vmem, hbm, vmem, vmem),
        scratch_shapes=[
            pltpu.VMEM((size, LANES), bf16),
            pltpu.VMEM((size, LANES), f32),
            pltpu.VMEM((blocks, LANES), f32),
            pltpu.VMEM((size, LANES), f32),
            pltpu.VMEM((4, rows_total, blocks + 16, LANES), f32),
            pltpu.SMEM(dilation.shape, dilation.dtype),
            pltpu.SemaphoreType.DMA,
        ]
        + [ringed] * 6
        + [spaced] * (2 * layers)
        + [pltpu.VMEM((size, wide), bf16)] * 2
        + [spaced] * (2 * layers)
        + [pltpu.VMEM((size + 8, wide), f32)] * (2 * (layers + 1))
        + [pltpu.VMEM((size, wide), f32)] * (2 * (layers + 1))
        + [pltpu.VMEM((layers * 3 * chan_count, chan_count), f32), pltpu.SemaphoreType.DMA((layers,))],
        compiler_params=pltpu.CompilerParams(vmem_limit_bytes=STEP_VMEM),
        interpret=INTERPRET,
        name="strip_step",
    )(stay(dilation), gathered, *weights)
    prediction, grad_in, grad_conv, grad_track, grad_out_t, grad_table_t = outs
    return (
        prediction,
        grad_in,
        grad_conv.reshape(w_conv_shape),
        grad_track.reshape(w_track_shape),
        grad_out_t.T,
        grad_table_t.T,
    )


def payload_kernel(*refs):
    sources, payload, held, rows, semaphores = refs[:4], refs[4], refs[5:9], refs[9], refs[10]
    bands, target, detector, flags = held
    for copy in fetch(sources, held, semaphores):
        copy.wait()
    blocks = bands.shape[1] // LANES
    rows_local = bands.shape[0]
    local = rows_local * blocks
    wide = bands[...].astype(jnp.float32)
    for block in range(blocks):
        rows[pl.ds(block, rows_local, stride=blocks), :] = wide[:, block * LANES : (block + 1) * LANES]
    payload[0:local, :] = rows[...].astype(payload.dtype)
    payload[local : local + target.shape[0], :] = target[...]
    shape = (8, LANES)
    lane = lax.broadcasted_iota(jnp.int32, shape, 1)
    line = jnp.zeros(shape, jnp.int32)
    for k in range(SLOTS):
        line = jnp.where(lane == k, detector[k] & 255, line)
        line = jnp.where(lane == SLOTS + k, detector[k] >> 8, line)
        line = jnp.where(lane == 2 * SLOTS + k, flags[k], line)
    payload[local + target.shape[0] :, :] = line.astype(jnp.float32).astype(payload.dtype)


def device_payload(bands, target, detector, flags, blocks):
    local = bands.shape[0] * blocks
    return pl.pallas_call(
        payload_kernel,
        out_shape=jax.ShapeDtypeStruct((local + target.shape[0] + 8, LANES), jnp.bfloat16),
        in_specs=[pl.BlockSpec(memory_space=pltpu.HBM)] * 4,
        out_specs=pl.BlockSpec(memory_space=pltpu.VMEM),
        scratch_shapes=[
            pltpu.VMEM(bands.shape, bands.dtype),
            pltpu.VMEM(target.shape, target.dtype),
            pltpu.SMEM(detector.shape, detector.dtype),
            pltpu.SMEM(flags.shape, flags.dtype),
            pltpu.VMEM((local, LANES), jnp.float32),
            pltpu.SemaphoreType.DMA((4,)),
        ],
        compiler_params=pltpu.CompilerParams(vmem_limit_bytes=PREPARE_VMEM),
        interpret=INTERPRET,
        name="payload",
    )(*[stay(a) for a in (bands, target, detector, flags)])


def gather_strip(payload, size):
    held = payload[None]
    distance = size // 2
    while distance:
        pairs = [(i, i ^ distance) for i in range(size)]
        held = jnp.concatenate([held, lax.ppermute(held, "strip", pairs)], axis=0)
        distance //= 2
    return held


def body_replicated(bands, target, w_in, w_conv, w_track, w_out, table, dilation, detector, flags):
    size = lax.axis_size("strip")
    rows_total = bands.shape[0] * size
    blocks = bands.shape[1] // LANES
    weights = prepare_weights(w_in, w_conv, w_track, w_out, table)
    gathered = gather_strip(device_payload(bands, target, detector, flags, blocks), size)
    return replicated_step(
        gathered, weights, w_track.shape, w_conv.shape, table.shape, dilation, rows_total, blocks
    )


def strip_fits(bands, target, w_in, w_conv, w_track, w_out, table, dilation, detector, flags):
    size = lax.axis_size("strip")
    band_count, chan_count = w_in.shape
    rows_local = bands.shape[0]
    rows_total = rows_local * size
    blocks = bands.shape[1] // LANES
    held = rows_total * blocks * SLOTS * chan_count * 44
    return (
        size & (size - 1) == 0
        and chan_count == 2 * HALF
        and band_count * SLOTS == LANES
        and w_conv.shape[2:] == (4, HALF // 2, HALF // 2)
        and w_out.shape[1] == band_count
        and target.shape == (rows_total, LANES)
        and blocks == size
        and blocks % 16 == 0
        and held <= VMEM_BUDGET
    )


def body(*args):
    return body_replicated(*args) if strip_fits(*args) else body_distributed(*args)


def solution(mesh):
    placed = (
        P(("groups", "strip"), None),
        P("groups", "strip"),
        P(),
        P(),
        P(),
        P(),
        P(),
        P(),
        P(("groups", "strip")),
        P(("groups", "strip")),
    )
    return jax.shard_map(
        body,
        mesh=mesh,
        in_specs=placed,
        out_specs=(
            P("groups", "strip"),
            P("groups", None),
            P("groups", None, None, None, None),
            P("groups", None, None, None),
            P("groups", None),
            P("groups", None),
        ),
        check_vma=False,
    )
```
